32 devices in a mesh: img: 16 (over z, y, core), cap: 2 (over x).
Axes of the slice: x: 2, y: 2, z: 4, core: 2. Of those that a mesh axis runs over, the one named last changes fastest.
Arguments:
- feats_img: bfloat16 [12288, 768], P(('img', 'cap')), may hold values from -6 to 6
- feats_cap: bfloat16 [12288, 768], P(('img', 'cap')), may hold values from -6 to 6
- cot_img: bfloat16 [12288, 512], P(('img', 'cap')), may hold values from -60 to 60
- cot_cap: bfloat16 [12288, 512], P(('img', 'cap')), may hold values from -60 to 60
- w_in: bfloat16 [2048, 768], replicated, may hold values from -0.21875 to 0.21875
- b_in: float32 [2048], replicated, may hold values from -3 to 3
- w_out: bfloat16 [2048, 512], replicated, may hold values from -0.125 to 0.125
- tile_seed: int32 [96, 4], P(('img', 'cap')), may hold values from 0 to 16777214
- tile_cols: int32 [96, 4], P(('img', 'cap')), may hold values from 0 to 95, as said below
- tile_count: int32 [96], P(('img', 'cap')), may hold values from 1 to 4, as said below
Outputs:
- grad_feats_img: bfloat16 [12288, 768], P(('img', 'cap'))
- grad_feats_cap: bfloat16 [12288, 768], P(('img', 'cap'))
- grad_w_in: float32 [2048, 768], P(('img', 'cap'))
- grad_w_out: float32 [2048, 512], P(('img', 'cap'))
- grad_b_in: float32 [2048], P(('img', 'cap'))
The draws below stay inside these ranges and needn't reach their ends.
Inputs may be any that keep to these rules, and one draw needn't show every extreme that they name: `tile_cols`: slot 0 of image tile t holds t itself; the other slots hold distinct caption tiles within 3 tiles of t; slot 1 of tile 96 - 4 holds the next tile and slot 1 of tile 96 - 3 the previous one. `tile_count`: the largest count, 4, is reached on some device in every draw, among others on tiles 96 - 4 and 93.
All inputs are finite; a program needn't handle non-finite values.
Results may differ from the reference program's by a relative error of at most 0.0061.
Values may be sent and summed in bfloat16 or wider, within the bound.
No kernel may reach another device: no remote copies, remote signals or barrier semaphores. Data moves between devices by JAX's collectives and lax.ppermute only.
A program may use at most 64 MiB of HBM per device.

```python
import math
import jax
import jax.numpy as jnp
from jax import lax

F_IN = 768
HID = 2048
C = 512
TILE = 128
HOPS = 2
TILE_DEV = 3
BAND = 3
SLOTS = 4
NT = 96
NI = 12288
NODES = 24576


def draw_tile_cols(key, part):
    band_reach = 2 * BAND + 1
    home_tile = jnp.arange(NT, dtype=jnp.int32)[:, None]
    offset = jnp.arange(band_reach, dtype=jnp.int32)[None, :] - BAND
    target = home_tile + offset
    usable = (target >= 0) & (target < NT) & (offset != 0)
    scores = jax.random.randint(key, (NT, band_reach), 0, 1 << 20, dtype=jnp.int32) * band_reach
    scores = scores + jnp.arange(band_reach, dtype=jnp.int32)[None, :]
    scores = jnp.where(usable, scores, 1 << 30)
    scores = scores.at[NT - TILE_DEV - 1, BAND + 1].set(-1)
    scores = scores.at[NT - TILE_DEV, BAND - 1].set(-1)
    ranked = jnp.argsort(scores, axis=1, stable=True)[:, :SLOTS - 1]
    chosen = jnp.take_along_axis(target, ranked, axis=1)
    return jnp.concatenate([home_tile, chosen], axis=1).astype(jnp.int32)


def draw_tile_count(key, part):
    device_count = NT // TILE_DEV
    key_level, key_count, key_peak = jax.random.split(jax.random.fold_in(key, 7), 3)
    device_level = jax.random.randint(key_level, (device_count,), 1, SLOTS + 1, dtype=jnp.int32)
    device_level = jnp.where(jnp.arange(device_count, dtype=jnp.int32) == 0, SLOTS, device_level)
    counts = jax.random.randint(key_count, (device_count, TILE_DEV), 1, device_level[:, None] + 1, dtype=jnp.int32)
    peak_slot = jax.random.randint(key_peak, (device_count,), 0, TILE_DEV, dtype=jnp.int32)
    counts = jnp.where(jnp.arange(TILE_DEV, dtype=jnp.int32)[None, :] == peak_slot[:, None], device_level[:, None], counts)
    counts = counts.reshape(NT)
    counts = counts.at[NT - TILE_DEV - 1].set(SLOTS)
    counts = counts.at[NT - TILE_DEV].set(SLOTS)
    return counts.astype(jnp.int32)


def plant(entries, own_key, low, top_value):
    longest = entries.shape.index(max(entries.shape))
    spots = []
    for shift in (0, 1):
        where = [jax.random.randint(jax.random.fold_in(own_key, axis), (), 0, length) for axis, length in enumerate(entries.shape)]
        where[longest] = (where[longest] + shift) % entries.shape[longest]
        spots.append(tuple(where))
    return entries.at[spots[0]].set(low).at[spots[1]].set(top_value)


def levels(rng, extent, cuts, least, high):
    loudness, own = 1.0, jax.random.fold_in(rng, 6)
    for position, blocks in cuts:
        steps = jnp.exp(jax.random.uniform(jax.random.fold_in(own, position), (blocks,), jnp.float32, least / len(cuts), high / len(cuts)))
        loudness = loudness * jnp.repeat(steps, extent[position] // blocks).reshape([-1 if axis == position else 1 for axis in range(len(extent))])
    return loudness


def bell_draw(stream_key, extent, deviation, reach, shards=(), kind=jnp.bfloat16):
    array = deviation * jax.random.normal(stream_key, extent, jnp.float32)
    if shards:
        array = array * levels(stream_key, extent, shards, -0.22, 0.18)
    return jnp.clip(array, -reach, reach).astype(kind)


def setup_inputs(seed: int = 0) -> dict:
    key_of = jax.random.split(jax.random.key(seed), 11)
    return {
        "feats_img": bell_draw(key_of[0], (NI, F_IN), 1.0, 6.0, ((0, 32),)),
        "feats_cap": bell_draw(key_of[1], (NI, F_IN), 1.0, 6.0, ((0, 32),)),
        "cot_img": bell_draw(key_of[2], (NI, C), 10.0, 60.0, ((0, 32),)),
        "cot_cap": bell_draw(key_of[3], (NI, C), 10.0, 60.0, ((0, 32),)),
        "w_in": bell_draw(key_of[4], (HID, F_IN), F_IN ** -0.5, 0.21875),
        "b_in": bell_draw(key_of[5], (HID,), 0.5, 3.0, (), jnp.float32),
        "w_out": bell_draw(key_of[6], (HID, C), HID ** -0.5, 0.125),
        "tile_seed": plant(jax.random.randint(key_of[7], (NT, SLOTS), 0, 16777215), jax.random.fold_in(key_of[7], 1), 0, 16777214).astype(jnp.int32),
        "tile_cols": draw_tile_cols(jax.random.fold_in(key_of[10], 71), 0),
        "tile_count": draw_tile_count(jax.random.fold_in(key_of[10], 71), 0),
    }


ALPHA = 0.1

def tile_patterns(seeds, counts):
    row_index = lax.broadcasted_iota(jnp.int32, (TILE, TILE), 0)
    col_index = lax.broadcasted_iota(jnp.int32, (TILE, TILE), 1)
    index_of_slot = lax.broadcasted_iota(jnp.int32, seeds.shape, 1)
    mixed = seeds[:, :, None, None] + row_index * 40503 + col_index * 9973
    mixed = mixed * 668265261
    mixed = jnp.bitwise_xor(mixed, jnp.right_shift(mixed, 15))
    mixed = mixed * 374761393
    mixed = jnp.bitwise_xor(mixed, jnp.right_shift(mixed, 13))
    has_edge = jnp.bitwise_and(mixed, 15) == 0
    on_diagonal = (row_index == col_index)[None, None] & (index_of_slot == 0)[:, :, None, None]
    is_live = (index_of_slot < counts[:, None])[:, :, None, None]
    return jnp.where(is_live & (has_edge | on_diagonal), 1.0, 0.0).astype(jnp.bfloat16)

def gelu_parts(preact):
    normal_cdf = 0.5 * (1.0 + jax.scipy.special.erf(preact * 0.7071067811865476))
    normal_pdf = jnp.exp(-0.5 * preact * preact) * 0.3989422804014327
    return (preact * normal_cdf, normal_cdf + preact * normal_pdf)

def forward_tiles(sparsity_layout, tile_cols, state):
    block_groups = state.reshape(NT, TILE, C).astype(jnp.float32)
    running_totals = jnp.zeros((NT, TILE, C), jnp.float32)
    for index_of_slot in range(SLOTS):
        selected_entries = block_groups[tile_cols[:, index_of_slot]]
        running_totals = running_totals + jnp.einsum('lpn,lns->lps', sparsity_layout[:, index_of_slot].astype(jnp.float32), selected_entries)
    return running_totals.reshape(NT * TILE, C)

def adjoint_tiles(sparsity_layout, tile_cols, state):
    block_groups = state.reshape(NT, TILE, C).astype(jnp.float32)
    running_totals = jnp.zeros((NT, TILE, C), jnp.float32)
    for index_of_slot in range(SLOTS):
        contribution = jnp.einsum('gmz,gms->gzs', sparsity_layout[:, index_of_slot].astype(jnp.float32), block_groups)
        running_totals = running_totals.at[tile_cols[:, index_of_slot]].add(contribution)
    return running_totals.reshape(NT * TILE, C)

def mlp_back(feats, logit_gradient, w_in, b_in, w_out):
    block_rows = math.gcd(NT * TILE, 4096)
    block_count = NT * TILE // block_rows
    feat_blocks = feats.reshape(block_count, block_rows, F_IN)
    logit_blocks = logit_gradient.reshape(block_count, block_rows, C)

    def one_block(carry, pieces):
        feat_piece, logit_piece = pieces
        sum_in, sum_out, sum_bias = carry
        preact = jnp.dot(feat_piece, w_in.T, preferred_element_type=jnp.float32) + b_in
        gelu_value, gelu_slope = gelu_parts(preact)
        hidden_act = gelu_value.astype(jnp.bfloat16)
        hidden_grad = jnp.dot(logit_piece, w_out.T, preferred_element_type=jnp.float32)
        preact_grad = (hidden_grad * gelu_slope).astype(jnp.bfloat16)
        feat_grad = jnp.dot(preact_grad, w_in, preferred_element_type=jnp.float32).astype(jnp.bfloat16)
        sum_in = sum_in + jnp.dot(preact_grad.T, feat_piece, preferred_element_type=jnp.float32)
        sum_out = sum_out + jnp.dot(hidden_act.T, logit_piece, preferred_element_type=jnp.float32)
        sum_bias = sum_bias + lax.optimization_barrier(jnp.sum(preact_grad, axis=0, dtype=jnp.float32))
        return ((sum_in, sum_out, sum_bias), feat_grad)
    start = (jnp.zeros((HID, F_IN), jnp.float32), jnp.zeros((HID, C), jnp.float32), jnp.zeros((HID,), jnp.float32))
    sums, feat_grads = lax.scan(one_block, start, (feat_blocks, logit_blocks))
    return (sums, feat_grads.reshape(NT * TILE, F_IN))

def reference(feats_img, feats_cap, cot_img, cot_cap, w_in, b_in, w_out, tile_seed, tile_cols, tile_count):
    sparsity_layout = tile_patterns(tile_seed, tile_count)
    degree_img = lax.optimization_barrier(jnp.sum(sparsity_layout, axis=(1, 3), dtype=jnp.float32)).reshape(NT * TILE)
    col_part = lax.optimization_barrier(jnp.sum(sparsity_layout, axis=2, dtype=jnp.float32))
    degree_cap = jnp.zeros((NT, TILE), jnp.float32).at[tile_cols].add(col_part).reshape(NT * TILE)
    norm_img = lax.rsqrt(degree_img)[:, None]
    norm_cap = lax.rsqrt(degree_cap)[:, None]
    flow_img = cot_img.astype(jnp.float32)
    flow_cap = cot_cap.astype(jnp.float32)
    sum_img = jnp.zeros_like(flow_img)
    sum_cap = jnp.zeros_like(flow_cap)
    for hop_index in range(HOPS):
        sum_img = sum_img + flow_img
        sum_cap = sum_cap + flow_cap
        state_img = (flow_img * norm_img).astype(jnp.bfloat16)
        state_cap = (flow_cap * norm_cap).astype(jnp.bfloat16)
        new_img = (1.0 - ALPHA) * norm_img * forward_tiles(sparsity_layout, tile_cols, state_cap)
        flow_cap = (1.0 - ALPHA) * norm_cap * adjoint_tiles(sparsity_layout, tile_cols, state_img)
        flow_img = new_img
    logit_img = (ALPHA * sum_img + flow_img).astype(jnp.bfloat16)
    logit_cap = (ALPHA * sum_cap + flow_cap).astype(jnp.bfloat16)
    sums_img, grad_feats_img = mlp_back(feats_img, logit_img, w_in, b_in, w_out)
    sums_cap, grad_feats_cap = mlp_back(feats_cap, logit_cap, w_in, b_in, w_out)
    grad_scale = 1.0 / math.sqrt(NODES)
    grad_w_in = (sums_img[0] + sums_cap[0]) * grad_scale
    grad_w_out = (sums_img[1] + sums_cap[1]) * grad_scale
    grad_b_in = (sums_img[2] + sums_cap[2]) * grad_scale
    return (grad_feats_img, grad_feats_cap, grad_w_in, grad_w_out, grad_b_in)
```

```python
import math

import jax
import jax.numpy as jnp
from jax import lax
from jax.experimental import pallas as pl
from jax.experimental.pallas import tpu as pltpu
from jax.sharding import PartitionSpec as P

TILE = 128
ALPHA = 0.1
AXES = ("img", "cap")
F32 = jnp.float32
BF16 = jnp.bfloat16


def gelu_parts(preact):
    normal_cdf = 0.5 * (1.0 + jax.scipy.special.erf(preact * 0.7071067811865476))
    normal_pdf = jnp.exp(-0.5 * preact * preact) * 0.3989422804014327
    return (preact * normal_cdf, normal_cdf + preact * normal_pdf)


def tiles_kernel(seed_ref, place_ref, count_ref, pat_ref, pat_t_ref, nimg_ref, ncap_ref, deg_ref, *, tiles, slots):
    all_tiles, mid = 7 * tiles, 5 * tiles
    deg_ref[...] = jnp.zeros_like(deg_ref)
    row = lax.broadcasted_iota(jnp.int32, (TILE, TILE), 0)
    col = lax.broadcasted_iota(jnp.int32, (TILE, TILE), 1)
    first, second = jnp.int32(668265261), jnp.int32(374761393)
    base = (row * 40503 + col * 9973) * first
    base_t = (col * 40503 + row * 9973) * first
    off_diag = row - col

    def pattern(start, seed, live, s):
        mixed = start + seed * first
        mixed = jnp.bitwise_xor(mixed, jnp.right_shift(mixed, 15))
        mixed = mixed * second
        mixed = jnp.bitwise_xor(mixed, jnp.right_shift(mixed, 13))
        edge = jnp.bitwise_and(mixed, 15) == jnp.where(live, 0, 16)
        if s == 0:
            edge = edge | (off_diag == jnp.where(live, 0, TILE))
        return jnp.where(edge, 1.0, 0.0)

    def one(q, full):
        total = None
        for s in range(slots):
            live = s < count_ref[q]
            seed = seed_ref[q * slots + s]
            e = pattern(base, seed, live, s)
            c = place_ref[q * slots + s]
            deg_ref[c] += jnp.sum(e, axis=0, keepdims=True)
            if full:
                m = q - tiles
                pat_ref[m, :, pl.ds(s * TILE, TILE)] = e.astype(BF16)
                pat_t_ref[m, pl.ds(s * TILE, TILE), :] = pattern(base_t, seed, live, s).astype(BF16)
                total = e if total is None else total + e
        if full:
            d = jnp.sum(total, axis=1, keepdims=True)
            n = jnp.where(d > 0.0, lax.rsqrt(d), 0.0)
            nimg_ref[q - tiles] = jnp.broadcast_to(n, (TILE, TILE))

    def edge_body(q, c):
        one(q, False)
        return c

    def mid_body(q, c):
        one(q, True)
        return c

    lax.fori_loop(0, tiles, edge_body, 0)
    lax.fori_loop(tiles, tiles + mid, mid_body, 0)
    lax.fori_loop(tiles + mid, all_tiles, edge_body, 0)
    for m in range(mid):
        d = deg_ref[m + 2 * tiles]
        n = jnp.where(d > 0.0, lax.rsqrt(d), 0.0)
        ncap_ref[m] = jnp.broadcast_to(n, (TILE, TILE)).T


def make_tiles(seeds, places, counts, tiles, slots):
    mid = 5 * tiles
    smem = pl.BlockSpec(memory_space=pltpu.SMEM)
    vmem = pl.BlockSpec(memory_space=pltpu.VMEM)
    return pl.pallas_call(
        lambda *r: tiles_kernel(*r, tiles=tiles, slots=slots),
        out_shape=(
            jax.ShapeDtypeStruct((mid, TILE, slots * TILE), BF16),
            jax.ShapeDtypeStruct((mid, slots * TILE, TILE), BF16),
            jax.ShapeDtypeStruct((mid, TILE, TILE), F32),
            jax.ShapeDtypeStruct((mid, TILE, TILE), F32),
        ),
        in_specs=[smem] * 3,
        out_specs=(vmem,) * 4,
        scratch_shapes=[pltpu.VMEM((9 * tiles, 1, TILE), F32)],
        compiler_params=pltpu.CompilerParams(vmem_limit_bytes=40 << 20),
        name="tiles",
    )(seeds, places, counts)


def hops_kernel(
    place_ref, base_ref, own_img, own_cap, low, high, mate, far, pat_ref, pat_t_ref, nimg_ref, ncap_ref,
    out_img, out_cap, img0, cap0, img1, cap1, acc, acc2, keep_img, keep_cap, *, tiles, slots, width,
):
    mid = 5 * tiles
    near = 3 * tiles
    keep = 1.0 - ALPHA

    def wide(n_ref, m):
        n = n_ref[m]
        return jnp.concatenate([n] * (width // TILE), axis=1)

    def scale(rows_img, rows_cap, base):
        for t in range(tiles):
            m = base + t
            img0[m] = (rows_img(t).astype(F32) * wide(nimg_ref, m)).astype(BF16)
            cap0[m] = (rows_cap(t).astype(F32) * wide(ncap_ref, m)).astype(BF16)

    def both(ref):
        return (lambda t: ref[pl.ds(t * TILE, TILE), :]), (lambda t: ref[pl.ds((tiles + t) * TILE, TILE), :])

    scale(lambda t: own_img[pl.ds(t * TILE, TILE), :], lambda t: own_cap[pl.ds(t * TILE, TILE), :], 2 * tiles)
    scale(*both(low), 0)
    scale(*both(high), 4 * tiles)
    scale(*both(mate), base_ref[0])
    scale(*both(far), base_ref[1])
    acc[...] = jnp.zeros_like(acc)
    acc2[...] = jnp.zeros_like(acc2)

    def push(q, state, target, lo, count):
        r = jnp.dot(pat_t_ref[q], state, preferred_element_type=F32)
        for s in range(slots):
            c = place_ref[q * slots + s] - lo
            c = jnp.where((c >= 0) & (c < count), c, count)
            target[c] += r[s * TILE : (s + 1) * TILE]

    def pull(q, source, lo):
        total = None
        for s in range(slots):
            c = place_ref[q * slots + s] - lo
            r = jnp.dot(pat_ref[q, :, pl.ds(s * TILE, TILE)], source[c], preferred_element_type=F32)
            total = r if total is None else total + r
        return total

    def push1(q, c):
        push(q, img0[q], acc, tiles, near)
        return c

    lax.fori_loop(0, mid, push1, 0)

    def pull1(q, c):
        n = wide(nimg_ref, q)
        flow = keep * n * pull(q, cap0, 0)
        img1[q - tiles] = (flow * n).astype(BF16)
        keep_img[q - tiles] = flow
        return c

    lax.fori_loop(tiles, tiles + near, pull1, 0)

    def finish1(m, c):
        n = wide(ncap_ref, m + tiles)
        flow = keep * n * acc[m]
        cap1[m] = (flow * n).astype(BF16)
        keep_cap[m] = flow
        return c

    lax.fori_loop(0, near, finish1, 0)

    def push2(q, c):
        push(q, img1[q - tiles], acc2, 2 * tiles, tiles)
        return c

    lax.fori_loop(tiles, tiles + near, push2, 0)
    for t in range(tiles):
        q = 2 * tiles + t
        rows = pl.ds(t * TILE, TILE)
        flow = keep * wide(nimg_ref, q) * pull(q, cap1, tiles)
        out_img[rows, :] = (ALPHA * (own_img[rows, :].astype(F32) + keep_img[tiles + t]) + flow).astype(BF16)
        flow = keep * wide(ncap_ref, q) * acc2[t]
        out_cap[rows, :] = (ALPHA * (own_cap[rows, :].astype(F32) + keep_cap[tiles + t]) + flow).astype(BF16)


def propagate(places, bases, own_img, own_cap, low, high, mate, far, pats, tiles, slots):
    width = own_img.shape[1]
    smem = pl.BlockSpec(memory_space=pltpu.SMEM)
    vmem = pl.BlockSpec(memory_space=pltpu.VMEM)
    mid, near = 5 * tiles, 3 * tiles
    return pl.pallas_call(
        lambda *r: hops_kernel(*r, tiles=tiles, slots=slots, width=width),
        out_shape=(jax.ShapeDtypeStruct(own_img.shape, BF16),) * 2,
        in_specs=[smem] * 2 + [vmem] * 10,
        out_specs=(vmem,) * 2,
        scratch_shapes=[
            pltpu.VMEM((mid, TILE, width), BF16),
            pltpu.VMEM((mid, TILE, width), BF16),
            pltpu.VMEM((near, TILE, width), BF16),
            pltpu.VMEM((near, TILE, width), BF16),
            pltpu.VMEM((near + 1, TILE, width), F32),
            pltpu.VMEM((tiles + 1, TILE, width), F32),
            pltpu.VMEM((near, TILE, width), F32),
            pltpu.VMEM((near, TILE, width), F32),
        ],
        compiler_params=pltpu.CompilerParams(vmem_limit_bytes=56 << 20),
        name="hops",
    )(places, bases, own_img, own_cap, low, high, mate, far, *pats)


def moved(array, count, by):
    return lax.ppermute(array, AXES, [(i, i + by) for i in range(count) if 0 <= i + by < count])


def flipped(array, count, mask):
    return lax.ppermute(array, AXES, [(i, i ^ mask) for i in range(count)])


def halve(array, axis, count, mask):
    kept = lax.index_in_dim(array, 0, axis, keepdims=False)
    sent = lax.index_in_dim(array, 1, axis, keepdims=False)
    return (kept.astype(F32) + flipped(sent, count, mask).astype(F32)).astype(BF16)


def scattered(part, count, bits, order):
    rows, lanes = part.shape[1:]
    part = part.reshape((2,) * len(bits) + (rows, lanes))
    left = list(bits)
    for bit in order:
        part = halve(part, left.index(bit), count, 1 << bit)
        left.remove(bit)
    part = part.reshape((4, rows, lanes))
    got = [flipped(part[k], count, ((k >> 1) << left[0]) | ((k & 1) << left[1])) for k in range(1, 4)]
    total = part[0].astype(F32)
    for piece in got:
        total = total + piece.astype(F32)
    return total


def per_device(
    feats_img, feats_cap, cot_img, cot_cap, w_in, b_in, w_out, tile_seed, tile_cols, tile_count
):
    local_rows = feats_img.shape[0]
    tiles = local_rows // TILE
    slots = tile_seed.shape[1]
    hid, f_in = w_in.shape
    n_img, n_cap = lax.axis_size("img"), lax.axis_size("cap")
    count = n_img * n_cap
    me = lax.axis_index(AXES)

    meta = jnp.concatenate([tile_seed, tile_cols, tile_count[:, None]], axis=1)
    bands = [moved(meta, count, by) for by in (3, 2, 1)] + [meta] + [moved(meta, count, -by) for by in (1, 2, 3)]
    block = jnp.concatenate([cot_img, cot_cap], axis=0)
    mate = flipped(block, count, 1)
    low = moved(block, count, 2)
    high = moved(block, count, -2)
    far = lax.ppermute(
        mate,
        AXES,
        [(i, i + 2) for i in range(0, count - 2, 2)] + [(i, i - 2) for i in range(3, count, 2)],
    )
    wide = jnp.concatenate(bands, axis=0)
    frame = jnp.arange(7 * tiles, dtype=jnp.int32)[:, None]
    counts = wide[:, 2 * slots]
    seeds = wide[:, :slots].reshape(-1)
    places = jnp.where(counts[:, None] > 0, wide[:, slots : 2 * slots] - (me - 3) * tiles, frame)
    pats = make_tiles(seeds, (places + tiles).reshape(-1), counts, tiles, slots)

    m = count.bit_length() - 1
    a = n_cap.bit_length() - 1
    cap_bits = list(range(a))
    img_bits = list(range(a + 1, m - 2))
    bits = [a] + cap_bits + img_bits + [m - 1, m - 2]
    pos = jnp.arange(count, dtype=jnp.int32)
    order = jnp.zeros_like(pos)
    for k, bit in enumerate(bits):
        order = order | (((pos >> (m - 1 - k)) & 1) << bit)
    order = order ^ me
    rows = hid // count
    w_in_p = jnp.take(w_in.reshape(count, rows, f_in), order, axis=0).reshape(hid, f_in)
    w_out_p = jnp.take(w_out.reshape(count, rows, -1), order, axis=0).reshape(hid, -1)
    b_in_p = jnp.take(b_in.reshape(count, rows), order, axis=0).reshape(hid)

    feats = jnp.concatenate([feats_img, feats_cap], axis=0)
    preact = (
        lax.dot_general(feats, w_in_p, (((1,), (1,)), ((), ())), preferred_element_type=F32) + b_in_p
    )
    gelu_value, gelu_slope = gelu_parts(preact)
    hidden_act = gelu_value.astype(BF16)
    gelu_slope = lax.optimization_barrier(gelu_slope)

    even = (me & 1) == 0
    bases = jnp.where(even, jnp.array([3, 1]), jnp.array([1, 3])).astype(jnp.int32) * tiles
    mid_places = (places - tiles)[tiles : 6 * tiles].reshape(-1)
    logit_img, logit_cap = propagate(
        mid_places, bases, cot_img, cot_cap, low, high, mate, far, pats, tiles, slots
    )
    logit_gradient = jnp.concatenate([logit_img, logit_cap], axis=0)
    over_rows = (((0,), (0,)), ((), ()))
    part_out = lax.dot_general(hidden_act, logit_gradient, over_rows, preferred_element_type=F32).astype(BF16)
    hidden_grad = lax.dot_general(
        logit_gradient, w_out_p, (((1,), (1,)), ((), ())), preferred_element_type=F32
    )
    preact_grad = (hidden_grad * gelu_slope).astype(BF16)
    part_in = lax.dot_general(preact_grad, feats, over_rows, preferred_element_type=F32).astype(BF16)
    part_bias = jnp.sum(preact_grad, axis=0, dtype=F32).astype(BF16)
    packed = jnp.concatenate([part_out, jnp.broadcast_to(part_bias[:, None], (hid, TILE))], axis=1)
    feat_grad = jnp.dot(preact_grad, w_in_p, preferred_element_type=F32).astype(BF16)

    grad_scale = 1.0 / math.sqrt(2 * local_rows * count)
    g_out = scattered(packed.reshape(count, rows, -1), count, bits, [a] + img_bits + cap_bits) * grad_scale
    g_in = scattered(part_in.reshape(count, rows, f_in), count, bits, [a] + cap_bits + img_bits) * grad_scale
    width = cot_img.shape[1]
    return (feat_grad[:local_rows], feat_grad[local_rows:], g_in, g_out[:, :width], g_out[:, width])


def solution(mesh):
    rows = P(("img", "cap"), None)
    in_specs = (rows, rows, rows, rows, P(), P(), P(), rows, rows, P(("img", "cap")))
    out_specs = (rows, rows, rows, rows, P(("img", "cap")))
    return jax.shard_map(
        per_device, mesh=mesh, in_specs=in_specs, out_specs=out_specs, check_vma=False
    )
```

```python
import math

import jax
import jax.numpy as jnp
from jax import lax
from jax.experimental import pallas as pl
from jax.experimental.pallas import tpu as pltpu
from jax.sharding import PartitionSpec as P

TILE = 128
ALPHA = 0.1
AXES = ("img", "cap")
F32 = jnp.float32
BF16 = jnp.bfloat16


def gelu_parts(preact):
    normal_cdf = 0.5 * (1.0 + jax.scipy.special.erf(preact * 0.7071067811865476))
    normal_pdf = jnp.exp(-0.5 * preact * preact) * 0.3989422804014327
    return (preact * normal_cdf, normal_cdf + preact * normal_pdf)


def tiles_kernel(seed_ref, place_ref, count_ref, pat_ref, pat_t_ref, nimg_ref, ncap_ref, deg_ref, *, tiles, slots):
    all_tiles, mid = 7 * tiles, 5 * tiles
    deg_ref[...] = jnp.zeros_like(deg_ref)
    row = lax.broadcasted_iota(jnp.int32, (TILE, TILE), 0)
    col = lax.broadcasted_iota(jnp.int32, (TILE, TILE), 1)
    first, second = jnp.int32(668265261), jnp.int32(374761393)
    base = (row * 40503 + col * 9973) * first
    base_t = (col * 40503 + row * 9973) * first
    off_diag = row - col

    def pattern(start, seed, live, s):
        mixed = start + seed * first
        mixed = jnp.bitwise_xor(mixed, jnp.right_shift(mixed, 15))
        mixed = mixed * second
        mixed = jnp.bitwise_xor(mixed, jnp.right_shift(mixed, 13))
        edge = jnp.bitwise_and(mixed, 15) == jnp.where(live, 0, 16)
        if s == 0:
            edge = edge | (off_diag == jnp.where(live, 0, TILE))
        return jnp.where(edge, 1.0, 0.0)

    def one(q, full):
        total = None
        for s in range(slots):
            live = s < count_ref[q]
            seed = seed_ref[q * slots + s]
            e = pattern(base, seed, live, s)
            c = place_ref[q * slots + s]
            deg_ref[c] += jnp.sum(e, axis=0, keepdims=True)
            if full:
                m = q - tiles
                pat_ref[m, :, pl.ds(s * TILE, TILE)] = e.astype(BF16)
                pat_t_ref[m, pl.ds(s * TILE, TILE), :] = pattern(base_t, seed, live, s).astype(BF16)
                total = e if total is None else total + e
        if full:
            d = jnp.sum(total, axis=1, keepdims=True)
            n = jnp.where(d > 0.0, lax.rsqrt(d), 0.0)
            nimg_ref[q - tiles] = jnp.broadcast_to(n, (TILE, TILE))

    def edge_body(q, c):
        one(q, False)
        return c

    def mid_body(q, c):
        one(q, True)
        return c

    lax.fori_loop(0, tiles, edge_body, 0)
    lax.fori_loop(tiles, tiles + mid, mid_body, 0)
    lax.fori_loop(tiles + mid, all_tiles, edge_body, 0)
    for m in range(mid):
        d = deg_ref[m + 2 * tiles]
        n = jnp.where(d > 0.0, lax.rsqrt(d), 0.0)
        ncap_ref[m] = jnp.broadcast_to(n, (TILE, TILE)).T


def make_tiles(seeds, places, counts, tiles, slots):
    mid = 5 * tiles
    smem = pl.BlockSpec(memory_space=pltpu.SMEM)
    vmem = pl.BlockSpec(memory_space=pltpu.VMEM)
    return pl.pallas_call(
        lambda *r: tiles_kernel(*r, tiles=tiles, slots=slots),
        out_shape=(
            jax.ShapeDtypeStruct((mid, TILE, slots * TILE), BF16),
            jax.ShapeDtypeStruct((mid, slots * TILE, TILE), BF16),
            jax.ShapeDtypeStruct((mid, TILE, TILE), F32),
            jax.ShapeDtypeStruct((mid, TILE, TILE), F32),
        ),
        in_specs=[smem] * 3,
        out_specs=(vmem,) * 4,
        scratch_shapes=[pltpu.VMEM((9 * tiles, 1, TILE), F32)],
        compiler_params=pltpu.CompilerParams(vmem_limit_bytes=40 << 20),
        name="tiles",
    )(seeds, places, counts)


def hops_kernel(
    place_ref, base_ref, own_img, own_cap, low_hbm, high_hbm, mate_hbm, far_hbm, pat_ref, pat_t_ref, nimg_ref, ncap_ref,
    out_ref, bands, img0, cap0, img1, cap1, acc, acc2, keep_img, keep_cap, sems, *, tiles, slots, width,
):
    mid = 5 * tiles
    near = 3 * tiles
    keep = 1.0 - ALPHA
    copies = [
        pltpu.make_async_copy(src, bands.at[k], sems.at[k])
        for k, src in enumerate((low_hbm, high_hbm, mate_hbm, far_hbm))
    ]
    for copy in copies:
        copy.start()

    def wide(n_ref, m):
        n = n_ref[m]
        return jnp.concatenate([n] * (width // TILE), axis=1)

    def scale(rows_img, rows_cap, base):
        for t in range(tiles):
            m = base + t
            img0[m] = (rows_img(t).astype(F32) * wide(nimg_ref, m)).astype(BF16)
            cap0[m] = (rows_cap(t).astype(F32) * wide(ncap_ref, m)).astype(BF16)

    def both(k):
        return (lambda t: bands[k, pl.ds(t * TILE, TILE), :]), (lambda t: bands[k, pl.ds((tiles + t) * TILE, TILE), :])

    acc[...] = jnp.zeros_like(acc)
    acc2[...] = jnp.zeros_like(acc2)
    scale(lambda t: own_img[pl.ds(t * TILE, TILE), :], lambda t: own_cap[pl.ds(t * TILE, TILE), :], 2 * tiles)
    for k, base in enumerate((0, 4 * tiles, base_ref[0], base_ref[1])):
        copies[k].wait()
        scale(*both(k), base)

    def push(q, state, target, lo, count):
        r = jnp.dot(pat_t_ref[q], state, preferred_element_type=F32)
        for s in range(slots):
            c = place_ref[q * slots + s] - lo
            c = jnp.where((c >= 0) & (c < count), c, count)
            target[c] += r[s * TILE : (s + 1) * TILE]

    def pull(q, source, lo):
        total = None
        for s in range(slots):
            c = place_ref[q * slots + s] - lo
            r = jnp.dot(pat_ref[q, :, pl.ds(s * TILE, TILE)], source[c], preferred_element_type=F32)
            total = r if total is None else total + r
        return total

    def push1(q, c):
        push(q, img0[q], acc, tiles, near)
        return c

    lax.fori_loop(0, mid, push1, 0)

    def pull1(q, c):
        n = wide(nimg_ref, q)
        flow = keep * n * pull(q, cap0, 0)
        img1[q - tiles] = (flow * n).astype(BF16)
        keep_img[q - tiles] = flow
        return c

    lax.fori_loop(tiles, tiles + near, pull1, 0)

    def finish1(m, c):
        n = wide(ncap_ref, m + tiles)
        flow = keep * n * acc[m]
        cap1[m] = (flow * n).astype(BF16)
        keep_cap[m] = flow
        return c

    lax.fori_loop(0, near, finish1, 0)

    def push2(q, c):
        push(q, img1[q - tiles], acc2, 2 * tiles, tiles)
        return c

    lax.fori_loop(tiles, tiles + near, push2, 0)
    for t in range(tiles):
        q = 2 * tiles + t
        rows = pl.ds(t * TILE, TILE)
        flow = keep * wide(nimg_ref, q) * pull(q, cap1, tiles)
        out_ref[rows, :] = (ALPHA * (own_img[rows, :].astype(F32) + keep_img[tiles + t]) + flow).astype(BF16)
        flow = keep * wide(ncap_ref, q) * acc2[t]
        out_ref[pl.ds((tiles + t) * TILE, TILE), :] = (
            ALPHA * (own_cap[rows, :].astype(F32) + keep_cap[tiles + t]) + flow
        ).astype(BF16)


def propagate(places, bases, own_img, own_cap, low, high, mate, far, pats, tiles, slots):
    width = own_img.shape[1]
    smem = pl.BlockSpec(memory_space=pltpu.SMEM)
    vmem = pl.BlockSpec(memory_space=pltpu.VMEM)
    hbm = pl.BlockSpec(memory_space=pl.ANY)
    mid, near = 5 * tiles, 3 * tiles
    return pl.pallas_call(
        lambda *r: hops_kernel(*r, tiles=tiles, slots=slots, width=width),
        out_shape=jax.ShapeDtypeStruct(low.shape, BF16),
        in_specs=[smem] * 2 + [vmem] * 2 + [hbm] * 4 + [vmem] * 4,
        out_specs=vmem,
        scratch_shapes=[
            pltpu.VMEM((4,) + low.shape, BF16),
            pltpu.VMEM((mid, TILE, width), BF16),
            pltpu.VMEM((mid, TILE, width), BF16),
            pltpu.VMEM((near, TILE, width), BF16),
            pltpu.VMEM((near, TILE, width), BF16),
            pltpu.VMEM((near + 1, TILE, width), F32),
            pltpu.VMEM((tiles + 1, TILE, width), F32),
            pltpu.VMEM((near, TILE, width), F32),
            pltpu.VMEM((near, TILE, width), F32),
            pltpu.SemaphoreType.DMA((4,)),
        ],
        compiler_params=pltpu.CompilerParams(vmem_limit_bytes=56 << 20),
        name="hops",
    )(places, bases, own_img, own_cap, low, high, mate, far, *pats)


BLOCK = 64
GROUP = 4


def grouped(width):
    return [
        pl.BlockSpec((BLOCK, width), lambda i, order, k=k: (order[i * GROUP + k], 0)) for k in range(GROUP)
    ]


def stacked(refs):
    return jnp.concatenate([r[...] for r in refs], axis=0)


def whole(shape):
    return pl.BlockSpec(shape, lambda i, order: (0,) * len(shape))


def out_kernel(order_ref, *refs):
    act, (logit_ref, part_ref) = refs[:GROUP], refs[GROUP:]
    part_ref[...] = jnp.dot(stacked(act), logit_ref[...], preferred_element_type=F32).astype(BF16)


def in_kernel(order_ref, *refs):
    slope, w_out = refs[:GROUP], refs[GROUP : 2 * GROUP]
    logit_ref, feats_ref, part_ref, grad_ref = refs[2 * GROUP :]
    hidden = lax.dot_general(
        stacked(w_out), logit_ref[...], (((1,), (1,)), ((), ())), preferred_element_type=F32
    )
    grad = (hidden * stacked(slope)).astype(BF16)
    grad_ref[...] = grad
    f_in = feats_ref.shape[1]
    part_ref[:, :f_in] = jnp.dot(grad, feats_ref[...], preferred_element_type=F32).astype(BF16)
    bias = jnp.sum(grad.astype(F32), axis=1, keepdims=True)
    part_ref[:, f_in:] = jnp.broadcast_to(bias, (bias.shape[0], TILE)).astype(BF16)


def feat_kernel(order_ref, *refs):
    w_in = refs[:GROUP]
    grad_ref, img_ref, cap_ref, acc_ref = refs[GROUP:]
    i = pl.program_id(0)

    @pl.when(i == 0)
    def _():
        acc_ref[...] = jnp.zeros_like(acc_ref)

    acc_ref[...] += lax.dot_general(
        grad_ref[...], stacked(w_in), (((0,), (0,)), ((), ())), preferred_element_type=F32
    )

    @pl.when(i == pl.num_programs(0) - 1)
    def _():
        half = img_ref.shape[0]
        img_ref[...] = acc_ref[:half].astype(BF16)
        cap_ref[...] = acc_ref[half:].astype(BF16)


def over_hidden(kernel, name, order, in_specs, out_specs, out_shape, scratch, args):
    return pl.pallas_call(
        kernel,
        out_shape=out_shape,
        grid_spec=pltpu.PrefetchScalarGridSpec(
            num_scalar_prefetch=1,
            grid=(order.shape[0] // GROUP,),
            in_specs=in_specs,
            out_specs=out_specs,
            scratch_shapes=scratch,
        ),
        compiler_params=pltpu.CompilerParams(
            dimension_semantics=("arbitrary",), vmem_limit_bytes=40 << 20
        ),
        name=name,
    )(order, *args)


def rows_of(width):
    return pl.BlockSpec((GROUP * BLOCK, width), lambda i, order: (i, 0))


def moved(array, count, by):
    return lax.ppermute(array, AXES, [(i, i + by) for i in range(count) if 0 <= i + by < count])


def flipped(array, count, mask):
    return lax.ppermute(array, AXES, [(i, i ^ mask) for i in range(count)])


def halve(array, axis, count, mask):
    kept = lax.index_in_dim(array, 0, axis, keepdims=False)
    sent = lax.index_in_dim(array, 1, axis, keepdims=False)
    return (kept.astype(F32) + flipped(sent, count, mask).astype(F32)).astype(BF16)


def nearest_pair(count, by):
    return [(i, i + by) for i in range(0, count - by, 2)] + [(i, i - by) for i in range(by + 1, count, 2)]


def scattered(part, count, bits, order):
    rows, lanes = part.shape[-2:]
    left = list(bits)
    for bit in order:
        part = halve(part, left.index(bit), count, 1 << bit)
        left.remove(bit)
    part = part.reshape((4, rows, lanes))
    got = [flipped(part[k], count, ((k >> 1) << left[0]) | ((k & 1) << left[1])) for k in range(1, 4)]
    total = part[0].astype(F32)
    for piece in got:
        total = total + piece.astype(F32)
    return total


def per_device(
    feats_img, feats_cap, cot_img, cot_cap, w_in, b_in, w_out, tile_seed, tile_cols, tile_count
):
    local_rows = feats_img.shape[0]
    tiles = local_rows // TILE
    slots = tile_seed.shape[1]
    hid, f_in = w_in.shape
    n_img, n_cap = lax.axis_size("img"), lax.axis_size("cap")
    count = n_img * n_cap
    me = lax.axis_index(AXES)

    block = jnp.concatenate([cot_img, cot_cap], axis=0)
    mate = flipped(block, count, 1)
    low = moved(block, count, 2)
    high = moved(block, count, -2)
    far = lax.ppermute(mate, AXES, nearest_pair(count, 2))
    even = (me & 1) == 0
    meta = jnp.concatenate([tile_seed, tile_cols, tile_count[:, None]], axis=1)
    other = flipped(meta, count, 1)
    pair = jnp.where(even, jnp.concatenate([meta, other]), jnp.concatenate([other, meta]))
    pair_low = moved(pair, count, 2)
    pair_high = moved(pair, count, -2)
    pair_far = lax.ppermute(pair, AXES, nearest_pair(count, 4))
    wide = jnp.where(
        even,
        jnp.concatenate([pair_far[tiles:], pair_low, pair, pair_high]),
        jnp.concatenate([pair_low, pair, pair_high, pair_far[:tiles]]),
    )
    frame = jnp.arange(7 * tiles, dtype=jnp.int32)[:, None]
    counts = wide[:, 2 * slots]
    seeds = wide[:, :slots].reshape(-1)
    places = jnp.where(counts[:, None] > 0, wide[:, slots : 2 * slots] - (me - 3) * tiles, frame)
    pats = make_tiles(seeds, (places + tiles).reshape(-1), counts, tiles, slots)

    m = count.bit_length() - 1
    a = n_cap.bit_length() - 1
    cap_bits = list(range(a))
    img_bits = list(range(a + 1, m - 2))
    bits = [a] + cap_bits + img_bits + [m - 1, m - 2]
    pos = jnp.arange(count, dtype=jnp.int32)
    order = jnp.zeros_like(pos)
    for k, bit in enumerate(bits):
        order = order | (((pos >> (m - 1 - k)) & 1) << bit)
    order = order ^ me
    rows = hid // count
    if rows % BLOCK:
        w_in, w_out, b_in = [
            jnp.take(v.reshape((count, rows) + v.shape[1:]), order, axis=0).reshape(v.shape) for v in (w_in, w_out, b_in)
        ]
        order = jnp.arange(hid // BLOCK, dtype=jnp.int32)
    else:
        order = (order[:, None] * (rows // BLOCK) + jnp.arange(rows // BLOCK, dtype=jnp.int32)).reshape(-1)

    feats = jnp.concatenate([feats_img, feats_cap], axis=0)
    across = (((1,), (1,)), ((), ()))
    preact = lax.dot_general(w_in, feats, across, preferred_element_type=F32) + b_in[:, None]
    gelu_value, gelu_slope = gelu_parts(preact)
    hidden_act, gelu_slope = lax.optimization_barrier((gelu_value.astype(BF16), gelu_slope))

    bases = jnp.where(even, jnp.array([3, 1]), jnp.array([1, 3])).astype(jnp.int32) * tiles
    mid_places = (places - tiles)[tiles : 6 * tiles].reshape(-1)
    logit = propagate(mid_places, bases, cot_img, cot_cap, low, high, mate, far, pats, tiles, slots)

    width = cot_img.shape[1]
    nodes = 2 * local_rows
    part_out = over_hidden(
        out_kernel, "part_out", order, grouped(nodes) + [whole(logit.shape)], rows_of(width),
        jax.ShapeDtypeStruct((hid, width), BF16), [], [hidden_act] * GROUP + [logit],
    )
    part_in, preact_grad = over_hidden(
        in_kernel, "part_in", order,
        grouped(nodes) + grouped(width) + [whole(logit.shape), whole(feats.shape)],
        (rows_of(f_in + TILE), rows_of(nodes)),
        (jax.ShapeDtypeStruct((hid, f_in + TILE), BF16), jax.ShapeDtypeStruct((hid, nodes), BF16)),
        [], [gelu_slope] * GROUP + [w_out] * GROUP + [logit, feats],
    )
    grad_img, grad_cap = over_hidden(
        feat_kernel, "feat_grad", order, grouped(f_in) + [rows_of(nodes)],
        (whole((local_rows, f_in)),) * 2, (jax.ShapeDtypeStruct((local_rows, f_in), BF16),) * 2,
        [pltpu.VMEM((nodes, f_in), F32)], [w_in] * GROUP + [preact_grad],
    )

    grad_scale = 1.0 / math.sqrt(nodes * count)
    blocked = (2,) * m + (rows,)
    rest = bits[1:]
    g_out = halve(part_out.reshape(blocked + (width,)), 0, count, 1 << a)
    g_in = halve(part_in.reshape(blocked + (f_in + TILE,)), 0, count, 1 << a)
    cut = f_in // 2
    g_out = scattered(g_out, count, rest, img_bits + cap_bits) * grad_scale
    g_a = scattered(g_in[..., :cut], count, rest, img_bits + cap_bits) * grad_scale
    g_b = scattered(g_in[..., cut:], count, rest, cap_bits + img_bits) * grad_scale
    g_in = jnp.concatenate([g_a, g_b[:, : f_in - cut]], axis=1)
    return (grad_img, grad_cap, g_in, g_out, g_b[:, f_in - cut])


def solution(mesh):
    rows = P(("img", "cap"), None)
    in_specs = (rows, rows, rows, rows, P(), P(), P(), rows, rows, P(("img", "cap")))
    out_specs = (rows, rows, rows, rows, P(("img", "cap")))
    return jax.shard_map(
        per_device, mesh=mesh, in_specs=in_specs, out_specs=out_specs, check_vma=False
    )
```

```python
import math

import jax
import jax.numpy as jnp
from jax import lax
from jax.experimental import pallas as pl
from jax.experimental.pallas import tpu as pltpu
from jax.sharding import PartitionSpec as P

TILE = 128
ALPHA = 0.1
SHORT = pl.CostEstimate(flops=1, transcendentals=0, bytes_accessed=1)
AXES = ("img", "cap")
F32 = jnp.float32
BF16 = jnp.bfloat16


def gelu_parts(preact):
    normal_cdf = 0.5 * (1.0 + jax.scipy.special.erf(preact * 0.7071067811865476))
    normal_pdf = jnp.exp(-0.5 * preact * preact) * 0.3989422804014327
    return (preact * normal_cdf, normal_cdf + preact * normal_pdf)


def tiles_kernel(seed_ref, place_ref, count_ref, pat_ref, pat_t_ref, nimg_ref, ncap_ref, deg_ref, *, tiles, slots):
    all_tiles, mid = 7 * tiles, 5 * tiles
    deg_ref[...] = jnp.zeros_like(deg_ref)
    row = lax.broadcasted_iota(jnp.int32, (TILE, TILE), 0)
    col = lax.broadcasted_iota(jnp.int32, (TILE, TILE), 1)
    first, second = jnp.int32(668265261), jnp.int32(374761393)
    base = (row * 40503 + col * 9973) * first
    base_t = (col * 40503 + row * 9973) * first
    off_diag = row - col

    def pattern(start, seed, live, s):
        mixed = start + seed * first
        mixed = jnp.bitwise_xor(mixed, jnp.right_shift(mixed, 15))
        mixed = mixed * second
        mixed = jnp.bitwise_xor(mixed, jnp.right_shift(mixed, 13))
        edge = jnp.bitwise_and(mixed, 15) == jnp.where(live, 0, 16)
        if s == 0:
            edge = edge | (off_diag == jnp.where(live, 0, TILE))
        return jnp.where(edge, 1.0, 0.0)

    def one(q, full):
        total = None
        for s in range(slots):
            live = s < count_ref[q]
            seed = seed_ref[q * slots + s]
            e = pattern(base, seed, live, s)
            c = place_ref[q * slots + s]
            deg_ref[c] += jnp.sum(e, axis=0, keepdims=True)
            if full:
                m = q - tiles
                pat_ref[m, :, pl.ds(s * TILE, TILE)] = e.astype(BF16)
                pat_t_ref[m, pl.ds(s * TILE, TILE), :] = pattern(base_t, seed, live, s).astype(BF16)
                total = e if total is None else total + e
        if full:
            d = jnp.sum(total, axis=1, keepdims=True)
            n = jnp.where(d > 0.0, lax.rsqrt(d), 0.0)
            nimg_ref[q - tiles] = jnp.broadcast_to(n, (TILE, TILE))

    def edge_body(q, c):
        one(q, False)
        return c

    def mid_body(q, c):
        one(q, True)
        return c

    lax.fori_loop(0, tiles, edge_body, 0)
    lax.fori_loop(tiles, tiles + mid, mid_body, 0)
    lax.fori_loop(tiles + mid, all_tiles, edge_body, 0)
    for m in range(mid):
        d = deg_ref[m + 2 * tiles]
        n = jnp.where(d > 0.0, lax.rsqrt(d), 0.0)
        ncap_ref[m] = jnp.broadcast_to(n, (TILE, TILE)).T


def make_tiles(seeds, places, counts, tiles, slots):
    mid = 5 * tiles
    smem = pl.BlockSpec(memory_space=pltpu.SMEM)
    vmem = pl.BlockSpec(memory_space=pltpu.VMEM)
    return pl.pallas_call(
        lambda *r: tiles_kernel(*r, tiles=tiles, slots=slots),
        out_shape=(
            jax.ShapeDtypeStruct((mid, TILE, slots * TILE), BF16),
            jax.ShapeDtypeStruct((mid, slots * TILE, TILE), BF16),
            jax.ShapeDtypeStruct((mid, TILE, TILE), F32),
            jax.ShapeDtypeStruct((mid, TILE, TILE), F32),
        ),
        in_specs=[smem] * 3,
        out_specs=(vmem,) * 4,
        scratch_shapes=[pltpu.VMEM((9 * tiles, 1, TILE), F32)],
        compiler_params=pltpu.CompilerParams(vmem_limit_bytes=28 << 20),
        cost_estimate=SHORT,
        name="tiles",
    )(seeds, places, counts)


def hops_kernel(
    place_ref, base_ref, own_img, own_cap, low_hbm, high_hbm, mate_hbm, far_hbm, pat_ref, pat_t_ref, nimg_ref, ncap_ref,
    out_ref, bands, img0, cap0, img1, cap1, acc, acc2, keep_img, keep_cap, sems, *, tiles, slots, width,
):
    mid = 5 * tiles
    near = 3 * tiles
    keep = 1.0 - ALPHA
    copies = [
        pltpu.make_async_copy(src, bands.at[k], sems.at[k])
        for k, src in enumerate((low_hbm, high_hbm, mate_hbm, far_hbm))
    ]
    for copy in copies:
        copy.start()

    def wide(n_ref, m):
        n = n_ref[m]
        return jnp.concatenate([n] * (width // TILE), axis=1)

    def scale(rows_img, rows_cap, base):
        for t in range(tiles):
            m = base + t
            img0[m] = (rows_img(t).astype(F32) * wide(nimg_ref, m)).astype(BF16)
            cap0[m] = (rows_cap(t).astype(F32) * wide(ncap_ref, m)).astype(BF16)

    def both(k):
        return (lambda t: bands[k, pl.ds(t * TILE, TILE), :]), (lambda t: bands[k, pl.ds((tiles + t) * TILE, TILE), :])

    acc[...] = jnp.zeros_like(acc)
    acc2[...] = jnp.zeros_like(acc2)
    scale(lambda t: own_img[pl.ds(t * TILE, TILE), :], lambda t: own_cap[pl.ds(t * TILE, TILE), :], 2 * tiles)
    for k, base in enumerate((0, 4 * tiles, base_ref[0], base_ref[1])):
        copies[k].wait()
        scale(*both(k), base)

    def push(q, state, target, lo, count):
        r = jnp.dot(pat_t_ref[q], state, preferred_element_type=F32)
        for s in range(slots):
            c = place_ref[q * slots + s] - lo
            c = jnp.where((c >= 0) & (c < count), c, count)
            target[c] += r[s * TILE : (s + 1) * TILE]

    def pull(q, source, lo):
        total = None
        for s in range(slots):
            c = place_ref[q * slots + s] - lo
            r = jnp.dot(pat_ref[q, :, pl.ds(s * TILE, TILE)], source[c], preferred_element_type=F32)
            total = r if total is None else total + r
        return total

    def push1(q, c):
        push(q, img0[q], acc, tiles, near)
        return c

    lax.fori_loop(0, mid, push1, 0, unroll=3)

    def pull1(q, c):
        n = wide(nimg_ref, q)
        flow = keep * n * pull(q, cap0, 0)
        img1[q - tiles] = (flow * n).astype(BF16)
        keep_img[q - tiles] = flow
        return c

    lax.fori_loop(tiles, tiles + near, pull1, 0, unroll=3)

    def finish1(m, c):
        n = wide(ncap_ref, m + tiles)
        flow = keep * n * acc[m]
        cap1[m] = (flow * n).astype(BF16)
        keep_cap[m] = flow
        return c

    lax.fori_loop(0, near, finish1, 0, unroll=3)

    def push2(q, c):
        push(q, img1[q - tiles], acc2, 2 * tiles, tiles)
        return c

    lax.fori_loop(tiles, tiles + near, push2, 0, unroll=3)
    for t in range(tiles):
        q = 2 * tiles + t
        rows = pl.ds(t * TILE, TILE)
        flow = keep * wide(nimg_ref, q) * pull(q, cap1, tiles)
        out_ref[rows, :] = (ALPHA * (own_img[rows, :].astype(F32) + keep_img[tiles + t]) + flow).astype(BF16)
        flow = keep * wide(ncap_ref, q) * acc2[t]
        out_ref[pl.ds((tiles + t) * TILE, TILE), :] = (
            ALPHA * (own_cap[rows, :].astype(F32) + keep_cap[tiles + t]) + flow
        ).astype(BF16)


def propagate(places, bases, own_img, own_cap, low, high, mate, far, pats, tiles, slots):
    width = own_img.shape[1]
    smem = pl.BlockSpec(memory_space=pltpu.SMEM)
    vmem = pl.BlockSpec(memory_space=pltpu.VMEM)
    hbm = pl.BlockSpec(memory_space=pltpu.HBM)
    mid, near = 5 * tiles, 3 * tiles
    return pl.pallas_call(
        lambda *r: hops_kernel(*r, tiles=tiles, slots=slots, width=width),
        out_shape=jax.ShapeDtypeStruct(low.shape, BF16),
        in_specs=[smem] * 2 + [vmem] * 2 + [hbm] * 4 + [vmem] * 4,
        out_specs=vmem,
        scratch_shapes=[
            pltpu.VMEM((4,) + low.shape, BF16),
            pltpu.VMEM((mid, TILE, width), BF16),
            pltpu.VMEM((mid, TILE, width), BF16),
            pltpu.VMEM((near, TILE, width), BF16),
            pltpu.VMEM((near, TILE, width), BF16),
            pltpu.VMEM((near + 1, TILE, width), F32),
            pltpu.VMEM((tiles + 1, TILE, width), F32),
            pltpu.VMEM((near, TILE, width), F32),
            pltpu.VMEM((near, TILE, width), F32),
            pltpu.SemaphoreType.DMA((4,)),
        ],
        compiler_params=pltpu.CompilerParams(vmem_limit_bytes=32 << 20),
        cost_estimate=SHORT,
        name="hops",
    )(places, bases, own_img, own_cap, low, high, mate, far, *pats)


BLOCK = 64
GROUP = 4


def grouped(width):
    return [
        pl.BlockSpec((BLOCK, width), lambda i, order, k=k: (order[i * GROUP + k], 0)) for k in range(GROUP)
    ]


def stacked(refs):
    return jnp.concatenate([r[...] for r in refs], axis=0)


def whole(shape):
    return pl.BlockSpec(shape, lambda i, order: (0,) * len(shape))


def out_kernel(order_ref, *refs):
    act, (logit_ref, part_ref) = refs[:GROUP], refs[GROUP:]
    part_ref[...] = jnp.dot(stacked(act), logit_ref[...], preferred_element_type=F32).astype(BF16)


def in_kernel(order_ref, *refs):
    slope, w_out = refs[:GROUP], refs[GROUP : 2 * GROUP]
    logit_ref, feats_ref, part_ref, grad_ref = refs[2 * GROUP :]
    hidden = lax.dot_general(
        stacked(w_out), logit_ref[...], (((1,), (1,)), ((), ())), preferred_element_type=F32
    )
    grad = (hidden * stacked(slope)).astype(BF16)
    grad_ref[...] = grad
    f_in = feats_ref.shape[1]
    part_ref[:, :f_in] = jnp.dot(grad, feats_ref[...], preferred_element_type=F32).astype(BF16)
    bias = jnp.sum(grad.astype(F32), axis=1, keepdims=True)
    part_ref[:, f_in:] = jnp.broadcast_to(bias, (bias.shape[0], TILE)).astype(BF16)


def feat_kernel(order_ref, *refs):
    w_in = refs[:GROUP]
    kept_ref, sent_ref, img_ref, cap_ref, acc_ref = refs[GROUP:]
    i = pl.program_id(0)
    steps = pl.num_programs(0)

    @pl.when(i == 0)
    def _():
        acc_ref[...] = jnp.zeros_like(acc_ref)

    grad = jnp.where(i < steps // 2, kept_ref[...], sent_ref[...])
    acc_ref[...] += lax.dot_general(
        grad, stacked(w_in), (((0,), (0,)), ((), ())), preferred_element_type=F32
    )

    @pl.when(i == steps - 1)
    def _():
        half = img_ref.shape[0]
        img_ref[...] = acc_ref[:half].astype(BF16)
        cap_ref[...] = acc_ref[half:].astype(BF16)


def over_hidden(kernel, name, order, in_specs, out_specs, out_shape, scratch, args):
    return pl.pallas_call(
        kernel,
        out_shape=out_shape,
        grid_spec=pltpu.PrefetchScalarGridSpec(
            num_scalar_prefetch=1,
            grid=(order.shape[0] // GROUP,),
            in_specs=in_specs,
            out_specs=out_specs,
            scratch_shapes=scratch,
        ),
        compiler_params=pltpu.CompilerParams(
            dimension_semantics=("arbitrary",), vmem_limit_bytes=28 << 20
        ),
        cost_estimate=SHORT,
        name=name,
    )(order, *args)


def rows_of_half(width, half, side):
    steps = half // GROUP
    if side:
        return pl.BlockSpec((GROUP * BLOCK, width), lambda i, order: (jnp.maximum(i - steps, 0), 0))
    return pl.BlockSpec((GROUP * BLOCK, width), lambda i, order: (jnp.minimum(i, steps - 1), 0))


def rows_of(width):
    return pl.BlockSpec((GROUP * BLOCK, width), lambda i, order: (i, 0))


def stack_kernel(top_ref, bottom_ref, out_ref, sems):
    half = top_ref.shape[0]
    copies = [
        pltpu.make_async_copy(src, out_ref.at[pl.ds(k * half, half)], sems.at[k])
        for k, src in enumerate((top_ref, bottom_ref))
    ]
    for copy in copies:
        copy.start()
    for copy in copies:
        copy.wait()


def stack(top, bottom):
    hbm = pl.BlockSpec(memory_space=pltpu.HBM)
    return pl.pallas_call(
        stack_kernel,
        out_shape=jax.ShapeDtypeStruct((2 * top.shape[0], top.shape[1]), top.dtype),
        in_specs=[hbm] * 2,
        out_specs=hbm,
        scratch_shapes=[pltpu.SemaphoreType.DMA((2,))],
        cost_estimate=SHORT,
        name="stack",
    )(top, bottom)


def after(value, *done):
    return lax.optimization_barrier((value,) + done)[0]


def moved(array, count, by):
    return lax.ppermute(array, AXES, [(i, i + by) for i in range(count) if 0 <= i + by < count])


def flipped(array, count, mask):
    return lax.ppermute(array, AXES, [(i, i ^ mask) for i in range(count)])


def added(kept, came):
    return (kept.astype(F32) + came.astype(F32)).astype(BF16)


def parts(array, axis):
    return lax.index_in_dim(array, 0, axis, keepdims=False), lax.index_in_dim(array, 1, axis, keepdims=False)


def meet(values, owners):
    for owner, value in zip(owners, lax.optimization_barrier(tuple(values))):
        owner.part = value


def nearest_pair(count, by):
    return [(i, i + by) for i in range(0, count - by, 2)] + [(i, i - by) for i in range(by + 1, count, 2)]


class Reduction:

    def __init__(self, part, count, bits, order):
        self.part, self.count, self.left, self.order = part, count, list(bits), list(order)

    def start(self):
        bit = self.order.pop(0)
        self.kept, sent = parts(self.part, self.left.index(bit))
        self.left.remove(bit)
        self.came = flipped(sent, self.count, 1 << bit)

    def finish(self):
        self.part = added(self.kept, self.came)
        return self.part

    def start_last(self):
        part = self.part.reshape((4,) + self.part.shape[-2:])
        hi, lo = self.left
        self.own = part[0]
        self.got = [flipped(part[k], self.count, ((k >> 1) << hi) | ((k & 1) << lo)) for k in range(1, 4)]

    def result(self):
        total = self.own.astype(F32)
        for piece in self.got:
            total = total + piece.astype(F32)
        return total


def per_device(
    feats_img, feats_cap, cot_img, cot_cap, w_in, b_in, w_out, tile_seed, tile_cols, tile_count
):
    local_rows = feats_img.shape[0]
    tiles = local_rows // TILE
    slots = tile_seed.shape[1]
    hid, f_in = w_in.shape
    n_img, n_cap = lax.axis_size("img"), lax.axis_size("cap")
    count = n_img * n_cap
    me = lax.axis_index(AXES)

    even = (me & 1) == 0
    meta = jnp.concatenate([tile_seed, tile_cols, tile_count[:, None]], axis=1)
    other = flipped(meta, count, 1)
    block = stack(cot_img, cot_cap)
    mate = flipped(block, count, 1)
    low = moved(block, count, 2)
    high = moved(block, count, -2)
    far = lax.ppermute(mate, AXES, nearest_pair(count, 2))
    pair = jnp.where(even, jnp.concatenate([meta, other]), jnp.concatenate([other, meta]))
    pair_low = moved(pair, count, 2)
    pair_high = moved(pair, count, -2)
    pair_far = lax.ppermute(pair, AXES, nearest_pair(count, 4))
    wide = jnp.where(
        even,
        jnp.concatenate([pair_far[tiles:], pair_low, pair, pair_high]),
        jnp.concatenate([pair_low, pair, pair_high, pair_far[:tiles]]),
    )
    frame = jnp.arange(7 * tiles, dtype=jnp.int32)[:, None]
    counts = wide[:, 2 * slots]
    seeds = wide[:, :slots].reshape(-1)
    places = jnp.where(counts[:, None] > 0, wide[:, slots : 2 * slots] - (me - 3) * tiles, frame)
    pats = make_tiles(seeds, (places + tiles).reshape(-1), counts, tiles, slots)

    m = count.bit_length() - 1
    a = n_cap.bit_length() - 1
    cap_bits = list(range(a))
    img_bits = list(range(a + 1, m - 2))
    bits = [a] + cap_bits + img_bits + [m - 1, m - 2]
    pos = jnp.arange(count, dtype=jnp.int32)
    order = jnp.zeros_like(pos)
    for k, bit in enumerate(bits):
        order = order | (((pos >> (m - 1 - k)) & 1) << bit)
    order = order ^ me
    rows = hid // count
    if rows % BLOCK:
        w_in, w_out, b_in = [
            jnp.take(v.reshape((count, rows) + v.shape[1:]), order, axis=0).reshape(v.shape) for v in (w_in, w_out, b_in)
        ]
        order = jnp.arange(hid // BLOCK, dtype=jnp.int32)
    else:
        order = (order[:, None] * (rows // BLOCK) + jnp.arange(rows // BLOCK, dtype=jnp.int32)).reshape(-1)

    feats = jnp.concatenate([feats_img, feats_cap], axis=0)
    across = (((1,), (1,)), ((), ()))
    preact = lax.dot_general(w_in, feats, across, preferred_element_type=F32) + b_in[:, None]
    gelu_value, gelu_slope = gelu_parts(preact)
    hidden_act, gelu_slope = lax.optimization_barrier((gelu_value.astype(BF16), gelu_slope))

    bases = jnp.where(even, jnp.array([3, 1]), jnp.array([1, 3])).astype(jnp.int32) * tiles
    mid_places = (places - tiles)[tiles : 6 * tiles].reshape(-1)
    logit = propagate(mid_places, bases, cot_img, cot_cap, low, high, mate, far, pats, tiles, slots)

    width = cot_img.shape[1]
    nodes = 2 * local_rows
    half = order.shape[0] // 2
    blocked = (2,) * (m - 1) + (rows,)

    def out_half(order, logit):
        return over_hidden(
            out_kernel, "part_out", order, grouped(nodes) + [whole(logit.shape)], rows_of(width),
            jax.ShapeDtypeStruct((hid // 2, width), BF16), [], [hidden_act] * GROUP + [logit],
        ).reshape(blocked + (width,))

    def in_half(order, logit):
        part, grad = over_hidden(
            in_kernel, "part_in", order,
            grouped(nodes) + grouped(width) + [whole(logit.shape), whole(feats.shape)],
            (rows_of(f_in + TILE), rows_of(nodes)),
            (jax.ShapeDtypeStruct((hid // 2, f_in + TILE), BF16), jax.ShapeDtypeStruct((hid // 2, nodes), BF16)),
            [], [gelu_slope] * GROUP + [w_out] * GROUP + [logit, feats],
        )
        return part.reshape(blocked + (f_in + TILE,)), grad

    core = 1 << a
    rest = bits[1:]
    out_sent = out_half(order[half:], logit)
    out_came = flipped(out_sent, count, core)
    out_kept = out_half(order[:half], after(logit, out_sent))
    r_out = Reduction(added(out_kept, out_came), count, rest, img_bits + cap_bits)
    r_out.start()
    in_sent, grad_sent = in_half(order[half:], after(logit, r_out.part))
    in_came = flipped(in_sent, count, core)
    in_kept, grad_kept = in_half(order[:half], after(logit, grad_sent))
    g_in = added(in_kept, in_came)
    cut = f_in // 3
    r_a = Reduction(g_in[..., :cut], count, rest, img_bits + cap_bits)
    r_b = Reduction(g_in[..., cut:], count, rest, cap_bits + img_bits)
    r_a.start()
    r_b.start()
    grad_kept = after(grad_kept, g_in)
    grad_img, grad_cap = over_hidden(
        feat_kernel, "feat_grad", order, grouped(f_in) + [rows_of_half(nodes, half, 0), rows_of_half(nodes, half, 1)],
        (whole((local_rows, f_in)),) * 2, (jax.ShapeDtypeStruct((local_rows, f_in), BF16),) * 2,
        [pltpu.VMEM((nodes, f_in), F32)], [w_in] * GROUP + [grad_kept, grad_sent],
    )
    chunks = (r_out, r_a, r_b)
    for _ in range(m - 4):
        meet([r.finish() for r in chunks], chunks)
        for r in chunks:
            r.start()
    meet([r.finish() for r in chunks], chunks)
    for r in chunks:
        r.start_last()
    grad_scale = 1.0 / math.sqrt(nodes * count)
    g_out, g_b, g_a = [r.result() * grad_scale for r in (r_out, r_b, r_a)]
    g_in = jnp.concatenate([g_a, g_b[:, : f_in - cut]], axis=1)
    return (grad_img, grad_cap, g_in, g_out, g_b[:, f_in - cut])


def solution(mesh):
    rows = P(("img", "cap"), None)
    in_specs = (rows, rows, rows, rows, P(), P(), P(), rows, rows, P(("img", "cap")))
    out_specs = (rows, rows, rows, rows, P(("img", "cap")))
    return jax.shard_map(
        per_device, mesh=mesh, in_specs=in_specs, out_specs=out_specs, check_vma=False
    )
```

```python
import math

import jax
import jax.numpy as jnp
from jax import lax
from jax.experimental import pallas as pl
from jax.experimental.pallas import tpu as pltpu
from jax.sharding import PartitionSpec as P

TILE = 128
ALPHA = 0.1
SHORT = pl.CostEstimate(flops=1, transcendentals=0, bytes_accessed=1)
AXES = ("img", "cap")
F32 = jnp.float32
BF16 = jnp.bfloat16


def gelu_parts(preact):
    normal_cdf = 0.5 * (1.0 + jax.scipy.special.erf(preact * 0.7071067811865476))
    normal_pdf = jnp.exp(-0.5 * preact * preact) * 0.3989422804014327
    return (preact * normal_cdf, normal_cdf + preact * normal_pdf)


def tiles_kernel(seed_ref, place_ref, count_ref, *refs, tiles, slots):
    outs, (pat_ref, pat_t_ref, nimg_ref, ncap_ref, deg_ref, sems) = refs[:4], refs[4:]
    all_tiles, mid = 7 * tiles, 5 * tiles
    deg_ref[...] = jnp.zeros_like(deg_ref)
    row = lax.broadcasted_iota(jnp.int32, (TILE, TILE), 0)
    col = lax.broadcasted_iota(jnp.int32, (TILE, TILE), 1)
    first, second = jnp.int32(668265261), jnp.int32(374761393)
    base = (row * 40503 + col * 9973) * first
    base_t = (col * 40503 + row * 9973) * first
    off_diag = row - col

    def pattern(start, seed, live, s):
        mixed = start + seed * first
        mixed = jnp.bitwise_xor(mixed, jnp.right_shift(mixed, 15))
        mixed = mixed * second
        mixed = jnp.bitwise_xor(mixed, jnp.right_shift(mixed, 13))
        edge = jnp.bitwise_and(mixed, 15) == jnp.where(live, 0, 16)
        if s == 0:
            edge = edge | (off_diag == jnp.where(live, 0, TILE))
        return jnp.where(edge, 1.0, 0.0)

    def one(q, full):
        total = None
        for s in range(slots):
            live = s < count_ref[q]
            seed = seed_ref[q * slots + s]
            e = pattern(base, seed, live, s)
            c = place_ref[q * slots + s]
            deg_ref[c] += jnp.sum(e, axis=0, keepdims=True)
            if full:
                m = q - tiles
                pat_ref[m, :, pl.ds(s * TILE, TILE)] = e.astype(BF16)
                pat_t_ref[m, pl.ds(s * TILE, TILE), :] = pattern(base_t, seed, live, s).astype(BF16)
                total = e if total is None else total + e
        if full:
            d = jnp.sum(total, axis=1, keepdims=True)
            n = jnp.where(d > 0.0, lax.rsqrt(d), 0.0)
            nimg_ref[q - tiles] = jnp.broadcast_to(n, (TILE, TILE))

    def edge_body(q, c):
        one(q, False)
        return c

    def mid_body(q, c):
        one(q, True)
        return c

    lax.fori_loop(0, tiles, edge_body, 0)
    lax.fori_loop(tiles, tiles + mid, mid_body, 0)
    copies = [
        pltpu.make_async_copy(src, dst, sems.at[k])
        for k, (src, dst) in enumerate(zip((pat_ref, pat_t_ref, nimg_ref, ncap_ref), outs))
    ]
    for copy in copies[:3]:
        copy.start()
    lax.fori_loop(tiles + mid, all_tiles, edge_body, 0)
    for m in range(mid):
        d = deg_ref[m + 2 * tiles]
        n = jnp.where(d > 0.0, lax.rsqrt(d), 0.0)
        ncap_ref[m] = jnp.broadcast_to(n, (TILE, TILE)).T
    copies[3].start()
    for copy in copies:
        copy.wait()


def table_shapes(tiles, slots):
    mid = 5 * tiles
    return (
        ((mid, TILE, slots * TILE), BF16),
        ((mid, slots * TILE, TILE), BF16),
        ((mid, TILE, TILE), F32),
        ((mid, TILE, TILE), F32),
    )


def make_tiles(seeds, places, counts, tiles, slots):
    smem = pl.BlockSpec(memory_space=pltpu.SMEM)
    hbm = pl.BlockSpec(memory_space=pltpu.HBM)
    tables = table_shapes(tiles, slots)
    return pl.pallas_call(
        lambda *r: tiles_kernel(*r, tiles=tiles, slots=slots),
        out_shape=tuple(jax.ShapeDtypeStruct(*t) for t in tables),
        in_specs=[smem] * 3,
        out_specs=(hbm,) * 4,
        scratch_shapes=[pltpu.VMEM(*t) for t in tables]
        + [pltpu.VMEM((9 * tiles, 1, TILE), F32), pltpu.SemaphoreType.DMA((4,))],
        compiler_params=pltpu.CompilerParams(vmem_limit_bytes=16 << 20),
        cost_estimate=SHORT,
        name="tiles",
    )(seeds, places, counts)


def hops_kernel(
    place_ref, base_ref, own_hbm, low_hbm, high_hbm, mate_hbm, far_hbm, pat_hbm, pat_t_hbm, nimg_hbm, ncap_hbm,
    out_ref, bands, pat_ref, pat_t_ref, nimg_ref, ncap_ref, img0, cap0, img1, cap1, acc, acc2, keep_img, keep_cap,
    sems, *, tiles, slots, width,
):
    mid = 5 * tiles
    near = 3 * tiles
    keep = 1.0 - ALPHA
    sources = (own_hbm, nimg_hbm, ncap_hbm, low_hbm, high_hbm, mate_hbm, far_hbm, pat_t_hbm, pat_hbm)
    targets = (bands.at[0], nimg_ref, ncap_ref) + tuple(bands.at[k] for k in range(1, 5)) + (pat_t_ref, pat_ref)
    copies = [pltpu.make_async_copy(s, t, sems.at[k]) for k, (s, t) in enumerate(zip(sources, targets))]
    for copy in copies:
        copy.start()

    def wide(n_ref, m):
        n = n_ref[m]
        return jnp.concatenate([n] * (width // TILE), axis=1)

    def scale(k, base):
        for t in range(tiles):
            m = base + t
            img0[m] = (bands[k, pl.ds(t * TILE, TILE), :].astype(F32) * wide(nimg_ref, m)).astype(BF16)
            cap0[m] = (bands[k, pl.ds((tiles + t) * TILE, TILE), :].astype(F32) * wide(ncap_ref, m)).astype(BF16)

    acc[...] = jnp.zeros_like(acc)
    acc2[...] = jnp.zeros_like(acc2)
    for copy in copies[:3]:
        copy.wait()
    for k, base in enumerate((2 * tiles, 0, 4 * tiles, base_ref[0], base_ref[1])):
        if k:
            copies[2 + k].wait()
        scale(k, base)
    for copy in copies[7:]:
        copy.wait()

    def push(q, state, target, lo, count):
        r = jnp.dot(pat_t_ref[q], state, preferred_element_type=F32)
        for s in range(slots):
            c = place_ref[q * slots + s] - lo
            c = jnp.where((c >= 0) & (c < count), c, count)
            target[c] += r[s * TILE : (s + 1) * TILE]

    def pull(q, source, lo):
        total = None
        for s in range(slots):
            c = place_ref[q * slots + s] - lo
            r = jnp.dot(pat_ref[q, :, pl.ds(s * TILE, TILE)], source[c], preferred_element_type=F32)
            total = r if total is None else total + r
        return total

    def push1(q, c):
        push(q, img0[q], acc, tiles, near)
        return c

    lax.fori_loop(0, mid, push1, 0, unroll=3)

    def pull1(q, c):
        n = wide(nimg_ref, q)
        flow = keep * n * pull(q, cap0, 0)
        img1[q - tiles] = (flow * n).astype(BF16)
        keep_img[q - tiles] = flow
        return c

    lax.fori_loop(tiles, tiles + near, pull1, 0, unroll=3)

    def finish1(m, c):
        n = wide(ncap_ref, m + tiles)
        flow = keep * n * acc[m]
        cap1[m] = (flow * n).astype(BF16)
        keep_cap[m] = flow
        return c

    lax.fori_loop(0, near, finish1, 0, unroll=3)

    def push2(q, c):
        push(q, img1[q - tiles], acc2, 2 * tiles, tiles)
        return c

    lax.fori_loop(tiles, tiles + near, push2, 0, unroll=3)
    for t in range(tiles):
        q = 2 * tiles + t
        rows = pl.ds(t * TILE, TILE)
        flow = keep * wide(nimg_ref, q) * pull(q, cap1, tiles)
        out_ref[rows, :] = (ALPHA * (bands[0, rows, :].astype(F32) + keep_img[tiles + t]) + flow).astype(BF16)
        flow = keep * wide(ncap_ref, q) * acc2[t]
        rows = pl.ds((tiles + t) * TILE, TILE)
        out_ref[rows, :] = (ALPHA * (bands[0, rows, :].astype(F32) + keep_cap[tiles + t]) + flow).astype(BF16)


def propagate(places, bases, own, low, high, mate, far, tables, tiles, slots):
    width = own.shape[1]
    smem = pl.BlockSpec(memory_space=pltpu.SMEM)
    vmem = pl.BlockSpec(memory_space=pltpu.VMEM)
    hbm = pl.BlockSpec(memory_space=pltpu.HBM)
    mid, near = 5 * tiles, 3 * tiles
    return pl.pallas_call(
        lambda *r: hops_kernel(*r, tiles=tiles, slots=slots, width=width),
        out_shape=jax.ShapeDtypeStruct(own.shape, BF16),
        in_specs=[smem] * 2 + [hbm] * 9,
        out_specs=vmem,
        scratch_shapes=[
            pltpu.VMEM((5,) + own.shape, BF16),
            *[pltpu.VMEM(*t) for t in table_shapes(tiles, slots)],
            pltpu.VMEM((mid, TILE, width), BF16),
            pltpu.VMEM((mid, TILE, width), BF16),
            pltpu.VMEM((near, TILE, width), BF16),
            pltpu.VMEM((near, TILE, width), BF16),
            pltpu.VMEM((near + 1, TILE, width), F32),
            pltpu.VMEM((tiles + 1, TILE, width), F32),
            pltpu.VMEM((near, TILE, width), F32),
            pltpu.VMEM((near, TILE, width), F32),
            pltpu.SemaphoreType.DMA((9,)),
        ],
        compiler_params=pltpu.CompilerParams(vmem_limit_bytes=34 << 20),
        cost_estimate=SHORT,
        name="hops",
    )(places, bases, own, low, high, mate, far, *tables)


BLOCK = 64
GROUP = 4


def grouped(width):
    return [
        pl.BlockSpec((BLOCK, width), lambda i, order, k=k: (order[i * GROUP + k], 0)) for k in range(GROUP)
    ]


def stacked(refs):
    return jnp.concatenate([r[...] for r in refs], axis=0)


def whole(shape):
    return pl.BlockSpec(shape, lambda i, order: (0,) * len(shape))


def out_kernel(order_ref, *refs):
    act, (logit_ref, part_ref) = refs[:GROUP], refs[GROUP:]
    part_ref[...] = jnp.dot(stacked(act), logit_ref[...], preferred_element_type=F32).astype(BF16)


def in_kernel(order_ref, *refs):
    slope, w_out = refs[:GROUP], refs[GROUP : 2 * GROUP]
    logit_ref, feats_ref, part_ref, grad_ref = refs[2 * GROUP :]
    hidden = lax.dot_general(
        stacked(w_out), logit_ref[...], (((1,), (1,)), ((), ())), preferred_element_type=F32
    )
    grad = (hidden * stacked(slope)).astype(BF16)
    grad_ref[...] = grad
    f_in = feats_ref.shape[1]
    part_ref[:, :f_in] = jnp.dot(grad, feats_ref[...], preferred_element_type=F32).astype(BF16)
    bias = jnp.sum(grad.astype(F32), axis=1, keepdims=True)
    part_ref[:, f_in:] = jnp.broadcast_to(bias, (bias.shape[0], TILE)).astype(BF16)


def feat_kernel(order_ref, *refs):
    w_in = refs[:GROUP]
    kept_ref, sent_ref, img_ref, cap_ref, acc_ref = refs[GROUP:]
    i = pl.program_id(0)
    steps = pl.num_programs(0)

    @pl.when(i == 0)
    def _():
        acc_ref[...] = jnp.zeros_like(acc_ref)

    grad = jnp.where(i < steps // 2, kept_ref[...], sent_ref[...])
    acc_ref[...] += lax.dot_general(
        grad, stacked(w_in), (((0,), (0,)), ((), ())), preferred_element_type=F32
    )

    @pl.when(i == steps - 1)
    def _():
        half = img_ref.shape[0]
        img_ref[...] = acc_ref[:half].astype(BF16)
        cap_ref[...] = acc_ref[half:].astype(BF16)


def over_hidden(kernel, name, order, in_specs, out_specs, out_shape, scratch, args):
    return pl.pallas_call(
        kernel,
        out_shape=out_shape,
        grid_spec=pltpu.PrefetchScalarGridSpec(
            num_scalar_prefetch=1,
            grid=(order.shape[0] // GROUP,),
            in_specs=in_specs,
            out_specs=out_specs,
            scratch_shapes=scratch,
        ),
        compiler_params=pltpu.CompilerParams(
            dimension_semantics=("arbitrary",), vmem_limit_bytes=28 << 20
        ),
        cost_estimate=SHORT,
        name=name,
    )(order, *args)


def rows_of_half(width, half, side):
    steps = half // GROUP
    if side:
        return pl.BlockSpec((GROUP * BLOCK, width), lambda i, order: (jnp.maximum(i - steps, 0), 0))
    return pl.BlockSpec((GROUP * BLOCK, width), lambda i, order: (jnp.minimum(i, steps - 1), 0))


def rows_of(width):
    return pl.BlockSpec((GROUP * BLOCK, width), lambda i, order: (i, 0))


def stack_kernel(top_ref, bottom_ref, out_ref):
    half = top_ref.shape[0]
    out_ref[:half] = top_ref[...]
    out_ref[half:] = bottom_ref[...]


def stack(top, bottom):
    vmem = pl.BlockSpec(memory_space=pltpu.VMEM)
    return pl.pallas_call(
        stack_kernel,
        out_shape=jax.ShapeDtypeStruct((2 * top.shape[0], top.shape[1]), top.dtype),
        in_specs=[vmem] * 2,
        out_specs=vmem,
        cost_estimate=SHORT,
        name="stack",
    )(top, bottom)


def after(value, *done):
    return lax.optimization_barrier((value,) + done)[0]


def moved(array, count, by):
    return lax.ppermute(array, AXES, [(i, i + by) for i in range(count) if 0 <= i + by < count])


def flipped(array, count, mask):
    return lax.ppermute(array, AXES, [(i, i ^ mask) for i in range(count)])


def added(kept, came):
    return (kept.astype(F32) + came.astype(F32)).astype(BF16)


def parts(array, axis):
    return lax.index_in_dim(array, 0, axis, keepdims=False), lax.index_in_dim(array, 1, axis, keepdims=False)


def nearest_pair(count, by):
    return [(i, i + by) for i in range(0, count - by, 2)] + [(i, i - by) for i in range(by + 1, count, 2)]


class Reduction:

    def __init__(self, part, count, bits, order):
        self.part, self.count, self.left, self.order = part, count, list(bits), list(order)

    def start(self):
        bit = self.order.pop(0)
        self.kept, self.sent = parts(self.part, self.left.index(bit))
        self.left.remove(bit)
        self.came = flipped(self.sent, self.count, 1 << bit)

    def finish(self, *done):
        self.part = added(after(self.kept, *done), self.came)
        return self.part

    def start_last(self):
        part = self.part.reshape((4,) + self.part.shape[-2:])
        hi, lo = self.left
        self.own = part[0]
        self.got = [flipped(part[k], self.count, ((k >> 1) << hi) | ((k & 1) << lo)) for k in range(1, 4)]

    def result(self):
        total = self.own.astype(F32)
        for piece in self.got:
            total = total + piece.astype(F32)
        return total


def per_device(
    feats_img, feats_cap, cot_img, cot_cap, w_in, b_in, w_out, tile_seed, tile_cols, tile_count
):
    local_rows = feats_img.shape[0]
    tiles = local_rows // TILE
    slots = tile_seed.shape[1]
    hid, f_in = w_in.shape
    n_img, n_cap = lax.axis_size("img"), lax.axis_size("cap")
    count = n_img * n_cap
    me = lax.axis_index(AXES)

    even = (me & 1) == 0
    meta = jnp.concatenate([tile_seed, tile_cols, tile_count[:, None]], axis=1)
    other = flipped(meta, count, 1)
    block = stack(cot_img, cot_cap)
    mate = flipped(block, count, 1)
    low = moved(block, count, 2)
    high = moved(block, count, -2)
    far = lax.ppermute(mate, AXES, nearest_pair(count, 2))
    pair = jnp.where(even, jnp.concatenate([meta, other]), jnp.concatenate([other, meta]))
    pair_low = moved(pair, count, 2)
    pair_high = moved(pair, count, -2)
    pair_far = lax.ppermute(pair, AXES, nearest_pair(count, 4))
    wide = jnp.where(
        even,
        jnp.concatenate([pair_far[tiles:], pair_low, pair, pair_high]),
        jnp.concatenate([pair_low, pair, pair_high, pair_far[:tiles]]),
    )
    frame = jnp.arange(7 * tiles, dtype=jnp.int32)[:, None]
    counts = wide[:, 2 * slots]
    seeds = wide[:, :slots].reshape(-1)
    places = jnp.where(counts[:, None] > 0, wide[:, slots : 2 * slots] - (me - 3) * tiles, frame)
    pats = make_tiles(seeds, (places + tiles).reshape(-1), counts, tiles, slots)

    m = count.bit_length() - 1
    a = n_cap.bit_length() - 1
    cap_bits = list(range(a))
    img_bits = list(range(a + 1, m - 2))
    bits = [a] + cap_bits + img_bits + [m - 1, m - 2]
    pos = jnp.arange(count, dtype=jnp.int32)
    order = jnp.zeros_like(pos)
    for k, bit in enumerate(bits):
        order = order | (((pos >> (m - 1 - k)) & 1) << bit)
    order = order ^ me
    rows = hid // count
    if rows % BLOCK:
        w_in, w_out, b_in = [
            jnp.take(v.reshape((count, rows) + v.shape[1:]), order, axis=0).reshape(v.shape) for v in (w_in, w_out, b_in)
        ]
        order = jnp.arange(hid // BLOCK, dtype=jnp.int32)
    else:
        order = (order[:, None] * (rows // BLOCK) + jnp.arange(rows // BLOCK, dtype=jnp.int32)).reshape(-1)

    feats = after(jnp.concatenate([feats_img, feats_cap], axis=0), pair)
    across = (((1,), (1,)), ((), ()))
    preact = lax.dot_general(w_in, feats, across, preferred_element_type=F32) + b_in[:, None]
    gelu_value, gelu_slope = gelu_parts(preact)
    hidden_act, gelu_slope = lax.optimization_barrier((gelu_value.astype(BF16), gelu_slope))

    bases = jnp.where(even, jnp.array([3, 1]), jnp.array([1, 3])).astype(jnp.int32) * tiles
    mid_places = (places - tiles)[tiles : 6 * tiles].reshape(-1)
    logit = propagate(mid_places, bases, block, low, high, mate, far, pats, tiles, slots)

    width = cot_img.shape[1]
    nodes = 2 * local_rows
    half = order.shape[0] // 2
    blocked = (2,) * (m - 1) + (rows,)

    def out_half(order, logit):
        return over_hidden(
            out_kernel, "part_out", order, grouped(nodes) + [whole(logit.shape)], rows_of(width),
            jax.ShapeDtypeStruct((hid // 2, width), BF16), [], [hidden_act] * GROUP + [logit],
        ).reshape(blocked + (width,))

    def in_half(order, logit):
        part, grad = over_hidden(
            in_kernel, "part_in", order,
            grouped(nodes) + grouped(width) + [whole(logit.shape), whole(feats.shape)],
            (rows_of(f_in + TILE), rows_of(nodes)),
            (jax.ShapeDtypeStruct((hid // 2, f_in + TILE), BF16), jax.ShapeDtypeStruct((hid // 2, nodes), BF16)),
            [], [gelu_slope] * GROUP + [w_out] * GROUP + [logit, feats],
        )
        return part.reshape(blocked + (f_in + TILE,)), grad

    core = 1 << a
    rest = bits[1:]
    out_sent = out_half(order[half:], logit)
    out_came = flipped(out_sent, count, core)
    out_kept = out_half(order[:half], after(logit, out_sent))
    r_out = Reduction(added(out_kept, out_came), count, rest, img_bits + cap_bits)
    r_out.start()
    in_sent, grad_sent = in_half(order[half:], after(logit, r_out.part))
    in_came = flipped(in_sent, count, core)
    in_kept, grad_kept = in_half(order[:half], after(logit, grad_sent))
    g_in = added(in_kept, in_came)
    cut = f_in // 2
    r_a = Reduction(g_in[..., :cut], count, rest, img_bits + cap_bits)
    r_b = Reduction(g_in[..., cut:], count, rest, cap_bits + img_bits)
    r_a.start()
    r_b.start()
    grad_kept = after(grad_kept, g_in)
    grad_img, grad_cap = over_hidden(
        feat_kernel, "feat_grad", order, grouped(f_in) + [rows_of_half(nodes, half, 0), rows_of_half(nodes, half, 1)],
        (whole((local_rows, f_in)),) * 2, (jax.ShapeDtypeStruct((local_rows, f_in), BF16),) * 2,
        [pltpu.VMEM((nodes, f_in), F32)], [w_in] * GROUP + [grad_kept, grad_sent],
    )
    done = (r_a.sent, r_b.sent)
    for k in range(m - 3):
        for r in (r_out, r_b, r_a):
            done = (r.finish(*done),)
            if k < m - 4:
                r.start()
            else:
                r.start_last()
    grad_scale = 1.0 / math.sqrt(nodes * count)
    g_out, g_b, g_a = [r.result() * grad_scale for r in (r_out, r_b, r_a)]
    g_in = jnp.concatenate([g_a, g_b[:, : f_in - cut]], axis=1)
    return (grad_img, grad_cap, g_in, g_out, g_b[:, f_in - cut])


def solution(mesh):
    rows = P(("img", "cap"), None)
    in_specs = (rows, rows, rows, rows, P(), P(), P(), rows, rows, P(("img", "cap")))
    out_specs = (rows, rows, rows, rows, P(("img", "cap")))
    return jax.shard_map(
        per_device, mesh=mesh, in_specs=in_specs, out_specs=out_specs, check_vma=False
    )
```

```python
import math

import jax
import jax.numpy as jnp
from jax import lax
from jax.experimental import pallas as pl
from jax.experimental.pallas import tpu as pltpu
from jax.sharding import PartitionSpec as P

TILE = 128
ALPHA = 0.1
SHORT = pl.CostEstimate(flops=1, transcendentals=0, bytes_accessed=1)
AXES = ("img", "cap")
F32 = jnp.float32
BF16 = jnp.bfloat16


def gelu_parts(preact):
    normal_cdf = 0.5 * (1.0 + jax.scipy.special.erf(preact * 0.7071067811865476))
    normal_pdf = jnp.exp(-0.5 * preact * preact) * 0.3989422804014327
    return (preact * normal_cdf, normal_cdf + preact * normal_pdf)


def tiles_kernel(seed_ref, place_ref, count_ref, *refs, tiles, slots):
    outs, (pat_ref, pat_t_ref, nimg_ref, ncap_ref, deg_ref, sems) = refs[:4], refs[4:]
    all_tiles, mid = 7 * tiles, 5 * tiles
    deg_ref[...] = jnp.zeros_like(deg_ref)
    row = lax.broadcasted_iota(jnp.int32, (TILE, TILE), 0)
    col = lax.broadcasted_iota(jnp.int32, (TILE, TILE), 1)
    first, second = jnp.int32(668265261), jnp.int32(374761393)
    base = (row * 40503 + col * 9973) * first
    base_t = (col * 40503 + row * 9973) * first
    off_diag = row - col

    def pattern(start, seed, live, s):
        mixed = start + seed * first
        mixed = jnp.bitwise_xor(mixed, jnp.right_shift(mixed, 15))
        mixed = mixed * second
        mixed = jnp.bitwise_xor(mixed, jnp.right_shift(mixed, 13))
        edge = jnp.bitwise_and(mixed, 15) == jnp.where(live, 0, 16)
        if s == 0:
            edge = edge | (off_diag == jnp.where(live, 0, TILE))
        return jnp.where(edge, 1.0, 0.0)

    def one(q, full):
        total = None
        for s in range(slots):
            live = s < count_ref[q]
            seed = seed_ref[q * slots + s]
            e = pattern(base, seed, live, s)
            c = place_ref[q * slots + s]
            deg_ref[c] += jnp.sum(e, axis=0, keepdims=True)
            if full:
                m = q - tiles
                pat_ref[m, :, pl.ds(s * TILE, TILE)] = e.astype(BF16)
                pat_t_ref[m, pl.ds(s * TILE, TILE), :] = pattern(base_t, seed, live, s).astype(BF16)
                total = e if total is None else total + e
        if full:
            d = jnp.sum(total, axis=1, keepdims=True)
            n = jnp.where(d > 0.0, lax.rsqrt(d), 0.0)
            nimg_ref[q - tiles] = jnp.broadcast_to(n, (TILE, TILE))

    def edge_body(q, c):
        one(q, False)
        return c

    def mid_body(q, c):
        one(q, True)
        return c

    lax.fori_loop(0, tiles, edge_body, 0)
    lax.fori_loop(tiles, tiles + mid, mid_body, 0)
    copies = [
        pltpu.make_async_copy(src, dst, sems.at[k])
        for k, (src, dst) in enumerate(zip((pat_ref, pat_t_ref, nimg_ref, ncap_ref), outs))
    ]
    for copy in copies[:3]:
        copy.start()
    lax.fori_loop(tiles + mid, all_tiles, edge_body, 0)
    for m in range(mid):
        d = deg_ref[m + 2 * tiles]
        n = jnp.where(d > 0.0, lax.rsqrt(d), 0.0)
        ncap_ref[m] = jnp.broadcast_to(n, (TILE, TILE)).T
    copies[3].start()
    for copy in copies:
        copy.wait()


def table_shapes(tiles, slots):
    mid = 5 * tiles
    return (
        ((mid, TILE, slots * TILE), BF16),
        ((mid, slots * TILE, TILE), BF16),
        ((mid, TILE, TILE), F32),
        ((mid, TILE, TILE), F32),
    )


def make_tiles(seeds, places, counts, tiles, slots):
    smem = pl.BlockSpec(memory_space=pltpu.SMEM)
    hbm = pl.BlockSpec(memory_space=pltpu.HBM)
    tables = table_shapes(tiles, slots)
    return pl.pallas_call(
        lambda *r: tiles_kernel(*r, tiles=tiles, slots=slots),
        out_shape=tuple(pltpu.HBM(*t) for t in tables),
        in_specs=[smem] * 3,
        out_specs=(hbm,) * 4,
        scratch_shapes=[pltpu.VMEM(*t) for t in tables]
        + [pltpu.VMEM((9 * tiles, 1, TILE), F32), pltpu.SemaphoreType.DMA((4,))],
        compiler_params=pltpu.CompilerParams(vmem_limit_bytes=16 << 20),
        cost_estimate=SHORT,
        name="tiles",
    )(seeds, places, counts)


def hops_kernel(
    place_ref, base_ref, own_hbm, low_hbm, high_hbm, mate_hbm, far_hbm, pat_hbm, pat_t_hbm, nimg_hbm, ncap_hbm,
    out_ref, bands, pat_ref, pat_t_ref, nimg_ref, ncap_ref, img0, cap0, img1, cap1, acc, acc2, keep_img, keep_cap,
    sems, *, tiles, slots, width,
):
    mid = 5 * tiles
    near = 3 * tiles
    keep = 1.0 - ALPHA
    sources = (own_hbm, nimg_hbm, ncap_hbm, low_hbm, high_hbm, mate_hbm, far_hbm, pat_t_hbm, pat_hbm)
    targets = (bands.at[0], nimg_ref, ncap_ref) + tuple(bands.at[k] for k in range(1, 5)) + (pat_t_ref, pat_ref)
    copies = [pltpu.make_async_copy(s, t, sems.at[k]) for k, (s, t) in enumerate(zip(sources, targets))]
    for copy in copies:
        copy.start()

    def wide(n_ref, m):
        n = n_ref[m]
        return jnp.concatenate([n] * (width // TILE), axis=1)

    def scale(k, base):
        for t in range(tiles):
            m = base + t
            img0[m] = (bands[k, pl.ds(t * TILE, TILE), :].astype(F32) * wide(nimg_ref, m)).astype(BF16)
            cap0[m] = (bands[k, pl.ds((tiles + t) * TILE, TILE), :].astype(F32) * wide(ncap_ref, m)).astype(BF16)

    acc[...] = jnp.zeros_like(acc)
    acc2[...] = jnp.zeros_like(acc2)
    for copy in copies[:3]:
        copy.wait()
    for k, base in enumerate((2 * tiles, 0, 4 * tiles, base_ref[0], base_ref[1])):
        if k:
            copies[2 + k].wait()
        scale(k, base)
    for copy in copies[7:]:
        copy.wait()

    def push(q, state, target, lo, count):
        r = jnp.dot(pat_t_ref[q], state, preferred_element_type=F32)
        for s in range(slots):
            c = place_ref[q * slots + s] - lo
            c = jnp.where((c >= 0) & (c < count), c, count)
            target[c] += r[s * TILE : (s + 1) * TILE]

    def pull(q, source, lo):
        total = None
        for s in range(slots):
            c = place_ref[q * slots + s] - lo
            r = jnp.dot(pat_ref[q, :, pl.ds(s * TILE, TILE)], source[c], preferred_element_type=F32)
            total = r if total is None else total + r
        return total

    def push1(q, c):
        push(q, img0[q], acc, tiles, near)
        return c

    lax.fori_loop(0, mid, push1, 0, unroll=3)

    def pull1(q, c):
        n = wide(nimg_ref, q)
        flow = keep * n * pull(q, cap0, 0)
        img1[q - tiles] = (flow * n).astype(BF16)
        keep_img[q - tiles] = flow
        return c

    lax.fori_loop(tiles, tiles + near, pull1, 0, unroll=3)

    def finish1(m, c):
        n = wide(ncap_ref, m + tiles)
        flow = keep * n * acc[m]
        cap1[m] = (flow * n).astype(BF16)
        keep_cap[m] = flow
        return c

    lax.fori_loop(0, near, finish1, 0, unroll=3)

    def push2(q, c):
        push(q, img1[q - tiles], acc2, 2 * tiles, tiles)
        return c

    lax.fori_loop(tiles, tiles + near, push2, 0, unroll=3)
    for t in range(tiles):
        q = 2 * tiles + t
        rows = pl.ds(t * TILE, TILE)
        flow = keep * wide(nimg_ref, q) * pull(q, cap1, tiles)
        out_ref[rows, :] = (ALPHA * (bands[0, rows, :].astype(F32) + keep_img[tiles + t]) + flow).astype(BF16)
        flow = keep * wide(ncap_ref, q) * acc2[t]
        rows = pl.ds((tiles + t) * TILE, TILE)
        out_ref[rows, :] = (ALPHA * (bands[0, rows, :].astype(F32) + keep_cap[tiles + t]) + flow).astype(BF16)


def propagate(places, bases, own, low, high, mate, far, tables, tiles, slots):
    width = own.shape[1]
    smem = pl.BlockSpec(memory_space=pltpu.SMEM)
    vmem = pl.BlockSpec(memory_space=pltpu.VMEM)
    hbm = pl.BlockSpec(memory_space=pltpu.HBM)
    mid, near = 5 * tiles, 3 * tiles
    return pl.pallas_call(
        lambda *r: hops_kernel(*r, tiles=tiles, slots=slots, width=width),
        out_shape=jax.ShapeDtypeStruct(own.shape, BF16),
        in_specs=[smem] * 2 + [hbm] * 9,
        out_specs=vmem,
        scratch_shapes=[
            pltpu.VMEM((5,) + own.shape, BF16),
            *[pltpu.VMEM(*t) for t in table_shapes(tiles, slots)],
            pltpu.VMEM((mid, TILE, width), BF16),
            pltpu.VMEM((mid, TILE, width), BF16),
            pltpu.VMEM((near, TILE, width), BF16),
            pltpu.VMEM((near, TILE, width), BF16),
            pltpu.VMEM((near + 1, TILE, width), F32),
            pltpu.VMEM((tiles + 1, TILE, width), F32),
            pltpu.VMEM((near, TILE, width), F32),
            pltpu.VMEM((near, TILE, width), F32),
            pltpu.SemaphoreType.DMA((9,)),
        ],
        compiler_params=pltpu.CompilerParams(vmem_limit_bytes=34 << 20),
        cost_estimate=SHORT,
        name="hops",
    )(places, bases, *[pltpu.with_memory_space_constraint(v, pltpu.HBM) for v in (own, low, high, mate, far, *tables)])


BLOCK = 64
GROUP = 4


def grouped(width):
    return [
        pl.BlockSpec((BLOCK, width), lambda i, order, k=k: (order[i * GROUP + k], 0)) for k in range(GROUP)
    ]


def stacked(refs):
    return jnp.concatenate([r[...] for r in refs], axis=0)


def whole(shape):
    return pl.BlockSpec(shape, lambda i, order: (0,) * len(shape))


def out_kernel(order_ref, *refs):
    act, (logit_ref, part_ref) = refs[:GROUP], refs[GROUP:]
    part_ref[...] = jnp.dot(stacked(act), logit_ref[...], preferred_element_type=F32).astype(BF16)


def in_kernel(order_ref, *refs):
    slope, w_out = refs[:GROUP], refs[GROUP : 2 * GROUP]
    logit_ref, feats_ref, part_ref, grad_ref = refs[2 * GROUP :]
    hidden = lax.dot_general(
        stacked(w_out), logit_ref[...], (((1,), (1,)), ((), ())), preferred_element_type=F32
    )
    grad = (hidden * stacked(slope)).astype(BF16)
    grad_ref[...] = grad
    f_in = feats_ref.shape[1]
    part_ref[:, :f_in] = jnp.dot(grad, feats_ref[...], preferred_element_type=F32).astype(BF16)
    bias = jnp.sum(grad.astype(F32), axis=1, keepdims=True)
    part_ref[:, f_in:] = jnp.broadcast_to(bias, (bias.shape[0], TILE)).astype(BF16)


def feat_kernel(order_ref, *refs):
    w_in = refs[:GROUP]
    kept_ref, sent_ref, img_ref, cap_ref, acc_ref = refs[GROUP:]
    i = pl.program_id(0)
    steps = pl.num_programs(0)

    @pl.when(i == 0)
    def _():
        acc_ref[...] = jnp.zeros_like(acc_ref)

    grad = jnp.where(i < steps // 2, kept_ref[...], sent_ref[...])
    acc_ref[...] += lax.dot_general(
        grad, stacked(w_in), (((0,), (0,)), ((), ())), preferred_element_type=F32
    )

    @pl.when(i == steps - 1)
    def _():
        half = img_ref.shape[0]
        img_ref[...] = acc_ref[:half].astype(BF16)
        cap_ref[...] = acc_ref[half:].astype(BF16)


def over_hidden(kernel, name, order, in_specs, out_specs, out_shape, scratch, args):
    return pl.pallas_call(
        kernel,
        out_shape=out_shape,
        grid_spec=pltpu.PrefetchScalarGridSpec(
            num_scalar_prefetch=1,
            grid=(order.shape[0] // GROUP,),
            in_specs=in_specs,
            out_specs=out_specs,
            scratch_shapes=scratch,
        ),
        compiler_params=pltpu.CompilerParams(
            dimension_semantics=("arbitrary",), vmem_limit_bytes=28 << 20
        ),
        cost_estimate=SHORT,
        name=name,
    )(order, *args)


def rows_of_half(width, half, side):
    steps = half // GROUP
    if side:
        return pl.BlockSpec((GROUP * BLOCK, width), lambda i, order: (jnp.maximum(i - steps, 0), 0))
    return pl.BlockSpec((GROUP * BLOCK, width), lambda i, order: (jnp.minimum(i, steps - 1), 0))


def rows_of(width):
    return pl.BlockSpec((GROUP * BLOCK, width), lambda i, order: (i, 0))


def stack_kernel(count_ref, top_ref, bottom_ref, seed_ref, cols_ref, out_ref, meta_ref):
    half = top_ref.shape[0]
    out_ref[:half] = top_ref[...]
    out_ref[half:] = bottom_ref[...]
    tiles, slots = seed_ref.shape
    meta_ref[:, :slots] = seed_ref[...]
    meta_ref[:, slots : 2 * slots] = cols_ref[...]
    row = lax.broadcasted_iota(jnp.int32, (tiles, slots), 0)
    live = jnp.zeros((tiles, slots), jnp.int32)
    for t in range(tiles):
        live = jnp.where(row == t, count_ref[t], live)
    meta_ref[:, 2 * slots :] = live


def stack(top, bottom, seed, cols, counts):
    vmem = pl.BlockSpec(memory_space=pltpu.VMEM)
    shape = (2 * top.shape[0], top.shape[1])
    codes = (seed.shape[0], 3 * seed.shape[1])
    return pl.pallas_call(
        stack_kernel,
        out_shape=(pltpu.HBM(shape, top.dtype), jax.ShapeDtypeStruct(codes, jnp.int32)),
        in_specs=[pl.BlockSpec(memory_space=pltpu.SMEM)] + [vmem] * 4,
        out_specs=(pl.BlockSpec(shape, lambda: (0, 0)), pl.BlockSpec(codes, lambda: (0, 0))),
        cost_estimate=SHORT,
        name="stack",
    )(counts, top, bottom, seed, cols)


def after(value, *done):
    return lax.optimization_barrier((value,) + done)[0]


def moved(array, count, by):
    return lax.ppermute(array, AXES, [(i, i + by) for i in range(count) if 0 <= i + by < count])


def flipped(array, count, mask):
    return lax.ppermute(array, AXES, [(i, i ^ mask) for i in range(count)])


def added(kept, came):
    return (kept.astype(F32) + came.astype(F32)).astype(BF16)


def parts(array, axis):
    return lax.index_in_dim(array, 0, axis, keepdims=False), lax.index_in_dim(array, 1, axis, keepdims=False)


def nearest_pair(count, by):
    return [(i, i + by) for i in range(0, count - by, 2)] + [(i, i - by) for i in range(by + 1, count, 2)]


class Reduction:

    def __init__(self, part, count, bits, order):
        self.part, self.count, self.left, self.order = part, count, list(bits), list(order)

    def start(self):
        bit = self.order.pop(0)
        self.kept, self.sent = parts(self.part, self.left.index(bit))
        self.left.remove(bit)
        self.came = flipped(self.sent, self.count, 1 << bit)

    def finish(self, *done):
        self.part = added(after(self.kept, *done), self.came)
        return self.part

    def start_last(self):
        part = self.part.reshape((4,) + self.part.shape[-2:])
        hi, lo = self.left
        self.own = part[0]
        self.got = [flipped(part[k], self.count, ((k >> 1) << hi) | ((k & 1) << lo)) for k in range(1, 4)]

    def result(self):
        total = self.own.astype(F32)
        for piece in self.got:
            total = total + piece.astype(F32)
        return total


def per_device(
    feats_img, feats_cap, cot_img, cot_cap, w_in, b_in, w_out, tile_seed, tile_cols, tile_count
):
    local_rows = feats_img.shape[0]
    tiles = local_rows // TILE
    slots = tile_seed.shape[1]
    hid, f_in = w_in.shape
    n_img, n_cap = lax.axis_size("img"), lax.axis_size("cap")
    count = n_img * n_cap
    me = lax.axis_index(AXES)

    even = (me & 1) == 0
    block, meta = stack(cot_img, cot_cap, tile_seed, tile_cols, tile_count)
    other = flipped(meta, count, 1)
    block = after(block, other)
    mate = flipped(block, count, 1)
    low = moved(block, count, 2)
    high = moved(block, count, -2)
    far = lax.ppermute(mate, AXES, nearest_pair(count, 2))
    pair = jnp.where(even, jnp.concatenate([meta, other]), jnp.concatenate([other, meta]))
    feats = jnp.concatenate([feats_img, feats_cap], axis=0)
    pair, feats = lax.optimization_barrier((pair, after(feats, block)))
    pair_low = moved(pair, count, 2)
    pair_high = moved(pair, count, -2)
    pair_far = lax.ppermute(pair, AXES, nearest_pair(count, 4))
    wide = jnp.where(
        even,
        jnp.concatenate([pair_far[tiles:], pair_low, pair, pair_high]),
        jnp.concatenate([pair_low, pair, pair_high, pair_far[:tiles]]),
    )
    frame = jnp.arange(7 * tiles, dtype=jnp.int32)[:, None]
    counts = wide[:, 2 * slots]
    seeds = wide[:, :slots].reshape(-1)
    places = jnp.where(counts[:, None] > 0, wide[:, slots : 2 * slots] - (me - 3) * tiles, frame)
    pats = make_tiles(seeds, (places + tiles).reshape(-1), counts, tiles, slots)

    m = count.bit_length() - 1
    a = n_cap.bit_length() - 1
    cap_bits = list(range(a))
    img_bits = list(range(a + 1, m - 2))
    bits = [a] + cap_bits + img_bits + [m - 1, m - 2]
    pos = jnp.arange(count, dtype=jnp.int32)
    order = jnp.zeros_like(pos)
    for k, bit in enumerate(bits):
        order = order | (((pos >> (m - 1 - k)) & 1) << bit)
    order = order ^ me
    rows = hid // count
    if rows % BLOCK:
        w_in, w_out, b_in = [
            jnp.take(v.reshape((count, rows) + v.shape[1:]), order, axis=0).reshape(v.shape) for v in (w_in, w_out, b_in)
        ]
        order = jnp.arange(hid // BLOCK, dtype=jnp.int32)
    else:
        order = (order[:, None] * (rows // BLOCK) + jnp.arange(rows // BLOCK, dtype=jnp.int32)).reshape(-1)

    across = (((1,), (1,)), ((), ()))
    preact = lax.dot_general(w_in, feats, across, preferred_element_type=F32) + b_in[:, None]
    gelu_value, gelu_slope = gelu_parts(preact)
    hidden_act, gelu_slope = lax.optimization_barrier((gelu_value.astype(BF16), gelu_slope))

    bases = jnp.where(even, jnp.array([3, 1]), jnp.array([1, 3])).astype(jnp.int32) * tiles
    mid_places = (places - tiles)[tiles : 6 * tiles].reshape(-1)
    logit = propagate(mid_places, bases, block, low, high, mate, far, pats, tiles, slots)

    width = cot_img.shape[1]
    nodes = 2 * local_rows
    half = order.shape[0] // 2
    blocked = (2,) * (m - 1) + (rows,)

    def out_half(order, logit):
        return over_hidden(
            out_kernel, "part_out", order, grouped(nodes) + [whole(logit.shape)], rows_of(width),
            jax.ShapeDtypeStruct((hid // 2, width), BF16), [], [hidden_act] * GROUP + [logit],
        ).reshape(blocked + (width,))

    def in_half(order, logit):
        part, grad = over_hidden(
            in_kernel, "part_in", order,
            grouped(nodes) + grouped(width) + [whole(logit.shape), whole(feats.shape)],
            (rows_of(f_in + TILE), rows_of(nodes)),
            (jax.ShapeDtypeStruct((hid // 2, f_in + TILE), BF16), jax.ShapeDtypeStruct((hid // 2, nodes), BF16)),
            [], [gelu_slope] * GROUP + [w_out] * GROUP + [logit, feats],
        )
        return part.reshape(blocked + (f_in + TILE,)), grad

    core = 1 << a
    rest = bits[1:]
    out_sent = out_half(order[half:], logit)
    out_came = flipped(out_sent, count, core)
    out_kept = out_half(order[:half], after(logit, out_sent))
    r_out = Reduction(added(out_kept, out_came), count, rest, img_bits + cap_bits)
    r_out.start()
    in_sent, grad_sent = in_half(order[half:], after(logit, r_out.part))
    in_came = flipped(in_sent, count, core)
    in_kept, grad_kept = in_half(order[:half], after(logit, grad_sent))
    g_in = added(in_kept, in_came)
    cut = f_in // 2
    r_a = Reduction(g_in[..., :cut], count, rest, img_bits + cap_bits)
    r_b = Reduction(g_in[..., cut:], count, rest, cap_bits + img_bits)
    r_a.start()
    r_b.start()
    grad_kept = after(grad_kept, g_in)
    grad_img, grad_cap = over_hidden(
        feat_kernel, "feat_grad", order, grouped(f_in) + [rows_of_half(nodes, half, 0), rows_of_half(nodes, half, 1)],
        (whole((local_rows, f_in)),) * 2, (jax.ShapeDtypeStruct((local_rows, f_in), BF16),) * 2,
        [pltpu.VMEM((nodes, f_in), F32)], [w_in] * GROUP + [grad_kept, grad_sent],
    )
    done = (r_a.sent, r_b.sent)
    for k in range(m - 3):
        for r in (r_out, r_b, r_a):
            done = (r.finish(*done),)
            if k < m - 4:
                r.start()
            else:
                r.start_last()
    grad_scale = 1.0 / math.sqrt(nodes * count)
    g_out, g_b, g_a = [r.result() * grad_scale for r in (r_out, r_b, r_a)]
    g_in = jnp.concatenate([g_a, g_b[:, : f_in - cut]], axis=1)
    return (grad_img, grad_cap, g_in, g_out, g_b[:, f_in - cut])


def solution(mesh):
    rows = P(("img", "cap"), None)
    in_specs = (rows, rows, rows, rows, P(), P(), P(), rows, rows, P(("img", "cap")))
    out_specs = (rows, rows, rows, rows, P(("img", "cap")))
    return jax.shard_map(
        per_device, mesh=mesh, in_specs=in_specs, out_specs=out_specs, check_vma=False
    )
```

```python
import math

import jax
import jax.numpy as jnp
from jax import lax
from jax.experimental import pallas as pl
from jax.experimental.pallas import tpu as pltpu
from jax.sharding import PartitionSpec as P

TILE = 128
ALPHA = 0.1
SHORT = pl.CostEstimate(flops=1, transcendentals=0, bytes_accessed=1)
AXES = ("img", "cap")
F32 = jnp.float32
BF16 = jnp.bfloat16


def gelu_parts(preact):
    normal_cdf = 0.5 * (1.0 + jax.scipy.special.erf(preact * 0.7071067811865476))
    normal_pdf = jnp.exp(-0.5 * preact * preact) * 0.3989422804014327
    return (preact * normal_cdf, normal_cdf + preact * normal_pdf)


def tiles_kernel(seed_ref, place_ref, count_ref, *refs, tiles, slots):
    outs, (pat_ref, pat_t_ref, nimg_ref, ncap_ref, deg_ref, sems) = refs[:4], refs[4:]
    all_tiles, mid = 7 * tiles, 5 * tiles
    deg_ref[...] = jnp.zeros_like(deg_ref)
    row = lax.broadcasted_iota(jnp.int32, (TILE, TILE), 0)
    col = lax.broadcasted_iota(jnp.int32, (TILE, TILE), 1)
    first, second = jnp.int32(668265261), jnp.int32(374761393)
    base = (row * 40503 + col * 9973) * first
    base_t = (col * 40503 + row * 9973) * first
    off_diag = row - col

    def pattern(start, seed, live, s):
        mixed = start + seed * first
        mixed = jnp.bitwise_xor(mixed, jnp.right_shift(mixed, 15))
        mixed = mixed * second
        mixed = jnp.bitwise_xor(mixed, jnp.right_shift(mixed, 13))
        edge = jnp.bitwise_and(mixed, 15) == jnp.where(live, 0, 16)
        if s == 0:
            edge = edge | (off_diag == jnp.where(live, 0, TILE))
        return jnp.where(edge, 1.0, 0.0)

    def one(q, full):
        total = None
        for s in range(slots):
            live = s < count_ref[q]
            seed = seed_ref[q * slots + s]
            e = pattern(base, seed, live, s)
            c = place_ref[q * slots + s]
            deg_ref[c] += jnp.sum(e, axis=0, keepdims=True)
            if full:
                m = q - tiles
                pat_ref[m, :, pl.ds(s * TILE, TILE)] = e.astype(BF16)
                pat_t_ref[m, pl.ds(s * TILE, TILE), :] = pattern(base_t, seed, live, s).astype(BF16)
                total = e if total is None else total + e
        if full:
            d = jnp.sum(total, axis=1, keepdims=True)
            n = jnp.where(d > 0.0, lax.rsqrt(d), 0.0)
            nimg_ref[q - tiles] = jnp.broadcast_to(n, (TILE, TILE))

    def edge_body(q, c):
        one(q, False)
        return c

    def mid_body(q, c):
        one(q, True)
        return c

    lax.fori_loop(0, tiles, edge_body, 0)
    lax.fori_loop(tiles, tiles + mid, mid_body, 0)
    copies = [
        pltpu.make_async_copy(src, dst, sems.at[k])
        for k, (src, dst) in enumerate(zip((pat_ref, pat_t_ref, nimg_ref, ncap_ref), outs))
    ]
    for copy in copies[:3]:
        copy.start()
    lax.fori_loop(tiles + mid, all_tiles, edge_body, 0)
    for m in range(mid):
        d = deg_ref[m + 2 * tiles]
        n = jnp.where(d > 0.0, lax.rsqrt(d), 0.0)
        ncap_ref[m] = jnp.broadcast_to(n, (TILE, TILE)).T
    copies[3].start()
    for copy in copies:
        copy.wait()


def table_shapes(tiles, slots):
    mid = 5 * tiles
    return (
        ((mid, TILE, slots * TILE), BF16),
        ((mid, slots * TILE, TILE), BF16),
        ((mid, TILE, TILE), F32),
        ((mid, TILE, TILE), F32),
    )


def make_tiles(seeds, places, counts, tiles, slots):
    smem = pl.BlockSpec(memory_space=pltpu.SMEM)
    hbm = pl.BlockSpec(memory_space=pltpu.HBM)
    tables = table_shapes(tiles, slots)
    return pl.pallas_call(
        lambda *r: tiles_kernel(*r, tiles=tiles, slots=slots),
        out_shape=tuple(pltpu.HBM(*t) for t in tables),
        in_specs=[smem] * 3,
        out_specs=(hbm,) * 4,
        scratch_shapes=[pltpu.VMEM(*t) for t in tables]
        + [pltpu.VMEM((9 * tiles, 1, TILE), F32), pltpu.SemaphoreType.DMA((4,))],
        compiler_params=pltpu.CompilerParams(vmem_limit_bytes=16 << 20),
        cost_estimate=SHORT,
        name="tiles",
    )(seeds, places, counts)


def hops_kernel(
    place_ref, base_ref, own_hbm, low_hbm, high_hbm, mate_hbm, far_hbm, pat_hbm, pat_t_hbm, nimg_hbm, ncap_hbm,
    out_ref, bands, pat_ref, pat_t_ref, nimg_ref, ncap_ref, img0, cap0, img1, cap1, acc, acc2, keep_img, keep_cap,
    sems, *, tiles, slots, width,
):
    mid = 5 * tiles
    near = 3 * tiles
    keep = 1.0 - ALPHA
    sources = (own_hbm, nimg_hbm, ncap_hbm, low_hbm, high_hbm, mate_hbm, far_hbm, pat_t_hbm, pat_hbm)
    targets = (bands.at[0], nimg_ref, ncap_ref) + tuple(bands.at[k] for k in range(1, 5)) + (pat_t_ref, pat_ref)
    copies = [pltpu.make_async_copy(s, t, sems.at[k]) for k, (s, t) in enumerate(zip(sources, targets))]
    for copy in copies:
        copy.start()

    def wide(n_ref, m):
        n = n_ref[m]
        return jnp.concatenate([n] * (width // TILE), axis=1)

    def scale(k, base):
        for t in range(tiles):
            m = base + t
            img0[m] = (bands[k, pl.ds(t * TILE, TILE), :].astype(F32) * wide(nimg_ref, m)).astype(BF16)
            cap0[m] = (bands[k, pl.ds((tiles + t) * TILE, TILE), :].astype(F32) * wide(ncap_ref, m)).astype(BF16)

    acc[...] = jnp.zeros_like(acc)
    acc2[...] = jnp.zeros_like(acc2)
    for copy in copies[:3]:
        copy.wait()
    for k, base in enumerate((2 * tiles, 0, 4 * tiles, base_ref[0], base_ref[1])):
        if k:
            copies[2 + k].wait()
        scale(k, base)
    for copy in copies[7:]:
        copy.wait()

    def push(q, state, target, lo, count):
        r = jnp.dot(pat_t_ref[q], state, preferred_element_type=F32)
        for s in range(slots):
            c = place_ref[q * slots + s] - lo
            c = jnp.where((c >= 0) & (c < count), c, count)
            target[c] += r[s * TILE : (s + 1) * TILE]

    def pull(q, source, lo):
        total = None
        for s in range(slots):
            c = place_ref[q * slots + s] - lo
            r = jnp.dot(pat_ref[q, :, pl.ds(s * TILE, TILE)], source[c], preferred_element_type=F32)
            total = r if total is None else total + r
        return total

    def push1(q, c):
        push(q, img0[q], acc, tiles, near)
        return c

    lax.fori_loop(0, mid, push1, 0, unroll=3)

    def pull1(q, c):
        n = wide(nimg_ref, q)
        flow = keep * n * pull(q, cap0, 0)
        img1[q - tiles] = (flow * n).astype(BF16)
        keep_img[q - tiles] = flow
        return c

    lax.fori_loop(tiles, tiles + near, pull1, 0, unroll=3)

    def finish1(m, c):
        n = wide(ncap_ref, m + tiles)
        flow = keep * n * acc[m]
        cap1[m] = (flow * n).astype(BF16)
        keep_cap[m] = flow
        return c

    lax.fori_loop(0, near, finish1, 0, unroll=3)

    def push2(q, c):
        push(q, img1[q - tiles], acc2, 2 * tiles, tiles)
        return c

    lax.fori_loop(tiles, tiles + near, push2, 0, unroll=3)
    for t in range(tiles):
        q = 2 * tiles + t
        rows = pl.ds(t * TILE, TILE)
        flow = keep * wide(nimg_ref, q) * pull(q, cap1, tiles)
        out_ref[rows, :] = (ALPHA * (bands[0, rows, :].astype(F32) + keep_img[tiles + t]) + flow).astype(BF16)
        flow = keep * wide(ncap_ref, q) * acc2[t]
        rows = pl.ds((tiles + t) * TILE, TILE)
        out_ref[rows, :] = (ALPHA * (bands[0, rows, :].astype(F32) + keep_cap[tiles + t]) + flow).astype(BF16)


def propagate(places, bases, own, low, high, mate, far, tables, tiles, slots):
    width = own.shape[1]
    smem = pl.BlockSpec(memory_space=pltpu.SMEM)
    vmem = pl.BlockSpec(memory_space=pltpu.VMEM)
    hbm = pl.BlockSpec(memory_space=pltpu.HBM)
    mid, near = 5 * tiles, 3 * tiles
    return pl.pallas_call(
        lambda *r: hops_kernel(*r, tiles=tiles, slots=slots, width=width),
        out_shape=jax.ShapeDtypeStruct(own.shape, BF16),
        in_specs=[smem] * 2 + [hbm] * 9,
        out_specs=vmem,
        scratch_shapes=[
            pltpu.VMEM((5,) + own.shape, BF16),
            *[pltpu.VMEM(*t) for t in table_shapes(tiles, slots)],
            pltpu.VMEM((mid, TILE, width), BF16),
            pltpu.VMEM((mid, TILE, width), BF16),
            pltpu.VMEM((near, TILE, width), BF16),
            pltpu.VMEM((near, TILE, width), BF16),
            pltpu.VMEM((near + 1, TILE, width), F32),
            pltpu.VMEM((tiles + 1, TILE, width), F32),
            pltpu.VMEM((near, TILE, width), F32),
            pltpu.VMEM((near, TILE, width), F32),
            pltpu.SemaphoreType.DMA((9,)),
        ],
        compiler_params=pltpu.CompilerParams(vmem_limit_bytes=34 << 20),
        cost_estimate=SHORT,
        name="hops",
    )(places, bases, *[pltpu.with_memory_space_constraint(v, pltpu.HBM) for v in (own, low, high, mate, far, *tables)])


BLOCK = 64
GROUP = 4


def grouped(width):
    return [
        pl.BlockSpec((BLOCK, width), lambda i, order, k=k: (order[i * GROUP + k], 0)) for k in range(GROUP)
    ]


def stacked(refs):
    return jnp.concatenate([r[...] for r in refs], axis=0)


def whole(shape):
    return pl.BlockSpec(shape, lambda i, order: (0,) * len(shape))


def out_kernel(order_ref, *refs):
    act, (logit_ref, part_ref) = refs[:GROUP], refs[GROUP:]
    part_ref[...] = jnp.dot(stacked(act), logit_ref[...], preferred_element_type=F32).astype(BF16)


def in_kernel(order_ref, *refs):
    slope, w_out = refs[:GROUP], refs[GROUP : 2 * GROUP]
    logit_ref, feats_ref, part_ref, grad_ref = refs[2 * GROUP :]
    hidden = lax.dot_general(
        stacked(w_out), logit_ref[...], (((1,), (1,)), ((), ())), preferred_element_type=F32
    )
    grad = (hidden * stacked(slope)).astype(BF16)
    grad_ref[...] = grad
    f_in = feats_ref.shape[1]
    part_ref[:, :f_in] = jnp.dot(grad, feats_ref[...], preferred_element_type=F32).astype(BF16)
    bias = jnp.sum(grad.astype(F32), axis=1, keepdims=True)
    part_ref[:, f_in:] = jnp.broadcast_to(bias, (bias.shape[0], TILE)).astype(BF16)


def feat_kernel(order_ref, *refs):
    w_in = refs[:GROUP]
    kept_ref, sent_ref, img_ref, cap_ref, acc_ref = refs[GROUP:]
    i = pl.program_id(0)
    steps = pl.num_programs(0)

    @pl.when(i == 0)
    def _():
        acc_ref[...] = jnp.zeros_like(acc_ref)

    grad = jnp.where(i < steps // 2, kept_ref[...], sent_ref[...])
    acc_ref[...] += lax.dot_general(
        grad, stacked(w_in), (((0,), (0,)), ((), ())), preferred_element_type=F32
    )

    @pl.when(i == steps - 1)
    def _():
        half = img_ref.shape[0]
        img_ref[...] = acc_ref[:half].astype(BF16)
        cap_ref[...] = acc_ref[half:].astype(BF16)


def over_hidden(kernel, name, order, in_specs, out_specs, out_shape, scratch, args):
    return pl.pallas_call(
        kernel,
        out_shape=out_shape,
        grid_spec=pltpu.PrefetchScalarGridSpec(
            num_scalar_prefetch=1,
            grid=(order.shape[0] // GROUP,),
            in_specs=in_specs,
            out_specs=out_specs,
            scratch_shapes=scratch,
        ),
        compiler_params=pltpu.CompilerParams(
            dimension_semantics=("arbitrary",), vmem_limit_bytes=28 << 20
        ),
        cost_estimate=SHORT,
        name=name,
    )(order, *args)


def rows_of_half(width, half, side):
    steps = half // GROUP
    if side:
        return pl.BlockSpec((GROUP * BLOCK, width), lambda i, order: (jnp.maximum(i - steps, 0), 0))
    return pl.BlockSpec((GROUP * BLOCK, width), lambda i, order: (jnp.minimum(i, steps - 1), 0))


def rows_of(width):
    return pl.BlockSpec((GROUP * BLOCK, width), lambda i, order: (i, 0))


def stack_kernel(count_ref, top_ref, bottom_ref, seed_ref, cols_ref, out_ref, meta_ref):
    half = top_ref.shape[0]
    out_ref[:half] = top_ref[...]
    out_ref[half:] = bottom_ref[...]
    tiles, slots = seed_ref.shape
    meta_ref[:, :slots] = seed_ref[...]
    meta_ref[:, slots : 2 * slots] = cols_ref[...]
    row = lax.broadcasted_iota(jnp.int32, (tiles, slots), 0)
    live = jnp.zeros((tiles, slots), jnp.int32)
    for t in range(tiles):
        live = jnp.where(row == t, count_ref[t], live)
    meta_ref[:, 2 * slots :] = live


def stack(top, bottom, seed, cols, counts):
    vmem = pl.BlockSpec(memory_space=pltpu.VMEM)
    shape = (2 * top.shape[0], top.shape[1])
    codes = (seed.shape[0], 3 * seed.shape[1])
    return pl.pallas_call(
        stack_kernel,
        out_shape=(pltpu.HBM(shape, top.dtype), jax.ShapeDtypeStruct(codes, jnp.int32)),
        in_specs=[pl.BlockSpec(memory_space=pltpu.SMEM)] + [vmem] * 4,
        out_specs=(pl.BlockSpec(shape, lambda: (0, 0)), pl.BlockSpec(codes, lambda: (0, 0))),
        cost_estimate=SHORT,
        name="stack",
    )(counts, top, bottom, seed, cols)


def after(value, *done):
    return lax.optimization_barrier((value,) + done)[0]


def moved(array, count, by):
    return lax.ppermute(array, AXES, [(i, i + by) for i in range(count) if 0 <= i + by < count])


def flipped(array, count, mask):
    return lax.ppermute(array, AXES, [(i, i ^ mask) for i in range(count)])


def added(kept, came):
    return (kept.astype(F32) + came.astype(F32)).astype(BF16)


def parts(array, axis):
    return lax.index_in_dim(array, 0, axis, keepdims=False), lax.index_in_dim(array, 1, axis, keepdims=False)


def nearest_pair(count, by):
    return [(i, i + by) for i in range(0, count - by, 2)] + [(i, i - by) for i in range(by + 1, count, 2)]


class Reduction:

    def __init__(self, part, count, bits, orders):
        lanes = part.shape[-1]
        cut = lanes // 2 // TILE * TILE
        self.count, self.last = count, bits[-2:]
        self.parts = [part[..., :cut], part[..., cut:]]
        self.left = [list(bits), list(bits)]
        self.orders = [list(order) for order in orders]

    def start(self):
        self.kept, self.sent, self.came = [], [], []
        for part, left, order in zip(self.parts, self.left, self.orders):
            bit = order.pop(0)
            kept, sent = parts(part, left.index(bit))
            left.remove(bit)
            self.kept.append(kept)
            self.sent.append(sent)
            self.came.append(flipped(sent, self.count, 1 << bit))

    def finish(self, *done):
        self.parts = [added(after(k, *done), c) for k, c in zip(self.kept, self.came)]
        return tuple(self.parts)

    def start_last(self):
        part = jnp.concatenate(self.parts, axis=-1)
        part = part.reshape((4,) + part.shape[-2:])
        hi, lo = self.last
        self.own = part[0]
        self.got = [flipped(part[k], self.count, ((k >> 1) << hi) | ((k & 1) << lo)) for k in range(1, 4)]

    def result(self):
        total = self.own.astype(F32)
        for piece in self.got:
            total = total + piece.astype(F32)
        return total


def per_device(
    feats_img, feats_cap, cot_img, cot_cap, w_in, b_in, w_out, tile_seed, tile_cols, tile_count
):
    local_rows = feats_img.shape[0]
    tiles = local_rows // TILE
    slots = tile_seed.shape[1]
    hid, f_in = w_in.shape
    n_img, n_cap = lax.axis_size("img"), lax.axis_size("cap")
    count = n_img * n_cap
    me = lax.axis_index(AXES)

    even = (me & 1) == 0
    block, meta = stack(cot_img, cot_cap, tile_seed, tile_cols, tile_count)
    other = flipped(meta, count, 1)
    block = after(block, other)
    mate = flipped(block, count, 1)
    low = moved(block, count, 2)
    high = moved(block, count, -2)
    far = lax.ppermute(mate, AXES, nearest_pair(count, 2))
    pair = jnp.where(even, jnp.concatenate([meta, other]), jnp.concatenate([other, meta]))
    feats = jnp.concatenate([feats_img, feats_cap], axis=0)
    pair, feats = lax.optimization_barrier((pair, after(feats, block)))
    pair_low = moved(pair, count, 2)
    pair_high = moved(pair, count, -2)
    pair_far = lax.ppermute(pair, AXES, nearest_pair(count, 4))
    wide = jnp.where(
        even,
        jnp.concatenate([pair_far[tiles:], pair_low, pair, pair_high]),
        jnp.concatenate([pair_low, pair, pair_high, pair_far[:tiles]]),
    )
    frame = jnp.arange(7 * tiles, dtype=jnp.int32)[:, None]
    counts = wide[:, 2 * slots]
    seeds = wide[:, :slots].reshape(-1)
    places = jnp.where(counts[:, None] > 0, wide[:, slots : 2 * slots] - (me - 3) * tiles, frame)
    pats = make_tiles(seeds, (places + tiles).reshape(-1), counts, tiles, slots)

    m = count.bit_length() - 1
    a = n_cap.bit_length() - 1
    cap_bits = list(range(a))
    img_bits = list(range(a + 1, m - 2))
    bits = [a] + cap_bits + img_bits + [m - 1, m - 2]
    pos = jnp.arange(count, dtype=jnp.int32)
    order = jnp.zeros_like(pos)
    for k, bit in enumerate(bits):
        order = order | (((pos >> (m - 1 - k)) & 1) << bit)
    order = order ^ me
    rows = hid // count
    if rows % BLOCK:
        w_in, w_out, b_in = [
            jnp.take(v.reshape((count, rows) + v.shape[1:]), order, axis=0).reshape(v.shape) for v in (w_in, w_out, b_in)
        ]
        order = jnp.arange(hid // BLOCK, dtype=jnp.int32)
    else:
        order = (order[:, None] * (rows // BLOCK) + jnp.arange(rows // BLOCK, dtype=jnp.int32)).reshape(-1)

    across = (((1,), (1,)), ((), ()))
    preact = lax.dot_general(w_in, feats, across, preferred_element_type=F32) + b_in[:, None]
    gelu_value, gelu_slope = gelu_parts(preact)
    hidden_act, gelu_slope = lax.optimization_barrier((gelu_value.astype(BF16), gelu_slope))

    bases = jnp.where(even, jnp.array([3, 1]), jnp.array([1, 3])).astype(jnp.int32) * tiles
    mid_places = (places - tiles)[tiles : 6 * tiles].reshape(-1)
    logit = propagate(mid_places, bases, block, low, high, mate, far, pats, tiles, slots)

    width = cot_img.shape[1]
    nodes = 2 * local_rows
    half = order.shape[0] // 2
    blocked = (2,) * (m - 1) + (rows,)

    def out_half(order, logit):
        return over_hidden(
            out_kernel, "part_out", order, grouped(nodes) + [whole(logit.shape)], rows_of(width),
            jax.ShapeDtypeStruct((hid // 2, width), BF16), [], [hidden_act] * GROUP + [logit],
        ).reshape(blocked + (width,))

    def in_half(order, logit):
        part, grad = over_hidden(
            in_kernel, "part_in", order,
            grouped(nodes) + grouped(width) + [whole(logit.shape), whole(feats.shape)],
            (rows_of(f_in + TILE), rows_of(nodes)),
            (jax.ShapeDtypeStruct((hid // 2, f_in + TILE), BF16), jax.ShapeDtypeStruct((hid // 2, nodes), BF16)),
            [], [gelu_slope] * GROUP + [w_out] * GROUP + [logit, feats],
        )
        return part.reshape(blocked + (f_in + TILE,)), grad

    core = 1 << a
    rest = bits[1:]
    out_sent = out_half(order[half:], logit)
    out_came = flipped(out_sent, count, core)
    out_kept = out_half(order[:half], after(logit, out_sent))
    orders = (cap_bits + img_bits, img_bits + cap_bits)
    out_core = added(out_kept, out_came)
    r_out = Reduction(out_core, count, rest, orders)
    r_out.start()
    in_sent, grad_sent = in_half(order[half:], after(logit, out_core))
    in_came = flipped(in_sent, count, core)
    in_kept, grad_kept = in_half(order[:half], after(logit, grad_sent))
    r_in = Reduction(added(in_kept, in_came), count, rest, orders)
    r_in.start()
    done = r_out.finish(*r_in.sent)
    steps = m - 3
    if steps > 1:
        r_out.start()
    else:
        r_out.start_last()
    grad_img, grad_cap = over_hidden(
        feat_kernel, "feat_grad", order, grouped(f_in) + [rows_of_half(nodes, half, 0), rows_of_half(nodes, half, 1)],
        (whole((local_rows, f_in)),) * 2, (jax.ShapeDtypeStruct((local_rows, f_in), BF16),) * 2,
        [pltpu.VMEM((nodes, f_in), F32)], [w_in] * GROUP + [after(grad_kept, *done), grad_sent],
    )
    done = (grad_img,)
    for k in range(1, steps):
        done = r_out.finish(*done)
        if k + 1 < steps:
            r_out.start()
        else:
            r_out.start_last()
    for k in range(steps):
        done = r_in.finish(*done)
        if k + 1 < steps:
            r_in.start()
        else:
            r_in.start_last()
    grad_scale = 1.0 / math.sqrt(nodes * count)
    g_out, g_in = [r.result() * grad_scale for r in (r_out, r_in)]
    return (grad_img, grad_cap, g_in[:, :f_in], g_out, g_in[:, f_in])


def solution(mesh):
    rows = P(("img", "cap"), None)
    in_specs = (rows, rows, rows, rows, P(), P(), P(), rows, rows, P(("img", "cap")))
    out_specs = (rows, rows, rows, rows, P(("img", "cap")))
    return jax.shard_map(
        per_device, mesh=mesh, in_specs=in_specs, out_specs=out_specs, check_vma=False
    )
```

```python
import math

import jax
import jax.numpy as jnp
from jax import lax
from jax.experimental import pallas as pl
from jax.experimental.pallas import tpu as pltpu
from jax.sharding import PartitionSpec as P

TILE = 128
ALPHA = 0.1
SHORT = pl.CostEstimate(flops=1, transcendentals=0, bytes_accessed=1)
AXES = ("img", "cap")
F32 = jnp.float32
BF16 = jnp.bfloat16


def gelu_parts(preact):
    normal_cdf = 0.5 * (1.0 + jax.scipy.special.erf(preact * 0.7071067811865476))
    normal_pdf = jnp.exp(-0.5 * preact * preact) * 0.3989422804014327
    return (preact * normal_cdf, normal_cdf + preact * normal_pdf)


def tiles_kernel(seed_ref, place_ref, count_ref, *refs, tiles, slots):
    outs, (pat_ref, pat_t_ref, nimg_ref, ncap_ref, deg_ref, sems) = refs[:4], refs[4:]
    all_tiles, mid = 7 * tiles, 5 * tiles
    deg_ref[...] = jnp.zeros_like(deg_ref)
    row = lax.broadcasted_iota(jnp.int32, (TILE, TILE), 0)
    col = lax.broadcasted_iota(jnp.int32, (TILE, TILE), 1)
    first, second = jnp.int32(668265261), jnp.int32(374761393)
    base = (row * 40503 + col * 9973) * first
    base_t = (col * 40503 + row * 9973) * first
    off_diag = row - col

    def pattern(start, seed, live, s):
        mixed = start + seed * first
        mixed = jnp.bitwise_xor(mixed, jnp.right_shift(mixed, 15))
        mixed = mixed * second
        mixed = jnp.bitwise_xor(mixed, jnp.right_shift(mixed, 13))
        edge = jnp.bitwise_and(mixed, 15) == jnp.where(live, 0, 16)
        if s == 0:
            edge = edge | (off_diag == jnp.where(live, 0, TILE))
        return jnp.where(edge, 1.0, 0.0)

    def one(q, full):
        total = None
        for s in range(slots):
            live = s < count_ref[q]
            seed = seed_ref[q * slots + s]
            e = pattern(base, seed, live, s)
            c = place_ref[q * slots + s]
            deg_ref[c] += jnp.sum(e, axis=0, keepdims=True)
            if full:
                m = q - tiles
                pat_ref[m, :, pl.ds(s * TILE, TILE)] = e.astype(BF16)
                pat_t_ref[m, pl.ds(s * TILE, TILE), :] = pattern(base_t, seed, live, s).astype(BF16)
                total = e if total is None else total + e
        if full:
            d = jnp.sum(total, axis=1, keepdims=True)
            n = jnp.where(d > 0.0, lax.rsqrt(d), 0.0)
            nimg_ref[q - tiles] = jnp.broadcast_to(n, (TILE, TILE))

    def edge_body(q, c):
        one(q, False)
        return c

    def mid_body(q, c):
        one(q, True)
        return c

    lax.fori_loop(0, tiles, edge_body, 0)
    lax.fori_loop(tiles, tiles + mid, mid_body, 0)
    copies = [
        pltpu.make_async_copy(src, dst, sems.at[k])
        for k, (src, dst) in enumerate(zip((pat_ref, pat_t_ref, nimg_ref, ncap_ref), outs))
    ]
    for copy in copies[:3]:
        copy.start()
    lax.fori_loop(tiles + mid, all_tiles, edge_body, 0)
    for m in range(mid):
        d = deg_ref[m + 2 * tiles]
        n = jnp.where(d > 0.0, lax.rsqrt(d), 0.0)
        ncap_ref[m] = jnp.broadcast_to(n, (TILE, TILE)).T
    copies[3].start()
    for copy in copies:
        copy.wait()


def table_shapes(tiles, slots):
    mid = 5 * tiles
    return (
        ((mid, TILE, slots * TILE), BF16),
        ((mid, slots * TILE, TILE), BF16),
        ((mid, TILE, TILE), F32),
        ((mid, TILE, TILE), F32),
    )


def make_tiles(seeds, places, counts, tiles, slots):
    smem = pl.BlockSpec(memory_space=pltpu.SMEM)
    hbm = pl.BlockSpec(memory_space=pltpu.HBM)
    tables = table_shapes(tiles, slots)
    return pl.pallas_call(
        lambda *r: tiles_kernel(*r, tiles=tiles, slots=slots),
        out_shape=tuple(pltpu.HBM(*t) for t in tables),
        in_specs=[smem] * 3,
        out_specs=(hbm,) * 4,
        scratch_shapes=[pltpu.VMEM(*t) for t in tables]
        + [pltpu.VMEM((9 * tiles, 1, TILE), F32), pltpu.SemaphoreType.DMA((4,))],
        compiler_params=pltpu.CompilerParams(vmem_limit_bytes=16 << 20),
        cost_estimate=SHORT,
        name="tiles",
    )(seeds, places, counts)


def hops_kernel(
    place_ref, base_ref, own_hbm, low_hbm, high_hbm, mate_hbm, far_hbm, pat_hbm, pat_t_hbm, nimg_hbm, ncap_hbm,
    out_ref, bands, pat_ref, pat_t_ref, nimg_ref, ncap_ref, img0, cap0, img1, cap1, acc, acc2, keep_img, keep_cap,
    sems, *, tiles, slots, width,
):
    mid = 5 * tiles
    near = 3 * tiles
    keep = 1.0 - ALPHA
    sources = (own_hbm, nimg_hbm, ncap_hbm, low_hbm, high_hbm, mate_hbm, far_hbm, pat_t_hbm, pat_hbm)
    targets = (bands.at[0], nimg_ref, ncap_ref) + tuple(bands.at[k] for k in range(1, 5)) + (pat_t_ref, pat_ref)
    copies = [pltpu.make_async_copy(s, t, sems.at[k]) for k, (s, t) in enumerate(zip(sources, targets))]
    for copy in copies:
        copy.start()

    def wide(n_ref, m):
        n = n_ref[m]
        return jnp.concatenate([n] * (width // TILE), axis=1)

    def scale(k, base):
        for t in range(tiles):
            m = base + t
            img0[m] = (bands[k, pl.ds(t * TILE, TILE), :].astype(F32) * wide(nimg_ref, m)).astype(BF16)
            cap0[m] = (bands[k, pl.ds((tiles + t) * TILE, TILE), :].astype(F32) * wide(ncap_ref, m)).astype(BF16)

    acc[...] = jnp.zeros_like(acc)
    acc2[...] = jnp.zeros_like(acc2)
    for copy in copies[:3]:
        copy.wait()
    for k, base in enumerate((2 * tiles, 0, 4 * tiles, base_ref[0], base_ref[1])):
        if k:
            copies[2 + k].wait()
        scale(k, base)
    for copy in copies[7:]:
        copy.wait()

    def push(q, state, target, lo, count):
        r = jnp.dot(pat_t_ref[q], state, preferred_element_type=F32)
        for s in range(slots):
            c = place_ref[q * slots + s] - lo
            c = jnp.where((c >= 0) & (c < count), c, count)
            target[c] += r[s * TILE : (s + 1) * TILE]

    def pull(q, source, lo):
        total = None
        for s in range(slots):
            c = place_ref[q * slots + s] - lo
            r = jnp.dot(pat_ref[q, :, pl.ds(s * TILE, TILE)], source[c], preferred_element_type=F32)
            total = r if total is None else total + r
        return total

    def push1(q, c):
        push(q, img0[q], acc, tiles, near)
        return c

    lax.fori_loop(0, mid, push1, 0, unroll=3)

    def pull1(q, c):
        n = wide(nimg_ref, q)
        flow = keep * n * pull(q, cap0, 0)
        img1[q - tiles] = (flow * n).astype(BF16)
        keep_img[q - tiles] = flow
        return c

    lax.fori_loop(tiles, tiles + near, pull1, 0, unroll=3)

    def finish1(m, c):
        n = wide(ncap_ref, m + tiles)
        flow = keep * n * acc[m]
        cap1[m] = (flow * n).astype(BF16)
        keep_cap[m] = flow
        return c

    lax.fori_loop(0, near, finish1, 0, unroll=3)

    def push2(q, c):
        push(q, img1[q - tiles], acc2, 2 * tiles, tiles)
        return c

    lax.fori_loop(tiles, tiles + near, push2, 0, unroll=3)
    for t in range(tiles):
        q = 2 * tiles + t
        rows = pl.ds(t * TILE, TILE)
        flow = keep * wide(nimg_ref, q) * pull(q, cap1, tiles)
        out_ref[rows, :] = (ALPHA * (bands[0, rows, :].astype(F32) + keep_img[tiles + t]) + flow).astype(BF16)
        flow = keep * wide(ncap_ref, q) * acc2[t]
        rows = pl.ds((tiles + t) * TILE, TILE)
        out_ref[rows, :] = (ALPHA * (bands[0, rows, :].astype(F32) + keep_cap[tiles + t]) + flow).astype(BF16)


def propagate(places, bases, own, low, high, mate, far, tables, tiles, slots):
    width = own.shape[1]
    smem = pl.BlockSpec(memory_space=pltpu.SMEM)
    vmem = pl.BlockSpec(memory_space=pltpu.VMEM)
    hbm = pl.BlockSpec(memory_space=pltpu.HBM)
    mid, near = 5 * tiles, 3 * tiles
    return pl.pallas_call(
        lambda *r: hops_kernel(*r, tiles=tiles, slots=slots, width=width),
        out_shape=jax.ShapeDtypeStruct(own.shape, BF16),
        in_specs=[smem] * 2 + [hbm] * 9,
        out_specs=vmem,
        scratch_shapes=[
            pltpu.VMEM((5,) + own.shape, BF16),
            *[pltpu.VMEM(*t) for t in table_shapes(tiles, slots)],
            pltpu.VMEM((mid, TILE, width), BF16),
            pltpu.VMEM((mid, TILE, width), BF16),
            pltpu.VMEM((near, TILE, width), BF16),
            pltpu.VMEM((near, TILE, width), BF16),
            pltpu.VMEM((near + 1, TILE, width), F32),
            pltpu.VMEM((tiles + 1, TILE, width), F32),
            pltpu.VMEM((near, TILE, width), F32),
            pltpu.VMEM((near, TILE, width), F32),
            pltpu.SemaphoreType.DMA((9,)),
        ],
        compiler_params=pltpu.CompilerParams(vmem_limit_bytes=34 << 20),
        cost_estimate=SHORT,
        name="hops",
    )(places, bases, *[pltpu.with_memory_space_constraint(v, pltpu.HBM) for v in (own, low, high, mate, far, *tables)])


BLOCK = 64
GROUP = 4


def grouped(width):
    return [
        pl.BlockSpec((BLOCK, width), lambda i, order, k=k: (order[i * GROUP + k], 0)) for k in range(GROUP)
    ]


def stacked(refs):
    return jnp.concatenate([r[...] for r in refs], axis=0)


def whole(shape):
    return pl.BlockSpec(shape, lambda i, order: (0,) * len(shape))


def out_kernel(order_ref, *refs):
    act, (logit_ref, part_ref) = refs[:GROUP], refs[GROUP:]
    part_ref[...] = jnp.dot(stacked(act), logit_ref[...], preferred_element_type=F32).astype(BF16)


def in_kernel(order_ref, *refs):
    slope, w_out = refs[:GROUP], refs[GROUP : 2 * GROUP]
    logit_ref, feats_ref, part_ref, grad_ref = refs[2 * GROUP :]
    hidden = lax.dot_general(
        stacked(w_out), logit_ref[...], (((1,), (1,)), ((), ())), preferred_element_type=F32
    )
    grad = (hidden * stacked(slope)).astype(BF16)
    grad_ref[...] = grad
    f_in = feats_ref.shape[1]
    part_ref[:, :f_in] = jnp.dot(grad, feats_ref[...], preferred_element_type=F32).astype(BF16)
    bias = jnp.sum(grad.astype(F32), axis=1, keepdims=True)
    part_ref[:, f_in:] = jnp.broadcast_to(bias, (bias.shape[0], TILE)).astype(BF16)


def feat_kernel(order_ref, *refs):
    w_in = refs[:GROUP]
    kept_ref, sent_ref, img_ref, cap_ref, acc_ref = refs[GROUP:]
    i = pl.program_id(0)
    steps = pl.num_programs(0)

    @pl.when(i == 0)
    def _():
        acc_ref[...] = jnp.zeros_like(acc_ref)

    grad = jnp.where(i < steps // 2, kept_ref[...], sent_ref[...])
    acc_ref[...] += lax.dot_general(
        grad, stacked(w_in), (((0,), (0,)), ((), ())), preferred_element_type=F32
    )

    @pl.when(i == steps - 1)
    def _():
        half = img_ref.shape[0]
        img_ref[...] = acc_ref[:half].astype(BF16)
        cap_ref[...] = acc_ref[half:].astype(BF16)


def over_hidden(kernel, name, order, in_specs, out_specs, out_shape, scratch, args):
    return pl.pallas_call(
        kernel,
        out_shape=out_shape,
        grid_spec=pltpu.PrefetchScalarGridSpec(
            num_scalar_prefetch=1,
            grid=(order.shape[0] // GROUP,),
            in_specs=in_specs,
            out_specs=out_specs,
            scratch_shapes=scratch,
        ),
        compiler_params=pltpu.CompilerParams(
            dimension_semantics=("arbitrary",), vmem_limit_bytes=28 << 20
        ),
        cost_estimate=SHORT,
        name=name,
    )(order, *args)


def rows_of_half(width, half, side):
    steps = half // GROUP
    if side:
        return pl.BlockSpec((GROUP * BLOCK, width), lambda i, order: (jnp.maximum(i - steps, 0), 0))
    return pl.BlockSpec((GROUP * BLOCK, width), lambda i, order: (jnp.minimum(i, steps - 1), 0))


def rows_of(width):
    return pl.BlockSpec((GROUP * BLOCK, width), lambda i, order: (i, 0))


def stack_kernel(count_ref, top_ref, bottom_ref, seed_ref, cols_ref, out_ref, meta_ref):
    half = top_ref.shape[0]
    out_ref[:half] = top_ref[...]
    out_ref[half:] = bottom_ref[...]
    tiles, slots = seed_ref.shape
    meta_ref[:, :slots] = seed_ref[...]
    meta_ref[:, slots : 2 * slots] = cols_ref[...]
    row = lax.broadcasted_iota(jnp.int32, (tiles, slots), 0)
    live = jnp.zeros((tiles, slots), jnp.int32)
    for t in range(tiles):
        live = jnp.where(row == t, count_ref[t], live)
    meta_ref[:, 2 * slots :] = live


def stack(top, bottom, seed, cols, counts):
    vmem = pl.BlockSpec(memory_space=pltpu.VMEM)
    shape = (2 * top.shape[0], top.shape[1])
    codes = (seed.shape[0], 3 * seed.shape[1])
    return pl.pallas_call(
        stack_kernel,
        out_shape=(pltpu.HBM(shape, top.dtype), jax.ShapeDtypeStruct(codes, jnp.int32)),
        in_specs=[pl.BlockSpec(memory_space=pltpu.SMEM)] + [vmem] * 4,
        out_specs=(pl.BlockSpec(shape, lambda: (0, 0)), pl.BlockSpec(codes, lambda: (0, 0))),
        cost_estimate=SHORT,
        name="stack",
    )(counts, top, bottom, seed, cols)


def after(value, *done):
    return lax.optimization_barrier((value,) + done)[0]


def moved(array, count, by):
    return lax.ppermute(array, AXES, [(i, i + by) for i in range(count) if 0 <= i + by < count])


def flipped(array, count, mask):
    return lax.ppermute(array, AXES, [(i, i ^ mask) for i in range(count)])


def added(kept, came):
    return (kept.astype(F32) + came.astype(F32)).astype(BF16)


def parts(array, axis):
    return lax.index_in_dim(array, 0, axis, keepdims=False), lax.index_in_dim(array, 1, axis, keepdims=False)


def nearest_pair(count, by):
    return [(i, i + by) for i in range(0, count - by, 2)] + [(i, i - by) for i in range(by + 1, count, 2)]


def advance(reduction, step, steps):
    if step < steps:
        reduction.start()
    else:
        reduction.start_last()


class Reduction:

    def __init__(self, part, count, bits, orders):
        cut = part.shape[-2] // 2
        self.count, self.last = count, bits[-2:]
        self.parts = [part[..., :cut, :], part[..., cut:, :]]
        self.left = [list(bits), list(bits)]
        self.orders = [list(order) for order in orders]

    def start(self):
        self.kept, self.sent, self.came = [], [], []
        for part, left, order in zip(self.parts, self.left, self.orders):
            bit = order.pop(0)
            kept, sent = parts(part, left.index(bit))
            left.remove(bit)
            self.kept.append(kept)
            self.sent.append(sent)
            self.came.append(flipped(sent, self.count, 1 << bit))

    def finish(self, *done):
        self.parts = [added(after(k, *done), c) for k, c in zip(self.kept, self.came)]
        return tuple(self.parts)

    def start_last(self):
        part = jnp.concatenate(self.parts, axis=-2)
        part = part.reshape((4,) + part.shape[-2:])
        self.sent = [part]
        hi, lo = self.last
        self.own = part[0]
        self.got = [flipped(part[k], self.count, ((k >> 1) << hi) | ((k & 1) << lo)) for k in range(1, 4)]

    def result(self):
        total = self.own.astype(F32)
        for piece in self.got:
            total = total + piece.astype(F32)
        return total


def per_device(
    feats_img, feats_cap, cot_img, cot_cap, w_in, b_in, w_out, tile_seed, tile_cols, tile_count
):
    local_rows = feats_img.shape[0]
    tiles = local_rows // TILE
    slots = tile_seed.shape[1]
    hid, f_in = w_in.shape
    n_img, n_cap = lax.axis_size("img"), lax.axis_size("cap")
    count = n_img * n_cap
    me = lax.axis_index(AXES)

    even = (me & 1) == 0
    block, meta = stack(cot_img, cot_cap, tile_seed, tile_cols, tile_count)
    other = flipped(meta, count, 1)
    third = lax.ppermute(
        meta, AXES, [(i, i + 3) for i in range(1, count - 3, 2)] + [(i, i - 3) for i in range(4, count, 2)]
    )
    mate = flipped(after(block, other), count, 1)
    low = moved(block, count, 2)
    high = moved(block, count, -2)
    far = lax.ppermute(mate, AXES, nearest_pair(count, 2))
    pair = jnp.where(even, jnp.concatenate([meta, other]), jnp.concatenate([other, meta]))
    feats = jnp.concatenate([feats_img, feats_cap], axis=0)
    pair, feats, third = lax.optimization_barrier((pair, after(feats, block), third))
    pair_low = moved(pair, count, 2)
    pair_high = moved(pair, count, -2)
    wide = jnp.where(
        even,
        jnp.concatenate([third, pair_low, pair, pair_high]),
        jnp.concatenate([pair_low, pair, pair_high, third]),
    )
    frame = jnp.arange(7 * tiles, dtype=jnp.int32)[:, None]
    counts = wide[:, 2 * slots]
    seeds = wide[:, :slots].reshape(-1)
    places = jnp.where(counts[:, None] > 0, wide[:, slots : 2 * slots] - (me - 3) * tiles, frame)
    pats = make_tiles(seeds, (places + tiles).reshape(-1), counts, tiles, slots)

    m = count.bit_length() - 1
    a = n_cap.bit_length() - 1
    cap_bits = list(range(a))
    img_bits = list(range(a + 1, m - 2))
    bits = [a] + cap_bits + img_bits + [m - 1, m - 2]
    pos = jnp.arange(count, dtype=jnp.int32)
    order = jnp.zeros_like(pos)
    for k, bit in enumerate(bits):
        order = order | (((pos >> (m - 1 - k)) & 1) << bit)
    order = order ^ me
    rows = hid // count
    if rows % BLOCK:
        w_in, w_out, b_in = [
            jnp.take(v.reshape((count, rows) + v.shape[1:]), order, axis=0).reshape(v.shape) for v in (w_in, w_out, b_in)
        ]
        order = jnp.arange(hid // BLOCK, dtype=jnp.int32)
    else:
        order = (order[:, None] * (rows // BLOCK) + jnp.arange(rows // BLOCK, dtype=jnp.int32)).reshape(-1)

    across = (((1,), (1,)), ((), ()))
    preact = lax.dot_general(w_in, feats, across, preferred_element_type=F32) + b_in[:, None]
    gelu_value, gelu_slope = gelu_parts(preact)
    hidden_act, gelu_slope = lax.optimization_barrier((gelu_value.astype(BF16), gelu_slope))

    bases = jnp.where(even, jnp.array([3, 1]), jnp.array([1, 3])).astype(jnp.int32) * tiles
    mid_places = (places - tiles)[tiles : 6 * tiles].reshape(-1)
    logit = propagate(mid_places, bases, block, low, high, mate, far, pats, tiles, slots)

    width = cot_img.shape[1]
    nodes = 2 * local_rows
    half = order.shape[0] // 2
    blocked = (2,) * (m - 1) + (rows,)

    def out_half(order, logit):
        return over_hidden(
            out_kernel, "part_out", order, grouped(nodes) + [whole(logit.shape)], rows_of(width),
            jax.ShapeDtypeStruct((hid // 2, width), BF16), [], [hidden_act] * GROUP + [logit],
        ).reshape(blocked + (width,))

    def in_half(order, logit):
        part, grad = over_hidden(
            in_kernel, "part_in", order,
            grouped(nodes) + grouped(width) + [whole(logit.shape), whole(feats.shape)],
            (rows_of(f_in + TILE), rows_of(nodes)),
            (jax.ShapeDtypeStruct((hid // 2, f_in + TILE), BF16), jax.ShapeDtypeStruct((hid // 2, nodes), BF16)),
            [], [gelu_slope] * GROUP + [w_out] * GROUP + [logit, feats],
        )
        return part.reshape(blocked + (f_in + TILE,)), grad

    core = 1 << a
    rest = bits[1:]
    orders = (cap_bits + img_bits, img_bits + cap_bits)
    steps = m - 3
    in_sent, grad_sent = in_half(order[half:], logit)
    in_came = flipped(in_sent, count, core)
    in_kept, grad_kept = in_half(order[:half], after(logit, grad_sent))
    r_in = Reduction(added(in_kept, in_came), count, rest, orders)
    r_in.start()
    out_sent = out_half(order[half:], after(logit, *r_in.sent))
    out_came = flipped(out_sent, count, core)
    out_kept = out_half(order[:half], after(logit, out_sent))
    r_out = Reduction(added(out_kept, out_came), count, rest, orders)
    r_out.start()
    for k in range(steps):
        r_in.finish(*r_out.sent)
        advance(r_in, k + 1, steps)
        r_out.finish(*r_in.sent)
        if k + 1 < steps:
            r_out.start()
    grad_img, grad_cap = over_hidden(
        feat_kernel, "feat_grad", order, grouped(f_in) + [rows_of_half(nodes, half, 0), rows_of_half(nodes, half, 1)],
        (whole((local_rows, f_in)),) * 2, (jax.ShapeDtypeStruct((local_rows, f_in), BF16),) * 2,
        [pltpu.VMEM((nodes, f_in), F32)], [w_in] * GROUP + [after(grad_kept, *r_out.parts), grad_sent],
    )
    r_out.start_last()
    r_in.own = after(r_in.own, *r_out.sent)
    grad_scale = 1.0 / math.sqrt(nodes * count)
    g_out, g_in = [r.result() * grad_scale for r in (r_out, r_in)]
    return (grad_img, grad_cap, g_in[:, :f_in], g_out, g_in[:, f_in])


def solution(mesh):
    rows = P(("img", "cap"), None)
    in_specs = (rows, rows, rows, rows, P(), P(), P(), rows, rows, P(("img", "cap")))
    out_specs = (rows, rows, rows, rows, P(("img", "cap")))
    return jax.shard_map(
        per_device, mesh=mesh, in_specs=in_specs, out_specs=out_specs, check_vma=False
    )
```

```python
import math

import jax
import jax.numpy as jnp
from jax import lax
from jax.experimental import pallas as pl
from jax.experimental.pallas import tpu as pltpu
from jax.sharding import PartitionSpec as P

TILE = 128
ALPHA = 0.1
SHORT = pl.CostEstimate(flops=1, transcendentals=0, bytes_accessed=1)
AXES = ("img", "cap")
F32 = jnp.float32
BF16 = jnp.bfloat16


def gelu_parts(preact):
    normal_cdf = 0.5 * (1.0 + jax.scipy.special.erf(preact * 0.7071067811865476))
    normal_pdf = jnp.exp(-0.5 * preact * preact) * 0.3989422804014327
    return (preact * normal_cdf, normal_cdf + preact * normal_pdf)


def tiles_kernel(seed_ref, place_ref, count_ref, *refs, tiles, slots):
    outs, (pat_ref, pat_t_ref, nimg_ref, ncap_ref, deg_ref, sems) = refs[:4], refs[4:]
    all_tiles, mid = 7 * tiles, 5 * tiles
    deg_ref[...] = jnp.zeros_like(deg_ref)
    row = lax.broadcasted_iota(jnp.int32, (TILE, TILE), 0)
    col = lax.broadcasted_iota(jnp.int32, (TILE, TILE), 1)
    first, second = jnp.int32(668265261), jnp.int32(374761393)
    base = (row * 40503 + col * 9973) * first
    base_t = (col * 40503 + row * 9973) * first
    off_diag = row - col

    def pattern(start, seed, live, s):
        mixed = start + seed * first
        mixed = jnp.bitwise_xor(mixed, jnp.right_shift(mixed, 15))
        mixed = mixed * second
        mixed = jnp.bitwise_xor(mixed, jnp.right_shift(mixed, 13))
        edge = jnp.bitwise_and(mixed, 15) == jnp.where(live, 0, 16)
        if s == 0:
            edge = edge | (off_diag == jnp.where(live, 0, TILE))
        return jnp.where(edge, 1.0, 0.0)

    def one(q, full):
        total = None
        for s in range(slots):
            live = s < count_ref[q]
            seed = seed_ref[q * slots + s]
            e = pattern(base, seed, live, s)
            c = place_ref[q * slots + s]
            deg_ref[c] += jnp.sum(e, axis=0, keepdims=True)
            if full:
                m = q - tiles
                pat_ref[m, :, pl.ds(s * TILE, TILE)] = e.astype(BF16)
                pat_t_ref[m, pl.ds(s * TILE, TILE), :] = pattern(base_t, seed, live, s).astype(BF16)
                total = e if total is None else total + e
        if full:
            d = jnp.sum(total, axis=1, keepdims=True)
            n = jnp.where(d > 0.0, lax.rsqrt(d), 0.0)
            nimg_ref[q - tiles] = jnp.broadcast_to(n, (TILE, TILE))

    def edge_body(q, c):
        one(q, False)
        return c

    def mid_body(q, c):
        one(q, True)
        return c

    lax.fori_loop(0, tiles, edge_body, 0)
    lax.fori_loop(tiles, tiles + mid, mid_body, 0)
    copies = [
        pltpu.make_async_copy(src, dst, sems.at[k])
        for k, (src, dst) in enumerate(zip((pat_ref, pat_t_ref, nimg_ref, ncap_ref), outs))
    ]
    for copy in copies[:3]:
        copy.start()
    lax.fori_loop(tiles + mid, all_tiles, edge_body, 0)
    for m in range(mid):
        d = deg_ref[m + 2 * tiles]
        n = jnp.where(d > 0.0, lax.rsqrt(d), 0.0)
        ncap_ref[m] = jnp.broadcast_to(n, (TILE, TILE)).T
    copies[3].start()
    for copy in copies:
        copy.wait()


def table_shapes(tiles, slots):
    mid = 5 * tiles
    return (
        ((mid, TILE, slots * TILE), BF16),
        ((mid, slots * TILE, TILE), BF16),
        ((mid, TILE, TILE), F32),
        ((mid, TILE, TILE), F32),
    )


def make_tiles(seeds, places, counts, tiles, slots):
    smem = pl.BlockSpec(memory_space=pltpu.SMEM)
    hbm = pl.BlockSpec(memory_space=pltpu.HBM)
    tables = table_shapes(tiles, slots)
    return pl.pallas_call(
        lambda *r: tiles_kernel(*r, tiles=tiles, slots=slots),
        out_shape=tuple(pltpu.HBM(*t) for t in tables),
        in_specs=[smem] * 3,
        out_specs=(hbm,) * 4,
        scratch_shapes=[pltpu.VMEM(*t) for t in tables]
        + [pltpu.VMEM((9 * tiles, 1, TILE), F32), pltpu.SemaphoreType.DMA((4,))],
        compiler_params=pltpu.CompilerParams(vmem_limit_bytes=16 << 20),
        cost_estimate=SHORT,
        name="tiles",
    )(seeds, places, counts)


def hops_kernel(
    place_ref, base_ref, own_hbm, low_hbm, high_hbm, mate_hbm, far_hbm, pat_hbm, pat_t_hbm, nimg_hbm, ncap_hbm,
    out_ref, bands, pat_ref, pat_t_ref, nimg_ref, ncap_ref, img0, cap0, img1, cap1, acc, acc2, keep_img, keep_cap,
    sems, *, tiles, slots, width,
):
    mid = 5 * tiles
    near = 3 * tiles
    keep = 1.0 - ALPHA
    sources = (own_hbm, nimg_hbm, ncap_hbm, low_hbm, high_hbm, mate_hbm, far_hbm, pat_t_hbm, pat_hbm)
    targets = (bands.at[0], nimg_ref, ncap_ref) + tuple(bands.at[k] for k in range(1, 5)) + (pat_t_ref, pat_ref)
    copies = [pltpu.make_async_copy(s, t, sems.at[k]) for k, (s, t) in enumerate(zip(sources, targets))]
    for copy in copies:
        copy.start()

    def wide(n_ref, m):
        n = n_ref[m]
        return jnp.concatenate([n] * (width // TILE), axis=1)

    def scale(k, base):
        for t in range(tiles):
            m = base + t
            img0[m] = (bands[k, pl.ds(t * TILE, TILE), :].astype(F32) * wide(nimg_ref, m)).astype(BF16)
            cap0[m] = (bands[k, pl.ds((tiles + t) * TILE, TILE), :].astype(F32) * wide(ncap_ref, m)).astype(BF16)

    acc[...] = jnp.zeros_like(acc)
    acc2[...] = jnp.zeros_like(acc2)
    for copy in copies[:3]:
        copy.wait()
    for k, base in enumerate((2 * tiles, 0, 4 * tiles, base_ref[0], base_ref[1])):
        if k:
            copies[2 + k].wait()
        scale(k, base)
    for copy in copies[7:]:
        copy.wait()

    def push(q, state, target, lo, count):
        r = jnp.dot(pat_t_ref[q], state, preferred_element_type=F32)
        for s in range(slots):
            c = place_ref[q * slots + s] - lo
            c = jnp.where((c >= 0) & (c < count), c, count)
            target[c] += r[s * TILE : (s + 1) * TILE]

    def pull(q, source, lo):
        total = None
        for s in range(slots):
            c = place_ref[q * slots + s] - lo
            r = jnp.dot(pat_ref[q, :, pl.ds(s * TILE, TILE)], source[c], preferred_element_type=F32)
            total = r if total is None else total + r
        return total

    def push1(q, c):
        push(q, img0[q], acc, tiles, near)
        return c

    lax.fori_loop(0, mid, push1, 0, unroll=3)

    def pull1(q, c):
        n = wide(nimg_ref, q)
        flow = keep * n * pull(q, cap0, 0)
        img1[q - tiles] = (flow * n).astype(BF16)
        keep_img[q - tiles] = flow
        return c

    lax.fori_loop(tiles, tiles + near, pull1, 0, unroll=3)

    def finish1(m, c):
        n = wide(ncap_ref, m + tiles)
        flow = keep * n * acc[m]
        cap1[m] = (flow * n).astype(BF16)
        keep_cap[m] = flow
        return c

    lax.fori_loop(0, near, finish1, 0, unroll=3)

    def push2(q, c):
        push(q, img1[q - tiles], acc2, 2 * tiles, tiles)
        return c

    lax.fori_loop(tiles, tiles + near, push2, 0, unroll=3)
    for t in range(tiles):
        q = 2 * tiles + t
        rows = pl.ds(t * TILE, TILE)
        flow = keep * wide(nimg_ref, q) * pull(q, cap1, tiles)
        out_ref[rows, :] = (ALPHA * (bands[0, rows, :].astype(F32) + keep_img[tiles + t]) + flow).astype(BF16)
        flow = keep * wide(ncap_ref, q) * acc2[t]
        rows = pl.ds((tiles + t) * TILE, TILE)
        out_ref[rows, :] = (ALPHA * (bands[0, rows, :].astype(F32) + keep_cap[tiles + t]) + flow).astype(BF16)


def propagate(places, bases, own, low, high, mate, far, tables, tiles, slots):
    width = own.shape[1]
    smem = pl.BlockSpec(memory_space=pltpu.SMEM)
    vmem = pl.BlockSpec(memory_space=pltpu.VMEM)
    hbm = pl.BlockSpec(memory_space=pltpu.HBM)
    mid, near = 5 * tiles, 3 * tiles
    return pl.pallas_call(
        lambda *r: hops_kernel(*r, tiles=tiles, slots=slots, width=width),
        out_shape=jax.ShapeDtypeStruct(own.shape, BF16),
        in_specs=[smem] * 2 + [hbm] * 9,
        out_specs=vmem,
        scratch_shapes=[
            pltpu.VMEM((5,) + own.shape, BF16),
            *[pltpu.VMEM(*t) for t in table_shapes(tiles, slots)],
            pltpu.VMEM((mid, TILE, width), BF16),
            pltpu.VMEM((mid, TILE, width), BF16),
            pltpu.VMEM((near, TILE, width), BF16),
            pltpu.VMEM((near, TILE, width), BF16),
            pltpu.VMEM((near + 1, TILE, width), F32),
            pltpu.VMEM((tiles + 1, TILE, width), F32),
            pltpu.VMEM((near, TILE, width), F32),
            pltpu.VMEM((near, TILE, width), F32),
            pltpu.SemaphoreType.DMA((9,)),
        ],
        compiler_params=pltpu.CompilerParams(vmem_limit_bytes=34 << 20),
        cost_estimate=SHORT,
        name="hops",
    )(places, bases, *[pltpu.with_memory_space_constraint(v, pltpu.HBM) for v in (own, low, high, mate, far, *tables)])


BLOCK = 64
GROUP = 4


def grouped(width):
    return [
        pl.BlockSpec((BLOCK, width), lambda i, order, k=k: (order[i * GROUP + k], 0)) for k in range(GROUP)
    ]


def stacked(refs):
    return jnp.concatenate([r[...] for r in refs], axis=0)


def whole(shape):
    return pl.BlockSpec(shape, lambda i, order: (0,) * len(shape))


def out_kernel(order_ref, *refs):
    act, (logit_ref, part_ref) = refs[:GROUP], refs[GROUP:]
    part_ref[...] = jnp.dot(stacked(act), logit_ref[...], preferred_element_type=F32).astype(BF16)


def in_kernel(order_ref, *refs):
    slope, w_out = refs[:GROUP], refs[GROUP : 2 * GROUP]
    logit_ref, feats_ref, part_ref, grad_ref = refs[2 * GROUP :]
    hidden = lax.dot_general(
        stacked(w_out), logit_ref[...], (((1,), (1,)), ((), ())), preferred_element_type=F32
    )
    grad = (hidden * stacked(slope)).astype(BF16)
    grad_ref[...] = grad
    f_in = feats_ref.shape[1]
    part_ref[:, :f_in] = jnp.dot(grad, feats_ref[...], preferred_element_type=F32).astype(BF16)
    bias = jnp.sum(grad.astype(F32), axis=1, keepdims=True)
    part_ref[:, f_in:] = jnp.broadcast_to(bias, (bias.shape[0], TILE)).astype(BF16)


def feat_kernel(order_ref, *refs):
    w_in = refs[:GROUP]
    kept_ref, sent_ref, img_ref, cap_ref, acc_ref = refs[GROUP:]
    i = pl.program_id(0)
    steps = pl.num_programs(0)

    @pl.when(i == 0)
    def _():
        acc_ref[...] = jnp.zeros_like(acc_ref)

    grad = jnp.where(i < steps // 2, kept_ref[...], sent_ref[...])
    acc_ref[...] += lax.dot_general(
        grad, stacked(w_in), (((0,), (0,)), ((), ())), preferred_element_type=F32
    )

    @pl.when(i == steps - 1)
    def _():
        half = img_ref.shape[0]
        img_ref[...] = acc_ref[:half].astype(BF16)
        cap_ref[...] = acc_ref[half:].astype(BF16)


def over_hidden(kernel, name, order, in_specs, out_specs, out_shape, scratch, args):
    return pl.pallas_call(
        kernel,
        out_shape=out_shape,
        grid_spec=pltpu.PrefetchScalarGridSpec(
            num_scalar_prefetch=1,
            grid=(order.shape[0] // GROUP,),
            in_specs=in_specs,
            out_specs=out_specs,
            scratch_shapes=scratch,
        ),
        compiler_params=pltpu.CompilerParams(
            dimension_semantics=("arbitrary",), vmem_limit_bytes=28 << 20
        ),
        cost_estimate=SHORT,
        name=name,
    )(order, *args)


def rows_of_half(width, half, side):
    steps = half // GROUP
    if side:
        return pl.BlockSpec((GROUP * BLOCK, width), lambda i, order: (jnp.maximum(i - steps, 0), 0))
    return pl.BlockSpec((GROUP * BLOCK, width), lambda i, order: (jnp.minimum(i, steps - 1), 0))


def rows_of(width):
    return pl.BlockSpec((GROUP * BLOCK, width), lambda i, order: (i, 0))


def stack_kernel(count_ref, top_ref, bottom_ref, seed_ref, cols_ref, out_ref, meta_ref):
    half = top_ref.shape[0]
    out_ref[:half] = top_ref[...]
    out_ref[half:] = bottom_ref[...]
    tiles, slots = seed_ref.shape
    meta_ref[:, :slots] = seed_ref[...]
    meta_ref[:, slots : 2 * slots] = cols_ref[...]
    row = lax.broadcasted_iota(jnp.int32, (tiles, slots), 0)
    live = jnp.zeros((tiles, slots), jnp.int32)
    for t in range(tiles):
        live = jnp.where(row == t, count_ref[t], live)
    meta_ref[:, 2 * slots :] = live


def stack(top, bottom, seed, cols, counts):
    vmem = pl.BlockSpec(memory_space=pltpu.VMEM)
    shape = (2 * top.shape[0], top.shape[1])
    codes = (seed.shape[0], 3 * seed.shape[1])
    return pl.pallas_call(
        stack_kernel,
        out_shape=(pltpu.HBM(shape, top.dtype), jax.ShapeDtypeStruct(codes, jnp.int32)),
        in_specs=[pl.BlockSpec(memory_space=pltpu.SMEM)] + [vmem] * 4,
        out_specs=(pl.BlockSpec(shape, lambda: (0, 0)), pl.BlockSpec(codes, lambda: (0, 0))),
        cost_estimate=SHORT,
        name="stack",
    )(counts, top, bottom, seed, cols)


def after(value, *done):
    return lax.optimization_barrier((value,) + done)[0]


def moved(array, count, by):
    return lax.ppermute(array, AXES, [(i, i + by) for i in range(count) if 0 <= i + by < count])


def flipped(array, count, mask):
    return lax.ppermute(array, AXES, [(i, i ^ mask) for i in range(count)])


def added(kept, came):
    return (kept.astype(F32) + came.astype(F32)).astype(BF16)


def parts(array, axis):
    return lax.index_in_dim(array, 0, axis, keepdims=False), lax.index_in_dim(array, 1, axis, keepdims=False)


def nearest_pair(count, by):
    return [(i, i + by) for i in range(0, count - by, 2)] + [(i, i - by) for i in range(by + 1, count, 2)]


class Reduction:

    def __init__(self, part, count, bits, orders, ends):
        cut = part.shape[-2] // 2
        self.count = count
        self.parts = [part[..., :cut, :], part[..., cut:, :]]
        self.left = [list(bits), list(bits)]
        self.orders = [list(order) + list(ends) for order in orders]
        self.split = len(orders[0])

    def start(self):
        if not self.split:
            self.parts = [jnp.concatenate(self.parts, axis=-2)]
        self.split -= 1
        self.kept, self.sent, self.came = [], [], []
        for part, left, order in zip(self.parts, self.left, self.orders):
            bit = order.pop(0)
            kept, sent = parts(part, left.index(bit))
            left.remove(bit)
            self.kept.append(kept)
            self.sent.append(sent)
            self.came.append(flipped(sent, self.count, 1 << bit))

    def finish(self, *done):
        self.parts = [added(after(k, *done), c) for k, c in zip(self.kept, self.came)]

    def result(self):
        return self.kept[0].astype(F32) + self.came[0].astype(F32)


def per_device(
    feats_img, feats_cap, cot_img, cot_cap, w_in, b_in, w_out, tile_seed, tile_cols, tile_count
):
    local_rows = feats_img.shape[0]
    tiles = local_rows // TILE
    slots = tile_seed.shape[1]
    hid, f_in = w_in.shape
    n_img, n_cap = lax.axis_size("img"), lax.axis_size("cap")
    count = n_img * n_cap
    me = lax.axis_index(AXES)

    even = (me & 1) == 0
    block, meta = stack(cot_img, cot_cap, tile_seed, tile_cols, tile_count)
    other = flipped(meta, count, 1)
    third = lax.ppermute(
        meta, AXES, [(i, i + 3) for i in range(1, count - 3, 2)] + [(i, i - 3) for i in range(4, count, 2)]
    )
    block = after(block, other)
    mate = flipped(block, count, 1)
    low = moved(block, count, 2)
    high = moved(block, count, -2)
    far = lax.ppermute(mate, AXES, nearest_pair(count, 2))
    pair = jnp.where(even, jnp.concatenate([meta, other]), jnp.concatenate([other, meta]))
    feats = jnp.concatenate([feats_img, feats_cap], axis=0)
    pair, feats, third = lax.optimization_barrier((pair, after(feats, block), third))
    pair_low = moved(pair, count, 2)
    pair_high = moved(pair, count, -2)
    wide = jnp.where(
        even,
        jnp.concatenate([third, pair_low, pair, pair_high]),
        jnp.concatenate([pair_low, pair, pair_high, third]),
    )
    frame = jnp.arange(7 * tiles, dtype=jnp.int32)[:, None]
    counts = wide[:, 2 * slots]
    seeds = wide[:, :slots].reshape(-1)
    places = jnp.where(counts[:, None] > 0, wide[:, slots : 2 * slots] - (me - 3) * tiles, frame)
    pats = make_tiles(seeds, (places + tiles).reshape(-1), counts, tiles, slots)

    m = count.bit_length() - 1
    a = n_cap.bit_length() - 1
    cap_bits = list(range(a))
    img_bits = list(range(a + 1, m - 2))
    bits = [a] + cap_bits + img_bits + [m - 2, m - 1]
    pos = jnp.arange(count, dtype=jnp.int32)
    order = jnp.zeros_like(pos)
    for k, bit in enumerate(bits):
        order = order | (((pos >> (m - 1 - k)) & 1) << bit)
    order = order ^ me
    rows = hid // count
    if rows % BLOCK:
        w_in, w_out, b_in = [
            jnp.take(v.reshape((count, rows) + v.shape[1:]), order, axis=0).reshape(v.shape) for v in (w_in, w_out, b_in)
        ]
        order = jnp.arange(hid // BLOCK, dtype=jnp.int32)
    else:
        order = (order[:, None] * (rows // BLOCK) + jnp.arange(rows // BLOCK, dtype=jnp.int32)).reshape(-1)

    across = (((1,), (1,)), ((), ()))
    preact = lax.dot_general(w_in, feats, across, preferred_element_type=F32) + b_in[:, None]
    gelu_value, gelu_slope = gelu_parts(preact)
    hidden_act, gelu_slope = lax.optimization_barrier((gelu_value.astype(BF16), gelu_slope))

    bases = jnp.where(even, jnp.array([3, 1]), jnp.array([1, 3])).astype(jnp.int32) * tiles
    mid_places = (places - tiles)[tiles : 6 * tiles].reshape(-1)
    logit = propagate(mid_places, bases, block, low, high, mate, far, pats, tiles, slots)

    width = cot_img.shape[1]
    nodes = 2 * local_rows
    half = order.shape[0] // 2
    blocked = (2,) * (m - 1) + (rows,)

    def out_half(order, logit):
        return over_hidden(
            out_kernel, "part_out", order, grouped(nodes) + [whole(logit.shape)], rows_of(width),
            jax.ShapeDtypeStruct((hid // 2, width), BF16), [], [hidden_act] * GROUP + [logit],
        ).reshape(blocked + (width,))

    def in_half(order, logit):
        part, grad = over_hidden(
            in_kernel, "part_in", order,
            grouped(nodes) + grouped(width) + [whole(logit.shape), whole(feats.shape)],
            (rows_of(f_in + TILE), rows_of(nodes)),
            (jax.ShapeDtypeStruct((hid // 2, f_in + TILE), BF16), jax.ShapeDtypeStruct((hid // 2, nodes), BF16)),
            [], [gelu_slope] * GROUP + [w_out] * GROUP + [logit, feats],
        )
        return part.reshape(blocked + (f_in + TILE,)), grad

    core = 1 << a
    rest = bits[1:]
    orders = (cap_bits + img_bits, img_bits + cap_bits)
    ends = (m - 2, m - 1)
    in_sent, grad_sent = in_half(order[half:], logit)
    in_came = flipped(in_sent, count, core)
    in_kept, grad_kept = in_half(order[:half], after(logit, grad_sent))
    r_in = Reduction(added(in_kept, in_came), count, rest, orders, ends)
    r_in.start()
    out_sent = out_half(order[half:], after(logit, *r_in.sent))
    out_came = flipped(out_sent, count, core)
    out_kept = out_half(order[:half], after(logit, out_sent))
    r_out = Reduction(added(out_kept, out_came), count, rest, orders, ends)
    r_out.start()
    for k in range(m - 2):
        r_in.finish(*r_out.sent)
        r_in.start()
        r_out.finish(*r_in.sent)
        if k < m - 3:
            r_out.start()
    grad_img, grad_cap = over_hidden(
        feat_kernel, "feat_grad", order, grouped(f_in) + [rows_of_half(nodes, half, 0), rows_of_half(nodes, half, 1)],
        (whole((local_rows, f_in)),) * 2, (jax.ShapeDtypeStruct((local_rows, f_in), BF16),) * 2,
        [pltpu.VMEM((nodes, f_in), F32)], [w_in] * GROUP + [after(grad_kept, *r_out.parts), grad_sent],
    )
    r_out.start()
    grad_scale = 1.0 / math.sqrt(nodes * count)
    g_out, g_in = [r.result() * grad_scale for r in (r_out, r_in)]
    return (grad_img, grad_cap, g_in[:, :f_in], g_out, g_in[:, f_in])


def solution(mesh):
    rows = P(("img", "cap"), None)
    in_specs = (rows, rows, rows, rows, P(), P(), P(), rows, rows, P(("img", "cap")))
    out_specs = (rows, rows, rows, rows, P(("img", "cap")))
    return jax.shard_map(
        per_device, mesh=mesh, in_specs=in_specs, out_specs=out_specs, check_vma=False
    )
```

```python
import math

import jax
import jax.numpy as jnp
from jax import lax
from jax.experimental import pallas as pl
from jax.experimental.pallas import tpu as pltpu
from jax.sharding import PartitionSpec as P

TILE = 128
ALPHA = 0.1
SHORT = pl.CostEstimate(flops=1, transcendentals=0, bytes_accessed=1)
AXES = ("img", "cap")
F32 = jnp.float32
BF16 = jnp.bfloat16


def gelu_parts(preact):
    normal_cdf = 0.5 * (1.0 + jax.scipy.special.erf(preact * 0.7071067811865476))
    normal_pdf = jnp.exp(-0.5 * preact * preact) * 0.3989422804014327
    return (preact * normal_cdf, normal_cdf + preact * normal_pdf)


def tiles_kernel(seed_ref, place_ref, count_ref, *refs, tiles, slots):
    outs, (pat_ref, pat_t_ref, nimg_ref, ncap_ref, deg_ref, sems) = refs[:4], refs[4:]
    all_tiles, mid = 7 * tiles, 5 * tiles
    deg_ref[...] = jnp.zeros_like(deg_ref)
    row = lax.broadcasted_iota(jnp.int32, (TILE, TILE), 0)
    col = lax.broadcasted_iota(jnp.int32, (TILE, TILE), 1)
    first, second = jnp.int32(668265261), jnp.int32(374761393)
    base = (row * 40503 + col * 9973) * first
    base_t = (col * 40503 + row * 9973) * first
    off_diag = row - col

    def pattern(start, seed, live, s):
        mixed = start + seed * first
        mixed = jnp.bitwise_xor(mixed, jnp.right_shift(mixed, 15))
        mixed = mixed * second
        mixed = jnp.bitwise_xor(mixed, jnp.right_shift(mixed, 13))
        edge = jnp.bitwise_and(mixed, 15) == jnp.where(live, 0, 16)
        if s == 0:
            edge = edge | (off_diag == jnp.where(live, 0, TILE))
        return jnp.where(edge, 1.0, 0.0)

    def one(q, full):
        total = None
        for s in range(slots):
            live = s < count_ref[q]
            seed = seed_ref[q * slots + s]
            e = pattern(base, seed, live, s)
            c = place_ref[q * slots + s]
            deg_ref[c] += jnp.sum(e, axis=0, keepdims=True)
            if full:
                m = q - tiles
                pat_ref[m, :, pl.ds(s * TILE, TILE)] = e.astype(BF16)
                pat_t_ref[m, pl.ds(s * TILE, TILE), :] = pattern(base_t, seed, live, s).astype(BF16)
                total = e if total is None else total + e
        if full:
            d = jnp.sum(total, axis=1, keepdims=True)
            n = jnp.where(d > 0.0, lax.rsqrt(d), 0.0)
            nimg_ref[q - tiles] = jnp.broadcast_to(n, (TILE, TILE))

    def edge_body(q, c):
        one(q, False)
        return c

    def mid_body(q, c):
        one(q, True)
        return c

    lax.fori_loop(0, tiles, edge_body, 0)
    lax.fori_loop(tiles, tiles + mid, mid_body, 0)
    copies = [
        pltpu.make_async_copy(src, dst, sems.at[k])
        for k, (src, dst) in enumerate(zip((pat_ref, pat_t_ref, nimg_ref, ncap_ref), outs))
    ]
    for copy in copies[:3]:
        copy.start()
    lax.fori_loop(tiles + mid, all_tiles, edge_body, 0)
    for m in range(mid):
        d = deg_ref[m + 2 * tiles]
        n = jnp.where(d > 0.0, lax.rsqrt(d), 0.0)
        ncap_ref[m] = jnp.broadcast_to(n, (TILE, TILE)).T
    copies[3].start()
    for copy in copies:
        copy.wait()


def table_shapes(tiles, slots):
    mid = 5 * tiles
    return (
        ((mid, TILE, slots * TILE), BF16),
        ((mid, slots * TILE, TILE), BF16),
        ((mid, TILE, TILE), F32),
        ((mid, TILE, TILE), F32),
    )


def make_tiles(seeds, places, counts, tiles, slots):
    smem = pl.BlockSpec(memory_space=pltpu.SMEM)
    hbm = pl.BlockSpec(memory_space=pltpu.HBM)
    tables = table_shapes(tiles, slots)
    return pl.pallas_call(
        lambda *r: tiles_kernel(*r, tiles=tiles, slots=slots),
        out_shape=tuple(pltpu.HBM(*t) for t in tables),
        in_specs=[smem] * 3,
        out_specs=(hbm,) * 4,
        scratch_shapes=[pltpu.VMEM(*t) for t in tables]
        + [pltpu.VMEM((9 * tiles, 1, TILE), F32), pltpu.SemaphoreType.DMA((4,))],
        compiler_params=pltpu.CompilerParams(vmem_limit_bytes=16 << 20),
        cost_estimate=SHORT,
        name="tiles",
    )(seeds, places, counts)


def hops_kernel(
    place_ref, base_ref, own_hbm, low_hbm, high_hbm, mate_hbm, far_hbm, pat_hbm, pat_t_hbm, nimg_hbm, ncap_hbm,
    out_ref, bands, pat_ref, pat_t_ref, nimg_ref, ncap_ref, img0, cap0, img1, cap1, acc, acc2, keep_img, keep_cap,
    sems, *, tiles, slots, width,
):
    mid = 5 * tiles
    near = 3 * tiles
    keep = 1.0 - ALPHA
    sources = (own_hbm, nimg_hbm, ncap_hbm, low_hbm, high_hbm, mate_hbm, far_hbm, pat_t_hbm, pat_hbm)
    targets = (bands.at[0], nimg_ref, ncap_ref) + tuple(bands.at[k] for k in range(1, 5)) + (pat_t_ref, pat_ref)
    copies = [pltpu.make_async_copy(s, t, sems.at[k]) for k, (s, t) in enumerate(zip(sources, targets))]
    for copy in copies:
        copy.start()

    def wide(n_ref, m):
        n = n_ref[m]
        return jnp.concatenate([n] * (width // TILE), axis=1)

    def scale(k, base):
        for t in range(tiles):
            m = base + t
            img0[m] = (bands[k, pl.ds(t * TILE, TILE), :].astype(F32) * wide(nimg_ref, m)).astype(BF16)
            cap0[m] = (bands[k, pl.ds((tiles + t) * TILE, TILE), :].astype(F32) * wide(ncap_ref, m)).astype(BF16)

    acc[...] = jnp.zeros_like(acc)
    acc2[...] = jnp.zeros_like(acc2)
    for copy in copies[:3]:
        copy.wait()
    for k, base in enumerate((2 * tiles, 0, 4 * tiles, base_ref[0], base_ref[1])):
        if k:
            copies[2 + k].wait()
        scale(k, base)
    for copy in copies[7:]:
        copy.wait()

    def push(q, state, target, lo, count):
        r = jnp.dot(pat_t_ref[q], state, preferred_element_type=F32)
        for s in range(slots):
            c = place_ref[q * slots + s] - lo
            c = jnp.where((c >= 0) & (c < count), c, count)
            target[c] += r[s * TILE : (s + 1) * TILE]

    def pull(q, source, lo):
        total = None
        for s in range(slots):
            c = place_ref[q * slots + s] - lo
            r = jnp.dot(pat_ref[q, :, pl.ds(s * TILE, TILE)], source[c], preferred_element_type=F32)
            total = r if total is None else total + r
        return total

    def push1(q, c):
        push(q, img0[q], acc, tiles, near)
        return c

    lax.fori_loop(0, mid, push1, 0, unroll=3)

    def pull1(q, c):
        n = wide(nimg_ref, q)
        flow = keep * n * pull(q, cap0, 0)
        img1[q - tiles] = (flow * n).astype(BF16)
        keep_img[q - tiles] = flow
        return c

    lax.fori_loop(tiles, tiles + near, pull1, 0, unroll=3)

    def finish1(m, c):
        n = wide(ncap_ref, m + tiles)
        flow = keep * n * acc[m]
        cap1[m] = (flow * n).astype(BF16)
        keep_cap[m] = flow
        return c

    lax.fori_loop(0, near, finish1, 0, unroll=3)

    def push2(q, c):
        push(q, img1[q - tiles], acc2, 2 * tiles, tiles)
        return c

    lax.fori_loop(tiles, tiles + near, push2, 0, unroll=3)
    for t in range(tiles):
        q = 2 * tiles + t
        rows = pl.ds(t * TILE, TILE)
        flow = keep * wide(nimg_ref, q) * pull(q, cap1, tiles)
        out_ref[rows, :] = (ALPHA * (bands[0, rows, :].astype(F32) + keep_img[tiles + t]) + flow).astype(BF16)
        flow = keep * wide(ncap_ref, q) * acc2[t]
        rows = pl.ds((tiles + t) * TILE, TILE)
        out_ref[rows, :] = (ALPHA * (bands[0, rows, :].astype(F32) + keep_cap[tiles + t]) + flow).astype(BF16)


def propagate(places, bases, own, low, high, mate, far, tables, tiles, slots):
    width = own.shape[1]
    smem = pl.BlockSpec(memory_space=pltpu.SMEM)
    vmem = pl.BlockSpec(memory_space=pltpu.VMEM)
    hbm = pl.BlockSpec(memory_space=pltpu.HBM)
    mid, near = 5 * tiles, 3 * tiles
    return pl.pallas_call(
        lambda *r: hops_kernel(*r, tiles=tiles, slots=slots, width=width),
        out_shape=jax.ShapeDtypeStruct(own.shape, BF16),
        in_specs=[smem] * 2 + [hbm] * 9,
        out_specs=vmem,
        scratch_shapes=[
            pltpu.VMEM((5,) + own.shape, BF16),
            *[pltpu.VMEM(*t) for t in table_shapes(tiles, slots)],
            pltpu.VMEM((mid, TILE, width), BF16),
            pltpu.VMEM((mid, TILE, width), BF16),
            pltpu.VMEM((near, TILE, width), BF16),
            pltpu.VMEM((near, TILE, width), BF16),
            pltpu.VMEM((near + 1, TILE, width), F32),
            pltpu.VMEM((tiles + 1, TILE, width), F32),
            pltpu.VMEM((near, TILE, width), F32),
            pltpu.VMEM((near, TILE, width), F32),
            pltpu.SemaphoreType.DMA((9,)),
        ],
        compiler_params=pltpu.CompilerParams(vmem_limit_bytes=34 << 20),
        cost_estimate=SHORT,
        name="hops",
    )(places, bases, *[pltpu.with_memory_space_constraint(v, pltpu.HBM) for v in (own, low, high, mate, far, *tables)])


BLOCK = 64
GROUP = 4


def grouped(width):
    return [
        pl.BlockSpec((BLOCK, width), lambda i, order, k=k: (order[i * GROUP + k], 0)) for k in range(GROUP)
    ]


def stacked(refs):
    return jnp.concatenate([r[...] for r in refs], axis=0)


def whole(shape):
    return pl.BlockSpec(shape, lambda i, order: (0,) * len(shape))


def out_kernel(order_ref, *refs):
    act, (logit_ref, part_ref) = refs[:GROUP], refs[GROUP:]
    part_ref[...] = jnp.dot(stacked(act), logit_ref[...], preferred_element_type=F32).astype(BF16)


def in_kernel(order_ref, *refs):
    slope, w_out = refs[:GROUP], refs[GROUP : 2 * GROUP]
    logit_ref, feats_ref, part_ref, grad_ref = refs[2 * GROUP :]
    hidden = lax.dot_general(
        stacked(w_out), logit_ref[...], (((1,), (1,)), ((), ())), preferred_element_type=F32
    )
    grad = (hidden * stacked(slope)).astype(BF16)
    grad_ref[...] = grad
    f_in = feats_ref.shape[1]
    part_ref[:, :f_in] = jnp.dot(grad, feats_ref[...], preferred_element_type=F32).astype(BF16)
    bias = jnp.sum(grad.astype(F32), axis=1, keepdims=True)
    part_ref[:, f_in:] = jnp.broadcast_to(bias, (bias.shape[0], TILE)).astype(BF16)


def feat_kernel(order_ref, *refs):
    w_in = refs[:GROUP]
    kept_ref, sent_ref, img_ref, cap_ref, acc_ref = refs[GROUP:]
    i = pl.program_id(0)
    steps = pl.num_programs(0)

    @pl.when(i == 0)
    def _():
        acc_ref[...] = jnp.zeros_like(acc_ref)

    grad = jnp.where(i < steps // 2, kept_ref[...], sent_ref[...])
    acc_ref[...] += lax.dot_general(
        grad, stacked(w_in), (((0,), (0,)), ((), ())), preferred_element_type=F32
    )

    @pl.when(i == steps - 1)
    def _():
        half = img_ref.shape[0]
        img_ref[...] = acc_ref[:half].astype(BF16)
        cap_ref[...] = acc_ref[half:].astype(BF16)


def over_hidden(kernel, name, order, in_specs, out_specs, out_shape, scratch, args):
    return pl.pallas_call(
        kernel,
        out_shape=out_shape,
        grid_spec=pltpu.PrefetchScalarGridSpec(
            num_scalar_prefetch=1,
            grid=(order.shape[0] // GROUP,),
            in_specs=in_specs,
            out_specs=out_specs,
            scratch_shapes=scratch,
        ),
        compiler_params=pltpu.CompilerParams(
            dimension_semantics=("arbitrary",), vmem_limit_bytes=28 << 20
        ),
        cost_estimate=SHORT,
        name=name,
    )(order, *args)


def rows_of_half(width, half, side):
    steps = half // GROUP
    if side:
        return pl.BlockSpec((GROUP * BLOCK, width), lambda i, order: (jnp.maximum(i - steps, 0), 0))
    return pl.BlockSpec((GROUP * BLOCK, width), lambda i, order: (jnp.minimum(i, steps - 1), 0))


def rows_of(width):
    return pl.BlockSpec((GROUP * BLOCK, width), lambda i, order: (i, 0))


def stack_kernel(count_ref, top_ref, bottom_ref, seed_ref, cols_ref, out_ref, meta_ref):
    half = top_ref.shape[0]
    out_ref[:half] = top_ref[...]
    out_ref[half:] = bottom_ref[...]
    tiles, slots = seed_ref.shape
    meta_ref[:, :slots] = seed_ref[...]
    meta_ref[:, slots : 2 * slots] = cols_ref[...]
    row = lax.broadcasted_iota(jnp.int32, (tiles, slots), 0)
    live = jnp.zeros((tiles, slots), jnp.int32)
    for t in range(tiles):
        live = jnp.where(row == t, count_ref[t], live)
    meta_ref[:, 2 * slots :] = live


def stack(top, bottom, seed, cols, counts):
    vmem = pl.BlockSpec(memory_space=pltpu.VMEM)
    shape = (2 * top.shape[0], top.shape[1])
    codes = (seed.shape[0], 3 * seed.shape[1])
    return pl.pallas_call(
        stack_kernel,
        out_shape=(pltpu.HBM(shape, top.dtype), jax.ShapeDtypeStruct(codes, jnp.int32)),
        in_specs=[pl.BlockSpec(memory_space=pltpu.SMEM)] + [vmem] * 4,
        out_specs=(pl.BlockSpec(shape, lambda: (0, 0)), pl.BlockSpec(codes, lambda: (0, 0))),
        cost_estimate=SHORT,
        name="stack",
    )(counts, top, bottom, seed, cols)


def after(value, *done):
    return lax.optimization_barrier((value,) + done)[0]


def moved(array, count, by):
    return lax.ppermute(array, AXES, [(i, i + by) for i in range(count) if 0 <= i + by < count])


def flipped(array, count, mask):
    return lax.ppermute(array, AXES, [(i, i ^ mask) for i in range(count)])


def added(kept, came):
    return (kept.astype(F32) + came.astype(F32)).astype(BF16)


def parts(array, axis):
    return lax.index_in_dim(array, 0, axis, keepdims=False), lax.index_in_dim(array, 1, axis, keepdims=False)


def nearest_pair(count, by):
    return [(i, i + by) for i in range(0, count - by, 2)] + [(i, i - by) for i in range(by + 1, count, 2)]


class Reduction:

    def __init__(self, part, count, bits, first, orders, ends):
        self.count, self.parts, self.left = count, [part], [list(bits)]
        self.steps = [(bit,) for bit in first] + list(zip(*orders)) + [(bit,) for bit in ends]

    def start(self):
        step = self.steps.pop(0)
        if len(step) > len(self.parts):
            part = self.parts[0]
            cut = part.shape[-2] // 2
            self.parts = [part[..., :cut, :], part[..., cut:, :]]
            self.left = [list(self.left[0]), list(self.left[0])]
        elif len(step) < len(self.parts):
            self.parts = [jnp.concatenate(self.parts, axis=-2)]
        self.kept, self.sent, self.came = [], [], []
        for part, left, bit in zip(self.parts, self.left, step):
            kept, sent = parts(part, left.index(bit))
            left.remove(bit)
            self.kept.append(kept)
            self.sent.append(sent)
            self.came.append(flipped(sent, self.count, 1 << bit))

    def finish(self, *done):
        self.parts = [added(after(k, *done), c) for k, c in zip(self.kept, self.came)]

    def result(self):
        return self.kept[0].astype(F32) + self.came[0].astype(F32)


def per_device(
    feats_img, feats_cap, cot_img, cot_cap, w_in, b_in, w_out, tile_seed, tile_cols, tile_count
):
    local_rows = feats_img.shape[0]
    tiles = local_rows // TILE
    slots = tile_seed.shape[1]
    hid, f_in = w_in.shape
    n_img, n_cap = lax.axis_size("img"), lax.axis_size("cap")
    count = n_img * n_cap
    me = lax.axis_index(AXES)

    even = (me & 1) == 0
    block, meta = stack(cot_img, cot_cap, tile_seed, tile_cols, tile_count)
    other = flipped(meta, count, 1)
    third = lax.ppermute(
        meta, AXES, [(i, i + 3) for i in range(1, count - 3, 2)] + [(i, i - 3) for i in range(4, count, 2)]
    )
    block = after(block, other)
    mate = flipped(block, count, 1)
    low = moved(block, count, 2)
    high = moved(block, count, -2)
    far = lax.ppermute(mate, AXES, nearest_pair(count, 2))
    pair = jnp.where(even, jnp.concatenate([meta, other]), jnp.concatenate([other, meta]))
    feats = jnp.concatenate([feats_img, feats_cap], axis=0)
    pair, feats, third = lax.optimization_barrier((pair, after(feats, block), third))
    pair_low = moved(pair, count, 2)
    pair_high = moved(pair, count, -2)
    wide = jnp.where(
        even,
        jnp.concatenate([third, pair_low, pair, pair_high]),
        jnp.concatenate([pair_low, pair, pair_high, third]),
    )
    frame = jnp.arange(7 * tiles, dtype=jnp.int32)[:, None]
    counts = wide[:, 2 * slots]
    seeds = wide[:, :slots].reshape(-1)
    places = jnp.where(counts[:, None] > 0, wide[:, slots : 2 * slots] - (me - 3) * tiles, frame)
    pats = make_tiles(seeds, (places + tiles).reshape(-1), counts, tiles, slots)

    m = count.bit_length() - 1
    a = n_cap.bit_length() - 1
    cap_bits = list(range(a))
    img_bits = list(range(a + 1, m - 2))
    bits = [a] + cap_bits + img_bits + [m - 2, m - 1]
    pos = jnp.arange(count, dtype=jnp.int32)
    order = jnp.zeros_like(pos)
    for k, bit in enumerate(bits):
        order = order | (((pos >> (m - 1 - k)) & 1) << bit)
    order = order ^ me
    rows = hid // count
    if rows % BLOCK:
        w_in, w_out, b_in = [
            jnp.take(v.reshape((count, rows) + v.shape[1:]), order, axis=0).reshape(v.shape) for v in (w_in, w_out, b_in)
        ]
        order = jnp.arange(hid // BLOCK, dtype=jnp.int32)
    else:
        order = (order[:, None] * (rows // BLOCK) + jnp.arange(rows // BLOCK, dtype=jnp.int32)).reshape(-1)

    across = (((1,), (1,)), ((), ()))
    preact = lax.dot_general(w_in, feats, across, preferred_element_type=F32) + b_in[:, None]
    gelu_value, gelu_slope = gelu_parts(preact)
    hidden_act, gelu_slope = lax.optimization_barrier((gelu_value.astype(BF16), gelu_slope))

    bases = jnp.where(even, jnp.array([3, 1]), jnp.array([1, 3])).astype(jnp.int32) * tiles
    mid_places = (places - tiles)[tiles : 6 * tiles].reshape(-1)
    logit = propagate(mid_places, bases, block, low, high, mate, far, pats, tiles, slots)

    width = cot_img.shape[1]
    nodes = 2 * local_rows
    half = order.shape[0] // 2
    blocked = (2,) * (m - 1) + (rows,)

    def out_half(order, logit):
        return over_hidden(
            out_kernel, "part_out", order, grouped(nodes) + [whole(logit.shape)], rows_of(width),
            jax.ShapeDtypeStruct((hid // 2, width), BF16), [], [hidden_act] * GROUP + [logit],
        ).reshape(blocked + (width,))

    def in_half(order, logit):
        part, grad = over_hidden(
            in_kernel, "part_in", order,
            grouped(nodes) + grouped(width) + [whole(logit.shape), whole(feats.shape)],
            (rows_of(f_in + TILE), rows_of(nodes)),
            (jax.ShapeDtypeStruct((hid // 2, f_in + TILE), BF16), jax.ShapeDtypeStruct((hid // 2, nodes), BF16)),
            [], [gelu_slope] * GROUP + [w_out] * GROUP + [logit, feats],
        )
        return part.reshape(blocked + (f_in + TILE,)), grad

    core = 1 << a
    rest = bits[1:]
    orders = (cap_bits + img_bits, img_bits + cap_bits)
    near, last = m - 2, m - 1
    in_sent, grad_sent = in_half(order[half:], logit)
    in_came = flipped(in_sent, count, core)
    in_kept, grad_kept = in_half(order[:half], after(logit, grad_sent))
    r_in = Reduction(added(in_kept, in_came), count, rest, (), orders, (near, last))
    r_in.start()
    out_sent = out_half(order[half:], after(logit, *r_in.sent))
    out_came = flipped(out_sent, count, core)
    out_kept = out_half(order[:half], after(logit, out_sent))
    r_out = Reduction(added(out_kept, out_came), count, rest, (near,), orders, (last,))
    r_out.start()
    grad_img, grad_cap = over_hidden(
        feat_kernel, "feat_grad", order, grouped(f_in) + [rows_of_half(nodes, half, 0), rows_of_half(nodes, half, 1)],
        (whole((local_rows, f_in)),) * 2, (jax.ShapeDtypeStruct((local_rows, f_in), BF16),) * 2,
        [pltpu.VMEM((nodes, f_in), F32)], [w_in] * GROUP + [after(grad_kept, *r_out.sent), grad_sent],
    )
    done = (grad_img,)
    for _ in range(m - 2):
        r_in.finish(*done)
        r_in.start()
        r_out.finish(*r_in.sent)
        r_out.start()
        done = r_out.sent
    grad_scale = 1.0 / math.sqrt(nodes * count)
    g_out, g_in = [r.result() * grad_scale for r in (r_out, r_in)]
    return (grad_img, grad_cap, g_in[:, :f_in], g_out, g_in[:, f_in])


def solution(mesh):
    rows = P(("img", "cap"), None)
    in_specs = (rows, rows, rows, rows, P(), P(), P(), rows, rows, P(("img", "cap")))
    out_specs = (rows, rows, rows, rows, P(("img", "cap")))
    return jax.shard_map(
        per_device, mesh=mesh, in_specs=in_specs, out_specs=out_specs, check_vma=False
    )
```

```python
import math

import jax
import jax.numpy as jnp
from jax import lax
from jax.experimental import pallas as pl
from jax.experimental.pallas import tpu as pltpu
from jax.sharding import PartitionSpec as P

TILE = 128
ALPHA = 0.1
SHORT = pl.CostEstimate(flops=1, transcendentals=0, bytes_accessed=1)
AXES = ("img", "cap")
F32 = jnp.float32
BF16 = jnp.bfloat16


def gelu_parts(preact):
    normal_cdf = 0.5 * (1.0 + jax.scipy.special.erf(preact * 0.7071067811865476))
    normal_pdf = jnp.exp(-0.5 * preact * preact) * 0.3989422804014327
    return (preact * normal_cdf, normal_cdf + preact * normal_pdf)


def tiles_kernel(seed_ref, place_ref, count_ref, *refs, tiles, slots):
    outs, (pat_ref, pat_t_ref, nimg_ref, ncap_ref, deg_ref, sems) = refs[:4], refs[4:]
    all_tiles, mid = 7 * tiles, 5 * tiles
    deg_ref[...] = jnp.zeros_like(deg_ref)
    row = lax.broadcasted_iota(jnp.int32, (TILE, TILE), 0)
    col = lax.broadcasted_iota(jnp.int32, (TILE, TILE), 1)
    first, second = jnp.int32(668265261), jnp.int32(374761393)
    base = (row * 40503 + col * 9973) * first
    base_t = (col * 40503 + row * 9973) * first
    off_diag = row - col

    def pattern(start, seed, live, s):
        mixed = start + seed * first
        mixed = jnp.bitwise_xor(mixed, jnp.right_shift(mixed, 15))
        mixed = mixed * second
        mixed = jnp.bitwise_xor(mixed, jnp.right_shift(mixed, 13))
        edge = jnp.bitwise_and(mixed, 15) == jnp.where(live, 0, 16)
        if s == 0:
            edge = edge | (off_diag == jnp.where(live, 0, TILE))
        return jnp.where(edge, 1.0, 0.0)

    def one(q, full):
        total = None
        for s in range(slots):
            live = s < count_ref[q]
            seed = seed_ref[q * slots + s]
            e = pattern(base, seed, live, s)
            c = place_ref[q * slots + s]
            deg_ref[c] += jnp.sum(e, axis=0, keepdims=True)
            if full:
                m = q - tiles
                pat_ref[m, :, pl.ds(s * TILE, TILE)] = e.astype(BF16)
                pat_t_ref[m, pl.ds(s * TILE, TILE), :] = pattern(base_t, seed, live, s).astype(BF16)
                total = e if total is None else total + e
        if full:
            d = jnp.sum(total, axis=1, keepdims=True)
            n = jnp.where(d > 0.0, lax.rsqrt(d), 0.0)
            nimg_ref[q - tiles] = jnp.broadcast_to(n, (TILE, TILE))

    def edge_body(q, c):
        one(q, False)
        return c

    def mid_body(q, c):
        one(q, True)
        return c

    lax.fori_loop(0, tiles, edge_body, 0)
    lax.fori_loop(tiles, tiles + mid, mid_body, 0)
    copies = [
        pltpu.make_async_copy(src, dst, sems.at[k])
        for k, (src, dst) in enumerate(zip((pat_ref, pat_t_ref, nimg_ref, ncap_ref), outs))
    ]
    for copy in copies[:3]:
        copy.start()
    lax.fori_loop(tiles + mid, all_tiles, edge_body, 0)
    for m in range(mid):
        d = deg_ref[m + 2 * tiles]
        n = jnp.where(d > 0.0, lax.rsqrt(d), 0.0)
        ncap_ref[m] = jnp.broadcast_to(n, (TILE, TILE)).T
    copies[3].start()
    for copy in copies:
        copy.wait()


def table_shapes(tiles, slots):
    mid = 5 * tiles
    return (
        ((mid, TILE, slots * TILE), BF16),
        ((mid, slots * TILE, TILE), BF16),
        ((mid, TILE, TILE), F32),
        ((mid, TILE, TILE), F32),
    )


def make_tiles(seeds, places, counts, tiles, slots):
    smem = pl.BlockSpec(memory_space=pltpu.SMEM)
    hbm = pl.BlockSpec(memory_space=pltpu.HBM)
    tables = table_shapes(tiles, slots)
    return pl.pallas_call(
        lambda *r: tiles_kernel(*r, tiles=tiles, slots=slots),
        out_shape=tuple(pltpu.HBM(*t) for t in tables),
        in_specs=[smem] * 3,
        out_specs=(hbm,) * 4,
        scratch_shapes=[pltpu.VMEM(*t) for t in tables]
        + [pltpu.VMEM((9 * tiles, 1, TILE), F32), pltpu.SemaphoreType.DMA((4,))],
        compiler_params=pltpu.CompilerParams(vmem_limit_bytes=16 << 20),
        cost_estimate=SHORT,
        name="tiles",
    )(seeds, places, counts)


def hops_kernel(
    place_ref, base_ref, own_hbm, low_hbm, high_hbm, mate_hbm, far_hbm, pat_hbm, pat_t_hbm, nimg_hbm, ncap_hbm,
    out_ref, bands, pat_ref, pat_t_ref, nimg_ref, ncap_ref, img0, cap0, img1, cap1, acc, acc2, keep_img, keep_cap,
    sems, *, tiles, slots, width,
):
    mid = 5 * tiles
    near = 3 * tiles
    keep = 1.0 - ALPHA
    sources = (own_hbm, nimg_hbm, ncap_hbm, pat_t_hbm, low_hbm, high_hbm, mate_hbm, far_hbm, pat_hbm)
    targets = (bands.at[0], nimg_ref, ncap_ref, pat_t_ref) + tuple(bands.at[k] for k in range(1, 5)) + (pat_ref,)
    copies = [pltpu.make_async_copy(s, t, sems.at[k]) for k, (s, t) in enumerate(zip(sources, targets))]
    for copy in copies:
        copy.start()

    def wide(n_ref, m):
        n = n_ref[m]
        return jnp.concatenate([n] * (width // TILE), axis=1)

    def scale(k, base):
        for t in range(tiles):
            m = base + t
            img0[m] = (bands[k, pl.ds(t * TILE, TILE), :].astype(F32) * wide(nimg_ref, m)).astype(BF16)
            cap0[m] = (bands[k, pl.ds((tiles + t) * TILE, TILE), :].astype(F32) * wide(ncap_ref, m)).astype(BF16)

    acc[...] = jnp.zeros_like(acc)
    acc2[...] = jnp.zeros_like(acc2)

    def push(q, state, target, lo, count):
        r = jnp.dot(pat_t_ref[q], state, preferred_element_type=F32)
        for s in range(slots):
            c = place_ref[q * slots + s] - lo
            c = jnp.where((c >= 0) & (c < count), c, count)
            target[c] += r[s * TILE : (s + 1) * TILE]

    def pull(q, source, lo):
        total = None
        for s in range(slots):
            c = place_ref[q * slots + s] - lo
            r = jnp.dot(pat_ref[q, :, pl.ds(s * TILE, TILE)], source[c], preferred_element_type=F32)
            total = r if total is None else total + r
        return total

    for copy in copies[:4]:
        copy.wait()
    for k, base in enumerate((2 * tiles, 0, 4 * tiles, base_ref[0], base_ref[1])):
        if k:
            copies[3 + k].wait()
        scale(k, base)
        for t in range(tiles):
            push(base + t, img0[base + t], acc, tiles, near)
    copies[8].wait()

    def pull1(q, c):
        n = wide(nimg_ref, q)
        flow = keep * n * pull(q, cap0, 0)
        img1[q - tiles] = (flow * n).astype(BF16)
        keep_img[q - tiles] = flow
        return c

    lax.fori_loop(tiles, tiles + near, pull1, 0, unroll=9)

    def finish1(m, c):
        n = wide(ncap_ref, m + tiles)
        flow = keep * n * acc[m]
        cap1[m] = (flow * n).astype(BF16)
        keep_cap[m] = flow
        return c

    lax.fori_loop(0, near, finish1, 0, unroll=3)

    def push2(q, c):
        push(q, img1[q - tiles], acc2, 2 * tiles, tiles)
        return c

    lax.fori_loop(tiles, tiles + near, push2, 0, unroll=3)
    for t in range(tiles):
        q = 2 * tiles + t
        rows = pl.ds(t * TILE, TILE)
        flow = keep * wide(nimg_ref, q) * pull(q, cap1, tiles)
        out_ref[rows, :] = (ALPHA * (bands[0, rows, :].astype(F32) + keep_img[tiles + t]) + flow).astype(BF16)
        flow = keep * wide(ncap_ref, q) * acc2[t]
        rows = pl.ds((tiles + t) * TILE, TILE)
        out_ref[rows, :] = (ALPHA * (bands[0, rows, :].astype(F32) + keep_cap[tiles + t]) + flow).astype(BF16)


def propagate(places, bases, own, low, high, mate, far, tables, tiles, slots):
    width = own.shape[1]
    smem = pl.BlockSpec(memory_space=pltpu.SMEM)
    vmem = pl.BlockSpec(memory_space=pltpu.VMEM)
    hbm = pl.BlockSpec(memory_space=pltpu.HBM)
    mid, near = 5 * tiles, 3 * tiles
    return pl.pallas_call(
        lambda *r: hops_kernel(*r, tiles=tiles, slots=slots, width=width),
        out_shape=jax.ShapeDtypeStruct(own.shape, BF16),
        in_specs=[smem] * 2 + [hbm] * 9,
        out_specs=vmem,
        scratch_shapes=[
            pltpu.VMEM((5,) + own.shape, BF16),
            *[pltpu.VMEM(*t) for t in table_shapes(tiles, slots)],
            pltpu.VMEM((mid, TILE, width), BF16),
            pltpu.VMEM((mid, TILE, width), BF16),
            pltpu.VMEM((near, TILE, width), BF16),
            pltpu.VMEM((near, TILE, width), BF16),
            pltpu.VMEM((near + 1, TILE, width), F32),
            pltpu.VMEM((tiles + 1, TILE, width), F32),
            pltpu.VMEM((near, TILE, width), F32),
            pltpu.VMEM((near, TILE, width), F32),
            pltpu.SemaphoreType.DMA((9,)),
        ],
        compiler_params=pltpu.CompilerParams(vmem_limit_bytes=34 << 20),
        cost_estimate=SHORT,
        name="hops",
    )(places, bases, *[pltpu.with_memory_space_constraint(v, pltpu.HBM) for v in (own, low, high, mate, far, *tables)])


BLOCK = 64
GROUP = 4


def grouped(width):
    return [
        pl.BlockSpec((BLOCK, width), lambda i, order, k=k: (order[i * GROUP + k], 0)) for k in range(GROUP)
    ]


def stacked(refs):
    return jnp.concatenate([r[...] for r in refs], axis=0)


def whole(shape):
    return pl.BlockSpec(shape, lambda i, order: (0,) * len(shape))


def out_kernel(order_ref, *refs):
    act, (logit_ref, part_ref) = refs[:GROUP], refs[GROUP:]
    part_ref[...] = jnp.dot(stacked(act), logit_ref[...], preferred_element_type=F32).astype(BF16)


def in_kernel(order_ref, *refs):
    slope, w_out = refs[:GROUP], refs[GROUP : 2 * GROUP]
    logit_ref, feats_ref, part_ref, grad_ref = refs[2 * GROUP :]
    hidden = lax.dot_general(
        stacked(w_out), logit_ref[...], (((1,), (1,)), ((), ())), preferred_element_type=F32
    )
    grad = (hidden * stacked(slope)).astype(BF16)
    grad_ref[...] = grad
    f_in = feats_ref.shape[1]
    part_ref[:, :f_in] = jnp.dot(grad, feats_ref[...], preferred_element_type=F32).astype(BF16)
    bias = jnp.sum(grad.astype(F32), axis=1, keepdims=True)
    part_ref[:, f_in:] = jnp.broadcast_to(bias, (bias.shape[0], TILE)).astype(BF16)


def feat_kernel(order_ref, *refs):
    w_in = refs[:GROUP]
    kept_ref, sent_ref, img_ref, cap_ref, acc_ref = refs[GROUP:]
    i = pl.program_id(0)
    steps = pl.num_programs(0)

    @pl.when(i == 0)
    def _():
        acc_ref[...] = jnp.zeros_like(acc_ref)

    grad = jnp.where(i < steps // 2, kept_ref[...], sent_ref[...])
    acc_ref[...] += lax.dot_general(
        grad, stacked(w_in), (((0,), (0,)), ((), ())), preferred_element_type=F32
    )

    @pl.when(i == steps - 1)
    def _():
        half = img_ref.shape[0]
        img_ref[...] = acc_ref[:half].astype(BF16)
        cap_ref[...] = acc_ref[half:].astype(BF16)


def over_hidden(kernel, name, order, in_specs, out_specs, out_shape, scratch, args):
    return pl.pallas_call(
        kernel,
        out_shape=out_shape,
        grid_spec=pltpu.PrefetchScalarGridSpec(
            num_scalar_prefetch=1,
            grid=(order.shape[0] // GROUP,),
            in_specs=in_specs,
            out_specs=out_specs,
            scratch_shapes=scratch,
        ),
        compiler_params=pltpu.CompilerParams(
            dimension_semantics=("arbitrary",), vmem_limit_bytes=28 << 20
        ),
        cost_estimate=SHORT,
        name=name,
    )(order, *args)


def rows_of_half(width, half, side):
    steps = half // GROUP
    if side:
        return pl.BlockSpec((GROUP * BLOCK, width), lambda i, order: (jnp.maximum(i - steps, 0), 0))
    return pl.BlockSpec((GROUP * BLOCK, width), lambda i, order: (jnp.minimum(i, steps - 1), 0))


def rows_of(width):
    return pl.BlockSpec((GROUP * BLOCK, width), lambda i, order: (i, 0))


def stack_kernel(count_ref, top_ref, bottom_ref, seed_ref, cols_ref, out_ref, meta_ref):
    half = top_ref.shape[0]
    out_ref[:half] = top_ref[...]
    out_ref[half:] = bottom_ref[...]
    tiles, slots = seed_ref.shape
    meta_ref[:, :slots] = seed_ref[...]
    meta_ref[:, slots : 2 * slots] = cols_ref[...]
    row = lax.broadcasted_iota(jnp.int32, (tiles, slots), 0)
    live = jnp.zeros((tiles, slots), jnp.int32)
    for t in range(tiles):
        live = jnp.where(row == t, count_ref[t], live)
    meta_ref[:, 2 * slots :] = live


def stack(top, bottom, seed, cols, counts):
    vmem = pl.BlockSpec(memory_space=pltpu.VMEM)
    shape = (2 * top.shape[0], top.shape[1])
    codes = (seed.shape[0], 3 * seed.shape[1])
    return pl.pallas_call(
        stack_kernel,
        out_shape=(pltpu.HBM(shape, top.dtype), jax.ShapeDtypeStruct(codes, jnp.int32)),
        in_specs=[pl.BlockSpec(memory_space=pltpu.SMEM)] + [vmem] * 4,
        out_specs=(pl.BlockSpec(shape, lambda: (0, 0)), pl.BlockSpec(codes, lambda: (0, 0))),
        cost_estimate=SHORT,
        name="stack",
    )(counts, top, bottom, seed, cols)


def after(value, *done):
    return lax.optimization_barrier((value,) + done)[0]


def moved(array, count, by):
    return lax.ppermute(array, AXES, [(i, i + by) for i in range(count) if 0 <= i + by < count])


def flipped(array, count, mask):
    return lax.ppermute(array, AXES, [(i, i ^ mask) for i in range(count)])


def added(kept, came):
    return (kept.astype(F32) + came.astype(F32)).astype(BF16)


def parts(array, axis):
    return lax.index_in_dim(array, 0, axis, keepdims=False), lax.index_in_dim(array, 1, axis, keepdims=False)


def nearest_pair(count, by):
    return [(i, i + by) for i in range(0, count - by, 2)] + [(i, i - by) for i in range(by + 1, count, 2)]


class Reduction:

    def __init__(self, part, count, bits, first, orders, ends):
        self.count, self.parts, self.left = count, [part], [list(bits)]
        self.steps = [(bit,) for bit in first] + list(zip(*orders)) + [(bit,) for bit in ends]

    def start(self):
        step = self.steps.pop(0)
        if len(step) > len(self.parts):
            part = self.parts[0]
            cut = part.shape[-2] // 2
            self.parts = [part[..., :cut, :], part[..., cut:, :]]
            self.left = [list(self.left[0]), list(self.left[0])]
        elif len(step) < len(self.parts):
            self.parts = [jnp.concatenate(self.parts, axis=-2)]
        self.kept, self.sent, self.came = [], [], []
        for part, left, bit in zip(self.parts, self.left, step):
            kept, sent = parts(part, left.index(bit))
            left.remove(bit)
            self.kept.append(kept)
            self.sent.append(sent)
            self.came.append(flipped(sent, self.count, 1 << bit))

    def finish(self, *done):
        self.parts = [added(after(k, *done), c) for k, c in zip(self.kept, self.came)]

    def result(self, lanes):
        return self.kept[0][:, lanes].astype(F32) + self.came[0][:, lanes].astype(F32)


def per_device(
    feats_img, feats_cap, cot_img, cot_cap, w_in, b_in, w_out, tile_seed, tile_cols, tile_count
):
    local_rows = feats_img.shape[0]
    tiles = local_rows // TILE
    slots = tile_seed.shape[1]
    hid, f_in = w_in.shape
    n_img, n_cap = lax.axis_size("img"), lax.axis_size("cap")
    count = n_img * n_cap
    me = lax.axis_index(AXES)

    even = (me & 1) == 0
    block, meta = stack(cot_img, cot_cap, tile_seed, tile_cols, tile_count)
    other = flipped(meta, count, 1)
    third = lax.ppermute(
        meta, AXES, [(i, i + 3) for i in range(1, count - 3, 2)] + [(i, i - 3) for i in range(4, count, 2)]
    )
    block = after(block, other)
    mate = flipped(block, count, 1)
    low = moved(block, count, 2)
    high = moved(block, count, -2)
    far = lax.ppermute(mate, AXES, nearest_pair(count, 2))
    pair = jnp.where(even, jnp.concatenate([meta, other]), jnp.concatenate([other, meta]))
    feats = jnp.concatenate([after(feats_img, block), feats_cap], axis=0)
    pair, feats, third = lax.optimization_barrier((pair, feats, third))
    pair_low = moved(pair, count, 2)
    pair_high = moved(pair, count, -2)
    wide = jnp.where(
        even,
        jnp.concatenate([third, pair_low, pair, pair_high]),
        jnp.concatenate([pair_low, pair, pair_high, third]),
    )
    frame = jnp.arange(7 * tiles, dtype=jnp.int32)[:, None]
    counts = wide[:, 2 * slots]
    seeds = wide[:, :slots].reshape(-1)
    places = jnp.where(counts[:, None] > 0, wide[:, slots : 2 * slots] - (me - 3) * tiles, frame)
    pats = make_tiles(seeds, (places + tiles).reshape(-1), counts, tiles, slots)

    m = count.bit_length() - 1
    a = n_cap.bit_length() - 1
    cap_bits = list(range(a))
    img_bits = list(range(a + 1, m - 2))
    bits = [a] + cap_bits + img_bits + [m - 2, m - 1]
    pos = jnp.arange(count, dtype=jnp.int32)
    order = jnp.zeros_like(pos)
    for k, bit in enumerate(bits):
        order = order | (((pos >> (m - 1 - k)) & 1) << bit)
    order = order ^ me
    rows = hid // count
    if rows % BLOCK:
        w_in, w_out, b_in = [
            jnp.take(v.reshape((count, rows) + v.shape[1:]), order, axis=0).reshape(v.shape) for v in (w_in, w_out, b_in)
        ]
        order = jnp.arange(hid // BLOCK, dtype=jnp.int32)
    else:
        order = (order[:, None] * (rows // BLOCK) + jnp.arange(rows // BLOCK, dtype=jnp.int32)).reshape(-1)

    across = (((1,), (1,)), ((), ()))
    preact = lax.dot_general(w_in, feats, across, preferred_element_type=F32) + b_in[:, None]
    gelu_value, gelu_slope = gelu_parts(preact)
    hidden_act, gelu_slope = lax.optimization_barrier((gelu_value.astype(BF16), gelu_slope))

    bases = jnp.where(even, jnp.array([3, 1]), jnp.array([1, 3])).astype(jnp.int32) * tiles
    mid_places = (places - tiles)[tiles : 6 * tiles].reshape(-1)
    logit = propagate(mid_places, bases, block, low, high, mate, far, pats, tiles, slots)

    width = cot_img.shape[1]
    nodes = 2 * local_rows
    half = order.shape[0] // 2
    blocked = (2,) * (m - 1) + (rows,)

    def out_half(order, logit):
        return over_hidden(
            out_kernel, "part_out", order, grouped(nodes) + [whole(logit.shape)], rows_of(width),
            jax.ShapeDtypeStruct((hid // 2, width), BF16), [], [hidden_act] * GROUP + [logit],
        ).reshape(blocked + (width,))

    def in_half(order, logit):
        part, grad = over_hidden(
            in_kernel, "part_in", order,
            grouped(nodes) + grouped(width) + [whole(logit.shape), whole(feats.shape)],
            (rows_of(f_in + TILE), rows_of(nodes)),
            (jax.ShapeDtypeStruct((hid // 2, f_in + TILE), BF16), jax.ShapeDtypeStruct((hid // 2, nodes), BF16)),
            [], [gelu_slope] * GROUP + [w_out] * GROUP + [logit, feats],
        )
        return part.reshape(blocked + (f_in + TILE,)), grad

    core = 1 << a
    rest = bits[1:]
    orders = (cap_bits + img_bits, img_bits + cap_bits)
    near, last = m - 2, m - 1
    in_sent, grad_sent = in_half(order[half:], logit)
    in_came = flipped(in_sent, count, core)
    in_kept, grad_kept = in_half(order[:half], after(logit, grad_sent))
    r_in = Reduction(added(in_kept, in_came), count, rest, (), orders, (near, last))
    r_in.start()
    out_sent = out_half(order[half:], after(logit, *r_in.sent))
    out_came = flipped(out_sent, count, core)
    out_kept = out_half(order[:half], after(logit, out_sent))
    r_out = Reduction(added(out_kept, out_came), count, rest, (near,), orders, (last,))
    r_out.start()
    grad_img, grad_cap = over_hidden(
        feat_kernel, "feat_grad", order, grouped(f_in) + [rows_of_half(nodes, half, 0), rows_of_half(nodes, half, 1)],
        (whole((local_rows, f_in)),) * 2, (jax.ShapeDtypeStruct((local_rows, f_in), BF16),) * 2,
        [pltpu.VMEM((nodes, f_in), F32)], [w_in] * GROUP + [after(grad_kept, *r_out.sent), grad_sent],
    )
    done = (grad_img,)
    for _ in range(m - 2):
        r_in.finish(*done)
        r_in.start()
        r_out.finish(*r_in.sent)
        r_out.start()
        done = r_out.sent
    grad_scale = 1.0 / math.sqrt(nodes * count)
    g_out = r_out.result(slice(None)) * grad_scale
    g_in = r_in.result(slice(0, f_in)) * grad_scale
    g_bias = r_in.result(f_in) * grad_scale
    return (grad_img, grad_cap, g_in, g_out, g_bias)


def solution(mesh):
    rows = P(("img", "cap"), None)
    in_specs = (rows, rows, rows, rows, P(), P(), P(), rows, rows, P(("img", "cap")))
    out_specs = (rows, rows, rows, rows, P(("img", "cap")))
    return jax.shard_map(
        per_device, mesh=mesh, in_specs=in_specs, out_specs=out_specs, check_vma=False
    )
```

```python
import math

import jax
import jax.numpy as jnp
from jax import lax
from jax.experimental import pallas as pl
from jax.experimental.pallas import tpu as pltpu
from jax.sharding import PartitionSpec as P

TILE = 128
ALPHA = 0.1
SHORT = pl.CostEstimate(flops=1, transcendentals=0, bytes_accessed=1)
AXES = ("img", "cap")
F32 = jnp.float32
BF16 = jnp.bfloat16


def gelu_parts(preact):
    normal_cdf = 0.5 * (1.0 + jax.scipy.special.erf(preact * 0.7071067811865476))
    normal_pdf = jnp.exp(-0.5 * preact * preact) * 0.3989422804014327
    return (preact * normal_cdf, normal_cdf + preact * normal_pdf)


def tiles_kernel(seed_ref, place_ref, count_ref, *refs, tiles, slots):
    outs, (pat_ref, pat_t_ref, nimg_ref, ncap_ref, deg_ref, sems) = refs[:4], refs[4:]
    all_tiles, mid = 7 * tiles, 5 * tiles
    deg_ref[...] = jnp.zeros_like(deg_ref)
    row = lax.broadcasted_iota(jnp.int32, (TILE, TILE), 0)
    col = lax.broadcasted_iota(jnp.int32, (TILE, TILE), 1)
    first, second = jnp.int32(668265261), jnp.int32(374761393)
    base = (row * 40503 + col * 9973) * first
    base_t = (col * 40503 + row * 9973) * first
    off_diag = row - col

    def pattern(start, seed, live, s):
        mixed = start + seed * first
        mixed = jnp.bitwise_xor(mixed, jnp.right_shift(mixed, 15))
        mixed = mixed * second
        mixed = jnp.bitwise_xor(mixed, jnp.right_shift(mixed, 13))
        edge = jnp.bitwise_and(mixed, 15) == jnp.where(live, 0, 16)
        if s == 0:
            edge = edge | (off_diag == jnp.where(live, 0, TILE))
        return jnp.where(edge, 1.0, 0.0)

    def one(q, full):
        total = None
        for s in range(slots):
            live = s < count_ref[q]
            seed = seed_ref[q * slots + s]
            e = pattern(base, seed, live, s)
            c = place_ref[q * slots + s]
            deg_ref[c] += jnp.sum(e, axis=0, keepdims=True)
            if full:
                m = q - tiles
                pat_ref[m, :, pl.ds(s * TILE, TILE)] = e.astype(BF16)
                pat_t_ref[m, pl.ds(s * TILE, TILE), :] = pattern(base_t, seed, live, s).astype(BF16)
                total = e if total is None else total + e
        if full:
            d = jnp.sum(total, axis=1, keepdims=True)
            n = jnp.where(d > 0.0, lax.rsqrt(d), 0.0)
            nimg_ref[q - tiles] = jnp.broadcast_to(n, (TILE, TILE))

    def edge_body(q, c):
        one(q, False)
        return c

    def mid_body(q, c):
        one(q, True)
        return c

    lax.fori_loop(0, tiles, edge_body, 0)
    lax.fori_loop(tiles, tiles + mid, mid_body, 0)
    copies = [
        pltpu.make_async_copy(src, dst, sems.at[k])
        for k, (src, dst) in enumerate(zip((pat_ref, pat_t_ref, nimg_ref, ncap_ref), outs))
    ]
    for copy in copies[:3]:
        copy.start()
    lax.fori_loop(tiles + mid, all_tiles, edge_body, 0)
    for m in range(mid):
        d = deg_ref[m + 2 * tiles]
        n = jnp.where(d > 0.0, lax.rsqrt(d), 0.0)
        ncap_ref[m] = jnp.broadcast_to(n, (TILE, TILE)).T
    copies[3].start()
    for copy in copies:
        copy.wait()


def table_shapes(tiles, slots):
    mid = 5 * tiles
    return (
        ((mid, TILE, slots * TILE), BF16),
        ((mid, slots * TILE, TILE), BF16),
        ((mid, TILE, TILE), F32),
        ((mid, TILE, TILE), F32),
    )


def make_tiles(seeds, places, counts, tiles, slots):
    smem = pl.BlockSpec(memory_space=pltpu.SMEM)
    hbm = pl.BlockSpec(memory_space=pltpu.HBM)
    tables = table_shapes(tiles, slots)
    return pl.pallas_call(
        lambda *r: tiles_kernel(*r, tiles=tiles, slots=slots),
        out_shape=tuple(pltpu.HBM(*t) for t in tables),
        in_specs=[smem] * 3,
        out_specs=(hbm,) * 4,
        scratch_shapes=[pltpu.VMEM(*t) for t in tables]
        + [pltpu.VMEM((9 * tiles, 1, TILE), F32), pltpu.SemaphoreType.DMA((4,))],
        compiler_params=pltpu.CompilerParams(vmem_limit_bytes=16 << 20),
        cost_estimate=SHORT,
        name="tiles",
    )(seeds, places, counts)


def hops_kernel(
    place_ref, base_ref, own_hbm, low_hbm, high_hbm, mate_img, mate_cap, far_img, far_cap, pat_hbm, pat_t_hbm, nimg_hbm, ncap_hbm,
    out_ref, bands, pat_ref, pat_t_ref, nimg_ref, ncap_ref, img0, cap0, img1, cap1, acc, acc2, keep_img, keep_cap,
    sems, *, tiles, slots, width,
):
    mid = 5 * tiles
    near = 3 * tiles
    keep = 1.0 - ALPHA
    rows = tiles * TILE
    upper, lower = pl.ds(0, rows), pl.ds(rows, rows)
    pairs = (
        (own_hbm, bands.at[0]), (nimg_hbm, nimg_ref), (ncap_hbm, ncap_ref), (pat_t_hbm, pat_t_ref),
        (low_hbm, bands.at[1]), (high_hbm, bands.at[2]),
        (mate_img, bands.at[3, upper]), (mate_cap, bands.at[3, lower]),
        (far_img, bands.at[4, upper]), (far_cap, bands.at[4, lower]), (pat_hbm, pat_ref),
    )
    copies = [pltpu.make_async_copy(s, t, sems.at[k]) for k, (s, t) in enumerate(pairs)]
    for copy in copies:
        copy.start()

    def wide(n_ref, m):
        n = n_ref[m]
        return jnp.concatenate([n] * (width // TILE), axis=1)

    def scale(k, base):
        for t in range(tiles):
            m = base + t
            img0[m] = (bands[k, pl.ds(t * TILE, TILE), :].astype(F32) * wide(nimg_ref, m)).astype(BF16)
            cap0[m] = (bands[k, pl.ds((tiles + t) * TILE, TILE), :].astype(F32) * wide(ncap_ref, m)).astype(BF16)

    acc[...] = jnp.zeros_like(acc)
    acc2[...] = jnp.zeros_like(acc2)

    def push(q, state, target, lo, count):
        r = jnp.dot(pat_t_ref[q], state, preferred_element_type=F32)
        for s in range(slots):
            c = place_ref[q * slots + s] - lo
            c = jnp.where((c >= 0) & (c < count), c, count)
            target[c] += r[s * TILE : (s + 1) * TILE]

    def pull(q, source, lo):
        total = None
        for s in range(slots):
            c = place_ref[q * slots + s] - lo
            r = jnp.dot(pat_ref[q, :, pl.ds(s * TILE, TILE)], source[c], preferred_element_type=F32)
            total = r if total is None else total + r
        return total

    for copy in copies[:4]:
        copy.wait()
    for k, base in enumerate((2 * tiles, 0, 4 * tiles, base_ref[0], base_ref[1])):
        for copy in ((), copies[4:5], copies[5:6], copies[6:8], copies[8:10])[k]:
            copy.wait()
        scale(k, base)
        for t in range(tiles):
            push(base + t, img0[base + t], acc, tiles, near)
    copies[10].wait()

    def pull1(q, c):
        n = wide(nimg_ref, q)
        flow = keep * n * pull(q, cap0, 0)
        img1[q - tiles] = (flow * n).astype(BF16)
        keep_img[q - tiles] = flow
        return c

    lax.fori_loop(tiles, tiles + near, pull1, 0, unroll=9)

    def finish1(m, c):
        n = wide(ncap_ref, m + tiles)
        flow = keep * n * acc[m]
        cap1[m] = (flow * n).astype(BF16)
        keep_cap[m] = flow
        return c

    lax.fori_loop(0, near, finish1, 0, unroll=3)

    def push2(q, c):
        push(q, img1[q - tiles], acc2, 2 * tiles, tiles)
        return c

    lax.fori_loop(tiles, tiles + near, push2, 0, unroll=3)
    for t in range(tiles):
        q = 2 * tiles + t
        rows = pl.ds(t * TILE, TILE)
        flow = keep * wide(nimg_ref, q) * pull(q, cap1, tiles)
        out_ref[rows, :] = (ALPHA * (bands[0, rows, :].astype(F32) + keep_img[tiles + t]) + flow).astype(BF16)
        flow = keep * wide(ncap_ref, q) * acc2[t]
        rows = pl.ds((tiles + t) * TILE, TILE)
        out_ref[rows, :] = (ALPHA * (bands[0, rows, :].astype(F32) + keep_cap[tiles + t]) + flow).astype(BF16)


def propagate(places, bases, own, low, high, mate, far, tables, tiles, slots):
    width = own.shape[1]
    smem = pl.BlockSpec(memory_space=pltpu.SMEM)
    vmem = pl.BlockSpec(memory_space=pltpu.VMEM)
    hbm = pl.BlockSpec(memory_space=pltpu.HBM)
    mid, near = 5 * tiles, 3 * tiles
    return pl.pallas_call(
        lambda *r: hops_kernel(*r, tiles=tiles, slots=slots, width=width),
        out_shape=jax.ShapeDtypeStruct(own.shape, BF16),
        in_specs=[smem] * 2 + [hbm] * 11,
        out_specs=vmem,
        scratch_shapes=[
            pltpu.VMEM((5,) + own.shape, BF16),
            *[pltpu.VMEM(*t) for t in table_shapes(tiles, slots)],
            pltpu.VMEM((mid, TILE, width), BF16),
            pltpu.VMEM((mid, TILE, width), BF16),
            pltpu.VMEM((near, TILE, width), BF16),
            pltpu.VMEM((near, TILE, width), BF16),
            pltpu.VMEM((near + 1, TILE, width), F32),
            pltpu.VMEM((tiles + 1, TILE, width), F32),
            pltpu.VMEM((near, TILE, width), F32),
            pltpu.VMEM((near, TILE, width), F32),
            pltpu.SemaphoreType.DMA((11,)),
        ],
        compiler_params=pltpu.CompilerParams(vmem_limit_bytes=34 << 20),
        cost_estimate=SHORT,
        name="hops",
    )(places, bases, *[pltpu.with_memory_space_constraint(v, pltpu.HBM) for v in (own, low, high, *mate, *far, *tables)])


BLOCK = 64
GROUP = 4


def grouped(width):
    return [
        pl.BlockSpec((BLOCK, width), lambda i, order, k=k: (order[i * GROUP + k], 0)) for k in range(GROUP)
    ]


def stacked(refs):
    return jnp.concatenate([r[...] for r in refs], axis=0)


def whole(shape):
    return pl.BlockSpec(shape, lambda i, order: (0,) * len(shape))


def out_kernel(order_ref, *refs):
    act, (logit_ref, part_ref) = refs[:GROUP], refs[GROUP:]
    part_ref[...] = jnp.dot(stacked(act), logit_ref[...], preferred_element_type=F32).astype(BF16)


def in_kernel(order_ref, *refs):
    slope, w_out = refs[:GROUP], refs[GROUP : 2 * GROUP]
    logit_ref, feats_ref, part_ref, grad_ref = refs[2 * GROUP :]
    hidden = lax.dot_general(
        stacked(w_out), logit_ref[...], (((1,), (1,)), ((), ())), preferred_element_type=F32
    )
    grad = (hidden * stacked(slope)).astype(BF16)
    grad_ref[...] = grad
    f_in = feats_ref.shape[1]
    part_ref[:, :f_in] = jnp.dot(grad, feats_ref[...], preferred_element_type=F32).astype(BF16)
    bias = jnp.sum(grad.astype(F32), axis=1, keepdims=True)
    part_ref[:, f_in:] = jnp.broadcast_to(bias, (bias.shape[0], TILE)).astype(BF16)


def feat_kernel(order_ref, *refs):
    w_in = refs[:GROUP]
    kept_ref, sent_ref, img_ref, cap_ref, acc_ref = refs[GROUP:]
    i = pl.program_id(0)
    steps = pl.num_programs(0)

    @pl.when(i == 0)
    def _():
        acc_ref[...] = jnp.zeros_like(acc_ref)

    grad = jnp.where(i < steps // 2, kept_ref[...], sent_ref[...])
    acc_ref[...] += lax.dot_general(
        grad, stacked(w_in), (((0,), (0,)), ((), ())), preferred_element_type=F32
    )

    @pl.when(i == steps - 1)
    def _():
        half = img_ref.shape[0]
        img_ref[...] = acc_ref[:half].astype(BF16)
        cap_ref[...] = acc_ref[half:].astype(BF16)


def over_hidden(kernel, name, order, in_specs, out_specs, out_shape, scratch, args):
    return pl.pallas_call(
        kernel,
        out_shape=out_shape,
        grid_spec=pltpu.PrefetchScalarGridSpec(
            num_scalar_prefetch=1,
            grid=(order.shape[0] // GROUP,),
            in_specs=in_specs,
            out_specs=out_specs,
            scratch_shapes=scratch,
        ),
        compiler_params=pltpu.CompilerParams(
            dimension_semantics=("arbitrary",), vmem_limit_bytes=28 << 20
        ),
        cost_estimate=SHORT,
        name=name,
    )(order, *args)


def rows_of_half(width, half, side):
    steps = half // GROUP
    if side:
        return pl.BlockSpec((GROUP * BLOCK, width), lambda i, order: (jnp.maximum(i - steps, 0), 0))
    return pl.BlockSpec((GROUP * BLOCK, width), lambda i, order: (jnp.minimum(i, steps - 1), 0))


def rows_of(width):
    return pl.BlockSpec((GROUP * BLOCK, width), lambda i, order: (i, 0))


def stack_kernel(count_ref, top_ref, bottom_ref, seed_ref, cols_ref, out_ref, meta_ref):
    half = top_ref.shape[0]
    out_ref[:half] = top_ref[...]
    out_ref[half:] = bottom_ref[...]
    tiles, slots = seed_ref.shape
    meta_ref[:, :slots] = seed_ref[...]
    meta_ref[:, slots : 2 * slots] = cols_ref[...]
    row = lax.broadcasted_iota(jnp.int32, (tiles, slots), 0)
    live = jnp.zeros((tiles, slots), jnp.int32)
    for t in range(tiles):
        live = jnp.where(row == t, count_ref[t], live)
    meta_ref[:, 2 * slots :] = live


def stack(top, bottom, seed, cols, counts):
    vmem = pl.BlockSpec(memory_space=pltpu.VMEM)
    shape = (2 * top.shape[0], top.shape[1])
    codes = (seed.shape[0], 3 * seed.shape[1])
    return pl.pallas_call(
        stack_kernel,
        out_shape=(pltpu.HBM(shape, top.dtype), jax.ShapeDtypeStruct(codes, jnp.int32)),
        in_specs=[pl.BlockSpec(memory_space=pltpu.SMEM)] + [vmem] * 4,
        out_specs=(pl.BlockSpec(shape, lambda: (0, 0)), pl.BlockSpec(codes, lambda: (0, 0))),
        cost_estimate=SHORT,
        name="stack",
    )(counts, top, bottom, seed, cols)


def after(value, *done):
    return lax.optimization_barrier((value,) + done)[0]


def moved(array, count, by):
    return lax.ppermute(array, AXES, [(i, i + by) for i in range(count) if 0 <= i + by < count])


def flipped(array, count, mask):
    return lax.ppermute(array, AXES, [(i, i ^ mask) for i in range(count)])


def added(kept, came):
    return (kept.astype(F32) + came.astype(F32)).astype(BF16)


def parts(array, axis):
    return lax.index_in_dim(array, 0, axis, keepdims=False), lax.index_in_dim(array, 1, axis, keepdims=False)


def nearest_pair(count, by):
    return [(i, i + by) for i in range(0, count - by, 2)] + [(i, i - by) for i in range(by + 1, count, 2)]


class Reduction:

    def __init__(self, part, count, bits, first, orders, ends):
        self.count, self.parts, self.left = count, [part], [list(bits)]
        self.steps = [(bit,) for bit in first] + list(zip(*orders)) + [(bit,) for bit in ends]

    def start(self):
        step = self.steps.pop(0)
        if len(step) > len(self.parts):
            part = self.parts[0]
            cut = part.shape[-2] // 2
            self.parts = [part[..., :cut, :], part[..., cut:, :]]
            self.left = [list(self.left[0]), list(self.left[0])]
        elif len(step) < len(self.parts):
            self.parts = [jnp.concatenate(self.parts, axis=-2)]
        self.kept, self.sent, self.came = [], [], []
        for part, left, bit in zip(self.parts, self.left, step):
            kept, sent = parts(part, left.index(bit))
            left.remove(bit)
            self.kept.append(kept)
            self.sent.append(sent)
            self.came.append(flipped(sent, self.count, 1 << bit))

    def finish(self, *done):
        self.parts = [added(after(k, *done), c) for k, c in zip(self.kept, self.came)]

    def result(self, lanes):
        return self.kept[0][:, lanes].astype(F32) + self.came[0][:, lanes].astype(F32)


def per_device(
    feats_img, feats_cap, cot_img, cot_cap, w_in, b_in, w_out, tile_seed, tile_cols, tile_count
):
    local_rows = feats_img.shape[0]
    tiles = local_rows // TILE
    slots = tile_seed.shape[1]
    hid, f_in = w_in.shape
    n_img, n_cap = lax.axis_size("img"), lax.axis_size("cap")
    count = n_img * n_cap
    me = lax.axis_index(AXES)

    even = (me & 1) == 0
    mate = [flipped(cot_img, count, 1)]
    block, meta = stack(cot_img, cot_cap, tile_seed, tile_cols, tile_count)
    low = moved(block, count, 2)
    high = moved(block, count, -2)
    other = flipped(meta, count, 1)
    cot_cap, meta = lax.optimization_barrier((cot_cap, meta, other))[:2]
    mate.append(flipped(cot_cap, count, 1))
    third = lax.ppermute(
        meta, AXES, [(i, i + 3) for i in range(1, count - 3, 2)] + [(i, i - 3) for i in range(4, count, 2)]
    )
    far = [lax.ppermute(v, AXES, nearest_pair(count, 2)) for v in mate]
    m = count.bit_length() - 1
    a = n_cap.bit_length() - 1
    cap_bits = list(range(a))
    img_bits = list(range(a + 1, m - 2))
    bits = [a] + cap_bits + img_bits + [m - 2, m - 1]
    pos = jnp.arange(count, dtype=jnp.int32)
    order = jnp.zeros_like(pos)
    for k, bit in enumerate(bits):
        order = order | (((pos >> (m - 1 - k)) & 1) << bit)
    order = order ^ me
    rows = hid // count
    if rows % BLOCK:
        w_in, w_out, b_in = [
            jnp.take(v.reshape((count, rows) + v.shape[1:]), order, axis=0).reshape(v.shape) for v in (w_in, w_out, b_in)
        ]
        order = jnp.arange(hid // BLOCK, dtype=jnp.int32)
    else:
        order = (order[:, None] * (rows // BLOCK) + jnp.arange(rows // BLOCK, dtype=jnp.int32)).reshape(-1)

    feats = jnp.concatenate([after(feats_img, other), feats_cap], axis=0)
    across = (((1,), (1,)), ((), ()))
    preact = lax.dot_general(w_in, feats, across, preferred_element_type=F32) + b_in[:, None]
    gelu_value, gelu_slope = gelu_parts(preact)
    hidden_act, gelu_slope = lax.optimization_barrier((gelu_value.astype(BF16), gelu_slope))

    pair = jnp.where(even, jnp.concatenate([meta, other]), jnp.concatenate([other, meta]))
    pair, hidden_act, third, low, high = lax.optimization_barrier((pair, hidden_act, third, low, high))
    pair_low = moved(pair, count, 2)
    pair_high = moved(pair, count, -2)
    wide = jnp.where(
        even,
        jnp.concatenate([third, pair_low, pair, pair_high]),
        jnp.concatenate([pair_low, pair, pair_high, third]),
    )
    frame = jnp.arange(7 * tiles, dtype=jnp.int32)[:, None]
    counts = wide[:, 2 * slots]
    seeds = wide[:, :slots].reshape(-1)
    places = jnp.where(counts[:, None] > 0, wide[:, slots : 2 * slots] - (me - 3) * tiles, frame)
    pats = make_tiles(seeds, (places + tiles).reshape(-1), counts, tiles, slots)

    bases = jnp.where(even, jnp.array([3, 1]), jnp.array([1, 3])).astype(jnp.int32) * tiles
    mid_places = (places - tiles)[tiles : 6 * tiles].reshape(-1)
    logit = propagate(mid_places, bases, block, low, high, mate, far, pats, tiles, slots)

    width = cot_img.shape[1]
    nodes = 2 * local_rows
    half = order.shape[0] // 2
    blocked = (2,) * (m - 1) + (rows,)

    def out_half(order, logit):
        return over_hidden(
            out_kernel, "part_out", order, grouped(nodes) + [whole(logit.shape)], rows_of(width),
            jax.ShapeDtypeStruct((hid // 2, width), BF16), [], [hidden_act] * GROUP + [logit],
        ).reshape(blocked + (width,))

    def in_half(order, logit):
        part, grad = over_hidden(
            in_kernel, "part_in", order,
            grouped(nodes) + grouped(width) + [whole(logit.shape), whole(feats.shape)],
            (rows_of(f_in + TILE), rows_of(nodes)),
            (jax.ShapeDtypeStruct((hid // 2, f_in + TILE), BF16), jax.ShapeDtypeStruct((hid // 2, nodes), BF16)),
            [], [gelu_slope] * GROUP + [w_out] * GROUP + [logit, feats],
        )
        return part.reshape(blocked + (f_in + TILE,)), grad

    core = 1 << a
    rest = bits[1:]
    orders = (cap_bits + img_bits, img_bits + cap_bits)
    near, last = m - 2, m - 1
    in_sent, grad_sent = in_half(order[half:], logit)
    in_came = flipped(in_sent, count, core)
    in_kept, grad_kept = in_half(order[:half], after(logit, grad_sent))
    r_in = Reduction(added(in_kept, in_came), count, rest, (), orders, (near, last))
    r_in.start()
    out_sent = out_half(order[half:], after(logit, *r_in.sent))
    out_came = flipped(out_sent, count, core)
    out_kept = out_half(order[:half], after(logit, out_sent))
    r_out = Reduction(added(out_kept, out_came), count, rest, (near,), orders, (last,))
    r_out.start()
    grad_img, grad_cap = over_hidden(
        feat_kernel, "feat_grad", order, grouped(f_in) + [rows_of_half(nodes, half, 0), rows_of_half(nodes, half, 1)],
        (whole((local_rows, f_in)),) * 2, (jax.ShapeDtypeStruct((local_rows, f_in), BF16),) * 2,
        [pltpu.VMEM((nodes, f_in), F32)], [w_in] * GROUP + [after(grad_kept, *r_out.sent), grad_sent],
    )
    done = (grad_img,)
    for _ in range(m - 2):
        r_in.finish(*done)
        r_in.start()
        r_out.finish(*r_in.sent)
        r_out.start()
        done = r_out.sent
    grad_scale = 1.0 / math.sqrt(nodes * count)
    g_out = r_out.result(slice(None)) * grad_scale
    g_in = r_in.result(slice(0, f_in)) * grad_scale
    g_bias = r_in.result(f_in) * grad_scale
    return (grad_img, grad_cap, g_in, g_out, g_bias)


def solution(mesh):
    rows = P(("img", "cap"), None)
    in_specs = (rows, rows, rows, rows, P(), P(), P(), rows, rows, P(("img", "cap")))
    out_specs = (rows, rows, rows, rows, P(("img", "cap")))
    return jax.shard_map(
        per_device, mesh=mesh, in_specs=in_specs, out_specs=out_specs, check_vma=False
    )
```

```python
import math

import jax
import jax.numpy as jnp
from jax import lax
from jax.experimental import pallas as pl
from jax.experimental.pallas import tpu as pltpu
from jax.sharding import PartitionSpec as P

TILE = 128
ALPHA = 0.1
SHORT = pl.CostEstimate(flops=1, transcendentals=0, bytes_accessed=1)
AXES = ("img", "cap")
F32 = jnp.float32
BF16 = jnp.bfloat16


def gelu_parts(preact):
    normal_cdf = 0.5 * (1.0 + jax.scipy.special.erf(preact * 0.7071067811865476))
    normal_pdf = jnp.exp(-0.5 * preact * preact) * 0.3989422804014327
    return (preact * normal_cdf, normal_cdf + preact * normal_pdf)


def tiles_kernel(seed_ref, place_ref, count_ref, *refs, tiles, slots):
    outs, (pat_ref, pat_t_ref, nimg_ref, ncap_ref, deg_ref, sems) = refs[:4], refs[4:]
    all_tiles, mid = 7 * tiles, 5 * tiles
    deg_ref[...] = jnp.zeros_like(deg_ref)
    row = lax.broadcasted_iota(jnp.int32, (TILE, TILE), 0)
    col = lax.broadcasted_iota(jnp.int32, (TILE, TILE), 1)
    first, second = jnp.int32(668265261), jnp.int32(374761393)
    base = (row * 40503 + col * 9973) * first
    base_t = (col * 40503 + row * 9973) * first
    off_diag = row - col

    def pattern(start, seed, live, s):
        mixed = start + seed * first
        mixed = jnp.bitwise_xor(mixed, jnp.right_shift(mixed, 15))
        mixed = mixed * second
        mixed = jnp.bitwise_xor(mixed, jnp.right_shift(mixed, 13))
        edge = jnp.bitwise_and(mixed, 15) == jnp.where(live, 0, 16)
        if s == 0:
            edge = edge | (off_diag == jnp.where(live, 0, TILE))
        return jnp.where(edge, 1.0, 0.0)

    def one(q, full):
        total = None
        for s in range(slots):
            live = s < count_ref[q]
            seed = seed_ref[q * slots + s]
            e = pattern(base, seed, live, s)
            c = place_ref[q * slots + s]
            deg_ref[c] += jnp.sum(e, axis=0, keepdims=True)
            if full:
                m = q - tiles
                pat_ref[m, :, pl.ds(s * TILE, TILE)] = e.astype(BF16)
                pat_t_ref[m, pl.ds(s * TILE, TILE), :] = pattern(base_t, seed, live, s).astype(BF16)
                total = e if total is None else total + e
        if full:
            d = jnp.sum(total, axis=1, keepdims=True)
            n = jnp.where(d > 0.0, lax.rsqrt(d), 0.0)
            nimg_ref[q - tiles] = jnp.broadcast_to(n, (TILE, TILE))
            for k, (src, dst) in enumerate(zip((pat_ref, pat_t_ref, nimg_ref), outs)):
                pltpu.make_async_copy(src.at[q - tiles], dst.at[q - tiles], sems.at[k]).start()

    def edge_body(q, c):
        one(q, False)
        return c

    def mid_body(q, c):
        one(q, True)
        return c

    lax.fori_loop(0, tiles, edge_body, 0)
    lax.fori_loop(tiles, tiles + mid, mid_body, 0)
    copies = [
        pltpu.make_async_copy(src, dst, sems.at[k])
        for k, (src, dst) in enumerate(zip((pat_ref, pat_t_ref, nimg_ref, ncap_ref), outs))
    ]
    lax.fori_loop(tiles + mid, all_tiles, edge_body, 0)
    for m in range(mid):
        d = deg_ref[m + 2 * tiles]
        n = jnp.where(d > 0.0, lax.rsqrt(d), 0.0)
        ncap_ref[m] = jnp.broadcast_to(n, (TILE, TILE)).T
    copies[3].start()
    for copy in copies:
        copy.wait()


def table_shapes(tiles, slots):
    mid = 5 * tiles
    return (
        ((mid, TILE, slots * TILE), BF16),
        ((mid, slots * TILE, TILE), BF16),
        ((mid, TILE, TILE), F32),
        ((mid, TILE, TILE), F32),
    )


def make_tiles(seeds, places, counts, tiles, slots):
    smem = pl.BlockSpec(memory_space=pltpu.SMEM)
    hbm = pl.BlockSpec(memory_space=pltpu.HBM)
    tables = table_shapes(tiles, slots)
    return pl.pallas_call(
        lambda *r: tiles_kernel(*r, tiles=tiles, slots=slots),
        out_shape=tuple(pltpu.HBM(*t) for t in tables),
        in_specs=[smem] * 3,
        out_specs=(hbm,) * 4,
        scratch_shapes=[pltpu.VMEM(*t) for t in tables]
        + [pltpu.VMEM((9 * tiles, 1, TILE), F32), pltpu.SemaphoreType.DMA((4,))],
        compiler_params=pltpu.CompilerParams(vmem_limit_bytes=16 << 20),
        cost_estimate=SHORT,
        name="tiles",
    )(seeds, places, counts)


def hops_kernel(
    place_ref, base_ref, own_hbm, low_hbm, high_hbm, mate_hbm, far_hbm, pat_hbm, pat_t_hbm, nimg_hbm, ncap_hbm,
    out_ref, bands, pat_ref, pat_t_ref, nimg_ref, ncap_ref, img0, cap0, img1, cap1, acc, acc2, keep_img, keep_cap,
    sems, *, tiles, slots, width,
):
    mid = 5 * tiles
    near = 3 * tiles
    keep = 1.0 - ALPHA
    sources = (own_hbm, nimg_hbm, ncap_hbm, pat_t_hbm, low_hbm, high_hbm, mate_hbm, far_hbm, pat_hbm)
    targets = (bands.at[0], nimg_ref, ncap_ref, pat_t_ref) + tuple(bands.at[k] for k in range(1, 5)) + (pat_ref,)
    copies = [pltpu.make_async_copy(s, t, sems.at[k]) for k, (s, t) in enumerate(zip(sources, targets))]
    for copy in copies:
        copy.start()

    def wide(n_ref, m):
        n = n_ref[m]
        return jnp.concatenate([n] * (width // TILE), axis=1)

    def scale(k, base):
        for t in range(tiles):
            m = base + t
            img0[m] = (bands[k, pl.ds(t * TILE, TILE), :].astype(F32) * wide(nimg_ref, m)).astype(BF16)
            cap0[m] = (bands[k, pl.ds((tiles + t) * TILE, TILE), :].astype(F32) * wide(ncap_ref, m)).astype(BF16)

    acc[...] = jnp.zeros_like(acc)
    acc2[...] = jnp.zeros_like(acc2)

    def push(q, state, target, lo, count):
        r = jnp.dot(pat_t_ref[q], state, preferred_element_type=F32)
        for s in range(slots):
            c = place_ref[q * slots + s] - lo
            c = jnp.where((c >= 0) & (c < count), c, count)
            target[c] += r[s * TILE : (s + 1) * TILE]

    def pull(q, source, lo):
        total = None
        for s in range(slots):
            c = place_ref[q * slots + s] - lo
            r = jnp.dot(pat_ref[q, :, pl.ds(s * TILE, TILE)], source[c], preferred_element_type=F32)
            total = r if total is None else total + r
        return total

    for copy in copies[:4]:
        copy.wait()
    for k, base in enumerate((2 * tiles, 0, 4 * tiles, base_ref[0], base_ref[1])):
        if k:
            copies[3 + k].wait()
        scale(k, base)
        for t in range(tiles):
            push(base + t, img0[base + t], acc, tiles, near)
    copies[8].wait()

    def pull1(q, c):
        n = wide(nimg_ref, q)
        flow = keep * n * pull(q, cap0, 0)
        img1[q - tiles] = (flow * n).astype(BF16)
        keep_img[q - tiles] = flow
        return c

    lax.fori_loop(tiles, tiles + near, pull1, 0, unroll=9)

    def finish1(m, c):
        n = wide(ncap_ref, m + tiles)
        flow = keep * n * acc[m]
        cap1[m] = (flow * n).astype(BF16)
        keep_cap[m] = flow
        return c

    lax.fori_loop(0, near, finish1, 0, unroll=3)

    def push2(q, c):
        push(q, img1[q - tiles], acc2, 2 * tiles, tiles)
        return c

    lax.fori_loop(tiles, tiles + near, push2, 0, unroll=3)
    for t in range(tiles):
        q = 2 * tiles + t
        rows = pl.ds(t * TILE, TILE)
        flow = keep * wide(nimg_ref, q) * pull(q, cap1, tiles)
        out_ref[rows, :] = (ALPHA * (bands[0, rows, :].astype(F32) + keep_img[tiles + t]) + flow).astype(BF16)
        flow = keep * wide(ncap_ref, q) * acc2[t]
        rows = pl.ds((tiles + t) * TILE, TILE)
        out_ref[rows, :] = (ALPHA * (bands[0, rows, :].astype(F32) + keep_cap[tiles + t]) + flow).astype(BF16)


def propagate(places, bases, own, low, high, mate, far, tables, tiles, slots):
    width = own.shape[1]
    smem = pl.BlockSpec(memory_space=pltpu.SMEM)
    vmem = pl.BlockSpec(memory_space=pltpu.VMEM)
    hbm = pl.BlockSpec(memory_space=pltpu.HBM)
    mid, near = 5 * tiles, 3 * tiles
    return pl.pallas_call(
        lambda *r: hops_kernel(*r, tiles=tiles, slots=slots, width=width),
        out_shape=jax.ShapeDtypeStruct(own.shape, BF16),
        in_specs=[smem] * 2 + [hbm] * 9,
        out_specs=vmem,
        scratch_shapes=[
            pltpu.VMEM((5,) + own.shape, BF16),
            *[pltpu.VMEM(*t) for t in table_shapes(tiles, slots)],
            pltpu.VMEM((mid, TILE, width), BF16),
            pltpu.VMEM((mid, TILE, width), BF16),
            pltpu.VMEM((near, TILE, width), BF16),
            pltpu.VMEM((near, TILE, width), BF16),
            pltpu.VMEM((near + 1, TILE, width), F32),
            pltpu.VMEM((tiles + 1, TILE, width), F32),
            pltpu.VMEM((near, TILE, width), F32),
            pltpu.VMEM((near, TILE, width), F32),
            pltpu.SemaphoreType.DMA((9,)),
        ],
        compiler_params=pltpu.CompilerParams(vmem_limit_bytes=34 << 20),
        cost_estimate=SHORT,
        name="hops",
    )(places, bases, *[pltpu.with_memory_space_constraint(v, pltpu.HBM) for v in (own, low, high, mate, far, *tables)])


BLOCK = 64
GROUP = 4


def grouped(width):
    return [
        pl.BlockSpec((BLOCK, width), lambda i, order, k=k: (order[i * GROUP + k], 0)) for k in range(GROUP)
    ]


def stacked(refs):
    return jnp.concatenate([r[...] for r in refs], axis=0)


def whole(shape):
    return pl.BlockSpec(shape, lambda i, order: (0,) * len(shape))


def out_kernel(order_ref, *refs):
    act, (logit_ref, bias_ref, part_ref) = refs[:GROUP], refs[GROUP:]
    width = logit_ref.shape[1]
    part_ref[:, :width] = jnp.dot(stacked(act), logit_ref[...], preferred_element_type=F32).astype(BF16)
    part_ref[:, width:] = bias_ref[...]


def in_kernel(order_ref, *refs):
    slope, w_out = refs[:GROUP], refs[GROUP : 2 * GROUP]
    logit_ref, feats_ref, part_ref, grad_ref, bias_ref = refs[2 * GROUP :]
    hidden = lax.dot_general(
        stacked(w_out), logit_ref[...], (((1,), (1,)), ((), ())), preferred_element_type=F32
    )
    grad = (hidden * stacked(slope)).astype(BF16)
    grad_ref[...] = grad
    part_ref[...] = jnp.dot(grad, feats_ref[...], preferred_element_type=F32).astype(BF16)
    bias = jnp.sum(grad.astype(F32), axis=1, keepdims=True)
    bias_ref[...] = jnp.broadcast_to(bias, (bias.shape[0], TILE)).astype(BF16)


def feat_kernel(order_ref, *refs):
    w_in = refs[:GROUP]
    kept_ref, sent_ref, img_ref, cap_ref, acc_ref = refs[GROUP:]
    i = pl.program_id(0)
    steps = pl.num_programs(0)

    @pl.when(i == 0)
    def _():
        acc_ref[...] = jnp.zeros_like(acc_ref)

    grad = jnp.where(i < steps // 2, kept_ref[...], sent_ref[...])
    acc_ref[...] += lax.dot_general(
        grad, stacked(w_in), (((0,), (0,)), ((), ())), preferred_element_type=F32
    )

    @pl.when(i == steps - 1)
    def _():
        half = img_ref.shape[0]
        img_ref[...] = acc_ref[:half].astype(BF16)
        cap_ref[...] = acc_ref[half:].astype(BF16)


def over_hidden(kernel, name, order, in_specs, out_specs, out_shape, scratch, args):
    return pl.pallas_call(
        kernel,
        out_shape=out_shape,
        grid_spec=pltpu.PrefetchScalarGridSpec(
            num_scalar_prefetch=1,
            grid=(order.shape[0] // GROUP,),
            in_specs=in_specs,
            out_specs=out_specs,
            scratch_shapes=scratch,
        ),
        compiler_params=pltpu.CompilerParams(
            dimension_semantics=("arbitrary",), vmem_limit_bytes=28 << 20
        ),
        cost_estimate=SHORT,
        name=name,
    )(order, *args)


def rows_of_half(width, half, side):
    steps = half // GROUP
    if side:
        return pl.BlockSpec((GROUP * BLOCK, width), lambda i, order: (jnp.maximum(i - steps, 0), 0))
    return pl.BlockSpec((GROUP * BLOCK, width), lambda i, order: (jnp.minimum(i, steps - 1), 0))


def rows_of(width):
    return pl.BlockSpec((GROUP * BLOCK, width), lambda i, order: (i, 0))


def stack_kernel(count_ref, top_ref, bottom_ref, seed_ref, cols_ref, out_ref, meta_ref):
    half = top_ref.shape[0]
    out_ref[:half] = top_ref[...]
    out_ref[half:] = bottom_ref[...]
    tiles, slots = seed_ref.shape
    meta_ref[:, :slots] = seed_ref[...]
    meta_ref[:, slots : 2 * slots] = cols_ref[...]
    row = lax.broadcasted_iota(jnp.int32, (tiles, slots), 0)
    live = jnp.zeros((tiles, slots), jnp.int32)
    for t in range(tiles):
        live = jnp.where(row == t, count_ref[t], live)
    meta_ref[:, 2 * slots :] = live


def stack(top, bottom, seed, cols, counts):
    vmem = pl.BlockSpec(memory_space=pltpu.VMEM)
    shape = (2 * top.shape[0], top.shape[1])
    codes = (seed.shape[0], 3 * seed.shape[1])
    return pl.pallas_call(
        stack_kernel,
        out_shape=(pltpu.HBM(shape, top.dtype), jax.ShapeDtypeStruct(codes, jnp.int32)),
        in_specs=[pl.BlockSpec(memory_space=pltpu.SMEM)] + [vmem] * 4,
        out_specs=(pl.BlockSpec(shape, lambda: (0, 0)), pl.BlockSpec(codes, lambda: (0, 0))),
        cost_estimate=SHORT,
        name="stack",
    )(counts, top, bottom, seed, cols)


def after(value, *done):
    return lax.optimization_barrier((value,) + done)[0]


def moved(array, count, by):
    return lax.ppermute(array, AXES, [(i, i + by) for i in range(count) if 0 <= i + by < count])


def flipped(array, count, mask):
    return lax.ppermute(array, AXES, [(i, i ^ mask) for i in range(count)])


def added(kept, came):
    return (kept.astype(F32) + came.astype(F32)).astype(BF16)


def parts(array, axis):
    return lax.index_in_dim(array, 0, axis, keepdims=False), lax.index_in_dim(array, 1, axis, keepdims=False)


def nearest_pair(count, by):
    return [(i, i + by) for i in range(0, count - by, 2)] + [(i, i - by) for i in range(by + 1, count, 2)]


class Reduction:

    def __init__(self, part, count, bits, first, orders, ends):
        self.count, self.parts, self.left = count, [part], [list(bits)]
        self.steps = [(bit,) for bit in first] + list(zip(*orders)) + [(bit,) for bit in ends]

    def start(self):
        step = self.steps.pop(0)
        if len(step) > len(self.parts):
            part = self.parts[0]
            cut = part.shape[-2] // 2
            self.parts = [part[..., :cut, :], part[..., cut:, :]]
            self.left = [list(self.left[0]), list(self.left[0])]
        elif len(step) < len(self.parts):
            self.parts = [jnp.concatenate(self.parts, axis=-2)]
        self.kept, self.sent, self.came = [], [], []
        for part, left, bit in zip(self.parts, self.left, step):
            kept, sent = parts(part, left.index(bit))
            left.remove(bit)
            self.kept.append(kept)
            self.sent.append(sent)
            self.came.append(flipped(sent, self.count, 1 << bit))

    def finish(self, *done):
        self.parts = [added(after(k, *done), c) for k, c in zip(self.kept, self.came)]

    def result(self, lanes):
        return self.kept[0][:, lanes].astype(F32) + self.came[0][:, lanes].astype(F32)


def per_device(
    feats_img, feats_cap, cot_img, cot_cap, w_in, b_in, w_out, tile_seed, tile_cols, tile_count
):
    local_rows = feats_img.shape[0]
    tiles = local_rows // TILE
    slots = tile_seed.shape[1]
    hid, f_in = w_in.shape
    n_img, n_cap = lax.axis_size("img"), lax.axis_size("cap")
    count = n_img * n_cap
    me = lax.axis_index(AXES)

    even = (me & 1) == 0
    block, meta = stack(cot_img, cot_cap, tile_seed, tile_cols, tile_count)
    other = flipped(meta, count, 1)
    third = lax.ppermute(
        meta, AXES, [(i, i + 3) for i in range(1, count - 3, 2)] + [(i, i - 3) for i in range(4, count, 2)]
    )
    block = after(block, other)
    mate = flipped(block, count, 1)
    low = moved(block, count, 2)
    high = moved(block, count, -2)
    far = lax.ppermute(mate, AXES, nearest_pair(count, 2))
    pair = jnp.where(even, jnp.concatenate([meta, other]), jnp.concatenate([other, meta]))
    feats = jnp.concatenate([after(feats_img, block), feats_cap], axis=0)
    pair, feats, third = lax.optimization_barrier((pair, feats, third))
    pair_low = moved(pair, count, 2)
    pair_high = moved(pair, count, -2)
    wide = jnp.where(
        even,
        jnp.concatenate([third, pair_low, pair, pair_high]),
        jnp.concatenate([pair_low, pair, pair_high, third]),
    )
    frame = jnp.arange(7 * tiles, dtype=jnp.int32)[:, None]
    counts = wide[:, 2 * slots]
    seeds = wide[:, :slots].reshape(-1)
    places = jnp.where(counts[:, None] > 0, wide[:, slots : 2 * slots] - (me - 3) * tiles, frame)
    pats = make_tiles(seeds, (places + tiles).reshape(-1), counts, tiles, slots)

    m = count.bit_length() - 1
    a = n_cap.bit_length() - 1
    cap_bits = list(range(a))
    img_bits = list(range(a + 1, m - 2))
    bits = [a] + cap_bits + img_bits + [m - 2, m - 1]
    pos = jnp.arange(count, dtype=jnp.int32)
    order = jnp.zeros_like(pos)
    for k, bit in enumerate(bits):
        order = order | (((pos >> (m - 1 - k)) & 1) << bit)
    order = order ^ me
    rows = hid // count
    if rows % BLOCK:
        w_in, w_out, b_in = [
            jnp.take(v.reshape((count, rows) + v.shape[1:]), order, axis=0).reshape(v.shape) for v in (w_in, w_out, b_in)
        ]
        order = jnp.arange(hid // BLOCK, dtype=jnp.int32)
    else:
        order = (order[:, None] * (rows // BLOCK) + jnp.arange(rows // BLOCK, dtype=jnp.int32)).reshape(-1)

    across = (((1,), (1,)), ((), ()))
    preact = lax.dot_general(w_in, feats, across, preferred_element_type=F32) + b_in[:, None]
    gelu_value, gelu_slope = gelu_parts(preact)
    hidden_act, gelu_slope = lax.optimization_barrier((gelu_value.astype(BF16), gelu_slope))

    bases = jnp.where(even, jnp.array([3, 1]), jnp.array([1, 3])).astype(jnp.int32) * tiles
    mid_places = (places - tiles)[tiles : 6 * tiles].reshape(-1)
    logit = propagate(mid_places, bases, block, low, high, mate, far, pats, tiles, slots)

    width = cot_img.shape[1]
    nodes = 2 * local_rows
    half = order.shape[0] // 2
    blocked = (2,) * (m - 1) + (rows,)

    def out_half(order, logit, bias):
        return over_hidden(
            out_kernel, "part_out", order, grouped(nodes) + [whole(logit.shape), rows_of(TILE)], rows_of(width + TILE),
            jax.ShapeDtypeStruct((hid // 2, width + TILE), BF16), [], [hidden_act] * GROUP + [logit, bias],
        ).reshape(blocked + (width + TILE,))

    def in_half(order, logit):
        part, grad, bias = over_hidden(
            in_kernel, "part_in", order,
            grouped(nodes) + grouped(width) + [whole(logit.shape), whole(feats.shape)],
            (rows_of(f_in), rows_of(nodes), rows_of(TILE)),
            tuple(jax.ShapeDtypeStruct((hid // 2, lanes), BF16) for lanes in (f_in, nodes, TILE)),
            [], [gelu_slope] * GROUP + [w_out] * GROUP + [logit, feats],
        )
        return part.reshape(blocked + (f_in,)), grad, bias

    core = 1 << a
    rest = bits[1:]
    orders = (cap_bits + img_bits, img_bits + cap_bits)
    near, last = m - 2, m - 1
    in_sent, grad_sent, bias_sent = in_half(order[half:], logit)
    in_came = flipped(in_sent, count, core)
    in_kept, grad_kept, bias_kept = in_half(order[:half], after(logit, grad_sent))
    r_in = Reduction(added(in_kept, in_came), count, rest, (), orders, (near, last))
    r_in.start()
    out_sent = out_half(order[half:], after(logit, *r_in.sent), bias_sent)
    out_came = flipped(out_sent, count, core)
    out_kept = out_half(order[:half], after(logit, out_sent), bias_kept)
    r_out = Reduction(added(out_kept, out_came), count, rest, (near,), orders, (last,))
    r_out.start()
    grad_img, grad_cap = over_hidden(
        feat_kernel, "feat_grad", order, grouped(f_in) + [rows_of_half(nodes, half, 0), rows_of_half(nodes, half, 1)],
        (whole((local_rows, f_in)),) * 2, (jax.ShapeDtypeStruct((local_rows, f_in), BF16),) * 2,
        [pltpu.VMEM((nodes, f_in), F32)], [w_in] * GROUP + [after(grad_kept, *r_out.sent), grad_sent],
    )
    done = (grad_img,)
    for _ in range(m - 2):
        r_in.finish(*done)
        r_in.start()
        r_out.finish(*r_in.sent)
        r_out.start()
        done = r_out.sent
    grad_scale = 1.0 / math.sqrt(nodes * count)
    g_out = r_out.result(slice(0, width)) * grad_scale
    g_bias = r_out.result(width) * grad_scale
    g_in = r_in.result(slice(None)) * grad_scale
    return (grad_img, grad_cap, g_in, g_out, g_bias)


def solution(mesh):
    rows = P(("img", "cap"), None)
    in_specs = (rows, rows, rows, rows, P(), P(), P(), rows, rows, P(("img", "cap")))
    out_specs = (rows, rows, rows, rows, P(("img", "cap")))
    return jax.shard_map(
        per_device, mesh=mesh, in_specs=in_specs, out_specs=out_specs, check_vma=False
    )
```

```python
import math

import jax
import jax.numpy as jnp
from jax import lax
from jax.experimental import pallas as pl
from jax.experimental.pallas import tpu as pltpu
from jax.sharding import PartitionSpec as P

TILE = 128
ALPHA = 0.1
SHORT = pl.CostEstimate(flops=1, transcendentals=0, bytes_accessed=1)
AXES = ("img", "cap")
F32 = jnp.float32
BF16 = jnp.bfloat16


def gelu_parts(preact):
    normal_cdf = 0.5 * (1.0 + jax.scipy.special.erf(preact * 0.7071067811865476))
    normal_pdf = jnp.exp(-0.5 * preact * preact) * 0.3989422804014327
    return (preact * normal_cdf, normal_cdf + preact * normal_pdf)


def tiles_kernel(seed_ref, place_ref, count_ref, *refs, tiles, slots):
    outs, (pat_ref, pat_t_ref, nimg_ref, ncap_ref, deg_ref, sems) = refs[:4], refs[4:]
    all_tiles, mid = 7 * tiles, 5 * tiles
    deg_ref[...] = jnp.zeros_like(deg_ref)
    row = lax.broadcasted_iota(jnp.int32, (TILE, TILE), 0)
    col = lax.broadcasted_iota(jnp.int32, (TILE, TILE), 1)
    first, second = jnp.int32(668265261), jnp.int32(374761393)
    base = (row * 40503 + col * 9973) * first
    base_t = (col * 40503 + row * 9973) * first
    off_diag = row - col

    def pattern(start, seed, live, s):
        mixed = start + seed * first
        mixed = jnp.bitwise_xor(mixed, jnp.right_shift(mixed, 15))
        mixed = mixed * second
        mixed = jnp.bitwise_xor(mixed, jnp.right_shift(mixed, 13))
        edge = jnp.bitwise_and(mixed, 15) == jnp.where(live, 0, 16)
        if s == 0:
            edge = edge | (off_diag == jnp.where(live, 0, TILE))
        return jnp.where(edge, 1.0, 0.0)

    def one(q, full):
        total = None
        for s in range(slots):
            live = s < count_ref[q]
            seed = seed_ref[q * slots + s]
            e = pattern(base, seed, live, s)
            c = place_ref[q * slots + s]
            deg_ref[c] += jnp.sum(e, axis=0, keepdims=True)
            if full:
                m = q - tiles
                pat_ref[m, :, pl.ds(s * TILE, TILE)] = e.astype(BF16)
                pat_t_ref[m, pl.ds(s * TILE, TILE), :] = pattern(base_t, seed, live, s).astype(BF16)
                total = e if total is None else total + e
        if full:
            d = jnp.sum(total, axis=1, keepdims=True)
            n = jnp.where(d > 0.0, lax.rsqrt(d), 0.0)
            nimg_ref[q - tiles] = jnp.broadcast_to(n, (TILE, TILE))
            for k, (src, dst) in enumerate(zip((pat_ref, pat_t_ref, nimg_ref), outs)):
                pltpu.make_async_copy(src.at[q - tiles], dst.at[q - tiles], sems.at[k]).start()

    def edge_body(q, c):
        one(q, False)
        return c

    def mid_body(q, c):
        one(q, True)
        return c

    lax.fori_loop(0, tiles, edge_body, 0)
    lax.fori_loop(tiles, tiles + mid, mid_body, 0)
    copies = [
        pltpu.make_async_copy(src, dst, sems.at[k])
        for k, (src, dst) in enumerate(zip((pat_ref, pat_t_ref, nimg_ref, ncap_ref), outs))
    ]
    lax.fori_loop(tiles + mid, all_tiles, edge_body, 0)
    for m in range(mid):
        d = deg_ref[m + 2 * tiles]
        n = jnp.where(d > 0.0, lax.rsqrt(d), 0.0)
        ncap_ref[m] = jnp.broadcast_to(n, (TILE, TILE)).T
    copies[3].start()
    for copy in copies:
        copy.wait()


def table_shapes(tiles, slots):
    mid = 5 * tiles
    return (
        ((mid, TILE, slots * TILE), BF16),
        ((mid, slots * TILE, TILE), BF16),
        ((mid, TILE, TILE), F32),
        ((mid, TILE, TILE), F32),
    )


def make_tiles(seeds, places, counts, tiles, slots):
    smem = pl.BlockSpec(memory_space=pltpu.SMEM)
    hbm = pl.BlockSpec(memory_space=pltpu.HBM)
    tables = table_shapes(tiles, slots)
    return pl.pallas_call(
        lambda *r: tiles_kernel(*r, tiles=tiles, slots=slots),
        out_shape=tuple(pltpu.HBM(*t) for t in tables),
        in_specs=[smem] * 3,
        out_specs=(hbm,) * 4,
        scratch_shapes=[pltpu.VMEM(*t) for t in tables]
        + [pltpu.VMEM((9 * tiles, 1, TILE), F32), pltpu.SemaphoreType.DMA((4,))],
        compiler_params=pltpu.CompilerParams(vmem_limit_bytes=16 << 20),
        cost_estimate=SHORT,
        name="tiles",
    )(seeds, places, counts)


def hops_kernel(
    place_ref, base_ref, own_hbm, low_hbm, high_hbm, mate_hbm, far_hbm, pat_hbm, pat_t_hbm, nimg_hbm, ncap_hbm,
    out_ref, bands, pat_ref, pat_t_ref, nimg_ref, ncap_ref, img0, cap0, img1, cap1, acc, acc2, keep_img, keep_cap,
    sems, *, tiles, slots, width,
):
    mid = 5 * tiles
    near = 3 * tiles
    keep = 1.0 - ALPHA
    sources = (own_hbm, nimg_hbm, ncap_hbm, pat_t_hbm, low_hbm, high_hbm, mate_hbm, far_hbm, pat_hbm)
    targets = (bands.at[0], nimg_ref, ncap_ref, pat_t_ref) + tuple(bands.at[k] for k in range(1, 5)) + (pat_ref,)
    copies = [pltpu.make_async_copy(s, t, sems.at[k]) for k, (s, t) in enumerate(zip(sources, targets))]
    for copy in copies:
        copy.start()

    def wide(n_ref, m):
        n = n_ref[m]
        return jnp.concatenate([n] * (width // TILE), axis=1)

    def scale(k, base):
        for t in range(tiles):
            m = base + t
            img0[m] = (bands[k, pl.ds(t * TILE, TILE), :].astype(F32) * wide(nimg_ref, m)).astype(BF16)
            cap0[m] = (bands[k, pl.ds((tiles + t) * TILE, TILE), :].astype(F32) * wide(ncap_ref, m)).astype(BF16)

    acc[...] = jnp.zeros_like(acc)
    acc2[...] = jnp.zeros_like(acc2)

    def push(q, state, target, lo, count):
        r = jnp.dot(pat_t_ref[q], state, preferred_element_type=F32)
        for s in range(slots):
            c = place_ref[q * slots + s] - lo
            c = jnp.where((c >= 0) & (c < count), c, count)
            target[c] += r[s * TILE : (s + 1) * TILE]

    def pull(q, source, lo):
        total = None
        for s in range(slots):
            c = place_ref[q * slots + s] - lo
            r = jnp.dot(pat_ref[q, :, pl.ds(s * TILE, TILE)], source[c], preferred_element_type=F32)
            total = r if total is None else total + r
        return total

    for copy in copies[:4]:
        copy.wait()
    for k, base in enumerate((2 * tiles, 0, 4 * tiles, base_ref[0], base_ref[1])):
        if k:
            copies[3 + k].wait()
        scale(k, base)
        for t in range(tiles):
            push(base + t, img0[base + t], acc, tiles, near)
    copies[8].wait()

    def pull1(q, c):
        n = wide(nimg_ref, q)
        flow = keep * n * pull(q, cap0, 0)
        img1[q - tiles] = (flow * n).astype(BF16)
        keep_img[q - tiles] = flow
        return c

    lax.fori_loop(tiles, tiles + near, pull1, 0, unroll=9)

    def finish1(m, c):
        n = wide(ncap_ref, m + tiles)
        flow = keep * n * acc[m]
        cap1[m] = (flow * n).astype(BF16)
        keep_cap[m] = flow
        return c

    lax.fori_loop(0, near, finish1, 0, unroll=3)

    def push2(q, c):
        push(q, img1[q - tiles], acc2, 2 * tiles, tiles)
        return c

    lax.fori_loop(tiles, tiles + near, push2, 0, unroll=3)
    for t in range(tiles):
        q = 2 * tiles + t
        rows = pl.ds(t * TILE, TILE)
        flow = keep * wide(nimg_ref, q) * pull(q, cap1, tiles)
        out_ref[rows, :] = (ALPHA * (bands[0, rows, :].astype(F32) + keep_img[tiles + t]) + flow).astype(BF16)
        flow = keep * wide(ncap_ref, q) * acc2[t]
        rows = pl.ds((tiles + t) * TILE, TILE)
        out_ref[rows, :] = (ALPHA * (bands[0, rows, :].astype(F32) + keep_cap[tiles + t]) + flow).astype(BF16)


def propagate(places, bases, own, low, high, mate, far, tables, tiles, slots):
    width = own.shape[1]
    smem = pl.BlockSpec(memory_space=pltpu.SMEM)
    vmem = pl.BlockSpec(memory_space=pltpu.VMEM)
    hbm = pl.BlockSpec(memory_space=pltpu.HBM)
    mid, near = 5 * tiles, 3 * tiles
    return pl.pallas_call(
        lambda *r: hops_kernel(*r, tiles=tiles, slots=slots, width=width),
        out_shape=jax.ShapeDtypeStruct(own.shape, BF16),
        in_specs=[smem] * 2 + [hbm] * 9,
        out_specs=vmem,
        scratch_shapes=[
            pltpu.VMEM((5,) + own.shape, BF16),
            *[pltpu.VMEM(*t) for t in table_shapes(tiles, slots)],
            pltpu.VMEM((mid, TILE, width), BF16),
            pltpu.VMEM((mid, TILE, width), BF16),
            pltpu.VMEM((near, TILE, width), BF16),
            pltpu.VMEM((near, TILE, width), BF16),
            pltpu.VMEM((near + 1, TILE, width), F32),
            pltpu.VMEM((tiles + 1, TILE, width), F32),
            pltpu.VMEM((near, TILE, width), F32),
            pltpu.VMEM((near, TILE, width), F32),
            pltpu.SemaphoreType.DMA((9,)),
        ],
        compiler_params=pltpu.CompilerParams(vmem_limit_bytes=34 << 20),
        cost_estimate=SHORT,
        name="hops",
    )(places, bases, *[pltpu.with_memory_space_constraint(v, pltpu.HBM) for v in (own, low, high, mate, far, *tables)])


BLOCK = 64
GROUP = 4


def grouped(width):
    return [
        pl.BlockSpec((BLOCK, width), lambda i, order, k=k: (order[i * GROUP + k], 0)) for k in range(GROUP)
    ]


def stacked(refs):
    return jnp.concatenate([r[...] for r in refs], axis=0)


def whole(shape):
    return pl.BlockSpec(shape, lambda i, order: (0,) * len(shape))


def out_kernel(order_ref, *refs):
    act, (logit_ref, part_ref) = refs[:GROUP], refs[GROUP:]
    part_ref[...] = jnp.dot(stacked(act), logit_ref[...], preferred_element_type=F32).astype(BF16)


def in_kernel(order_ref, *refs):
    slope, w_out = refs[:GROUP], refs[GROUP : 2 * GROUP]
    logit_ref, feats_ref, part_ref, grad_ref = refs[2 * GROUP :]
    hidden = lax.dot_general(
        stacked(w_out), logit_ref[...], (((1,), (1,)), ((), ())), preferred_element_type=F32
    )
    grad = (hidden * stacked(slope)).astype(BF16)
    grad_ref[...] = grad
    f_in = feats_ref.shape[1]
    part_ref[:, :f_in] = jnp.dot(grad, feats_ref[...], preferred_element_type=F32).astype(BF16)
    bias = jnp.sum(grad.astype(F32), axis=1, keepdims=True)
    part_ref[:, f_in:] = jnp.broadcast_to(bias, (bias.shape[0], TILE)).astype(BF16)


def feat_kernel(order_ref, *refs):
    w_in = refs[:GROUP]
    kept_ref, sent_ref, img_ref, cap_ref, acc_ref = refs[GROUP:]
    i = pl.program_id(0)
    steps = pl.num_programs(0)

    @pl.when(i == 0)
    def _():
        acc_ref[...] = jnp.zeros_like(acc_ref)

    grad = jnp.where(i < steps // 2, kept_ref[...], sent_ref[...])
    acc_ref[...] += lax.dot_general(
        grad, stacked(w_in), (((0,), (0,)), ((), ())), preferred_element_type=F32
    )

    @pl.when(i == steps - 1)
    def _():
        half = img_ref.shape[0]
        img_ref[...] = acc_ref[:half].astype(BF16)
        cap_ref[...] = acc_ref[half:].astype(BF16)


def over_hidden(kernel, name, order, in_specs, out_specs, out_shape, scratch, args):
    return pl.pallas_call(
        kernel,
        out_shape=out_shape,
        grid_spec=pltpu.PrefetchScalarGridSpec(
            num_scalar_prefetch=1,
            grid=(order.shape[0] // GROUP,),
            in_specs=in_specs,
            out_specs=out_specs,
            scratch_shapes=scratch,
        ),
        compiler_params=pltpu.CompilerParams(
            dimension_semantics=("arbitrary",), vmem_limit_bytes=28 << 20
        ),
        cost_estimate=SHORT,
        name=name,
    )(order, *args)


def rows_of_half(width, half, side):
    steps = half // GROUP
    if side:
        return pl.BlockSpec((GROUP * BLOCK, width), lambda i, order: (jnp.maximum(i - steps, 0), 0))
    return pl.BlockSpec((GROUP * BLOCK, width), lambda i, order: (jnp.minimum(i, steps - 1), 0))


def rows_of(width):
    return pl.BlockSpec((GROUP * BLOCK, width), lambda i, order: (i, 0))


def stack_kernel(count_ref, top_ref, bottom_ref, seed_ref, cols_ref, out_ref, meta_ref):
    half = top_ref.shape[0]
    out_ref[:half] = top_ref[...]
    out_ref[half:] = bottom_ref[...]
    tiles, slots = seed_ref.shape
    meta_ref[:, :slots] = seed_ref[...]
    meta_ref[:, slots : 2 * slots] = cols_ref[...]
    row = lax.broadcasted_iota(jnp.int32, (tiles, slots), 0)
    live = jnp.zeros((tiles, slots), jnp.int32)
    for t in range(tiles):
        live = jnp.where(row == t, count_ref[t], live)
    meta_ref[:, 2 * slots :] = live


def stack(top, bottom, seed, cols, counts):
    vmem = pl.BlockSpec(memory_space=pltpu.VMEM)
    shape = (2 * top.shape[0], top.shape[1])
    codes = (seed.shape[0], 3 * seed.shape[1])
    return pl.pallas_call(
        stack_kernel,
        out_shape=(pltpu.HBM(shape, top.dtype), jax.ShapeDtypeStruct(codes, jnp.int32)),
        in_specs=[pl.BlockSpec(memory_space=pltpu.SMEM)] + [vmem] * 4,
        out_specs=(pl.BlockSpec(shape, lambda: (0, 0)), pl.BlockSpec(codes, lambda: (0, 0))),
        cost_estimate=SHORT,
        name="stack",
    )(counts, top, bottom, seed, cols)


def after(value, *done):
    return lax.optimization_barrier((value,) + done)[0]


def moved(array, count, by):
    return lax.ppermute(array, AXES, [(i, i + by) for i in range(count) if 0 <= i + by < count])


def flipped(array, count, mask):
    return lax.ppermute(array, AXES, [(i, i ^ mask) for i in range(count)])


def added(kept, came):
    return (kept.astype(F32) + came.astype(F32)).astype(BF16)


def parts(array, axis):
    return lax.index_in_dim(array, 0, axis, keepdims=False), lax.index_in_dim(array, 1, axis, keepdims=False)


def nearest_pair(count, by):
    return [(i, i + by) for i in range(0, count - by, 2)] + [(i, i - by) for i in range(by + 1, count, 2)]


class Reduction:

    def __init__(self, part, count, bits, first, orders, ends):
        self.count, self.parts, self.left = count, [part], [list(bits)]
        self.steps = [(bit,) for bit in first] + list(zip(*orders)) + [(bit,) for bit in ends]

    def start(self):
        step = self.steps.pop(0)
        if len(step) > len(self.parts):
            part = self.parts[0]
            cut = part.shape[-2] // 2
            self.parts = [part[..., :cut, :], part[..., cut:, :]]
            self.left = [list(self.left[0]), list(self.left[0])]
        elif len(step) < len(self.parts):
            self.parts = [jnp.concatenate(self.parts, axis=-2)]
        self.kept, self.sent, self.came = [], [], []
        for part, left, bit in zip(self.parts, self.left, step):
            kept, sent = parts(part, left.index(bit))
            left.remove(bit)
            self.kept.append(kept)
            self.sent.append(sent)
            self.came.append(flipped(sent, self.count, 1 << bit))

    def finish(self, *done):
        self.parts = [added(after(k, *done), c) for k, c in zip(self.kept, self.came)]

    def result(self, lanes):
        return self.kept[0][:, lanes].astype(F32) + self.came[0][:, lanes].astype(F32)


def per_device(
    feats_img, feats_cap, cot_img, cot_cap, w_in, b_in, w_out, tile_seed, tile_cols, tile_count
):
    local_rows = feats_img.shape[0]
    tiles = local_rows // TILE
    slots = tile_seed.shape[1]
    hid, f_in = w_in.shape
    n_img, n_cap = lax.axis_size("img"), lax.axis_size("cap")
    count = n_img * n_cap
    me = lax.axis_index(AXES)

    even = (me & 1) == 0
    block, meta = stack(cot_img, cot_cap, tile_seed, tile_cols, tile_count)
    other = flipped(meta, count, 1)
    third = lax.ppermute(
        meta, AXES, [(i, i + 3) for i in range(1, count - 3, 2)] + [(i, i - 3) for i in range(4, count, 2)]
    )
    block = after(block, other)
    mate = flipped(block, count, 1)
    low = moved(block, count, 2)
    high = moved(block, count, -2)
    far = lax.ppermute(mate, AXES, nearest_pair(count, 2))
    pair = jnp.where(even, jnp.concatenate([meta, other]), jnp.concatenate([other, meta]))
    feats = jnp.concatenate([after(feats_img, block), feats_cap], axis=0)
    pair, feats, third = lax.optimization_barrier((pair, feats, third))
    pair_low = moved(pair, count, 2)
    pair_high = moved(pair, count, -2)
    wide = jnp.where(
        even,
        jnp.concatenate([third, pair_low, pair, pair_high]),
        jnp.concatenate([pair_low, pair, pair_high, third]),
    )
    frame = jnp.arange(7 * tiles, dtype=jnp.int32)[:, None]
    counts = wide[:, 2 * slots]
    seeds = wide[:, :slots].reshape(-1)
    places = jnp.where(counts[:, None] > 0, wide[:, slots : 2 * slots] - (me - 3) * tiles, frame)
    pats = make_tiles(seeds, (places + tiles).reshape(-1), counts, tiles, slots)

    m = count.bit_length() - 1
    a = n_cap.bit_length() - 1
    cap_bits = list(range(a))
    img_bits = list(range(a + 1, m - 2))
    bits = [a] + cap_bits + img_bits + [m - 2, m - 1]
    pos = jnp.arange(count, dtype=jnp.int32)
    order = jnp.zeros_like(pos)
    for k, bit in enumerate(bits):
        order = order | (((pos >> (m - 1 - k)) & 1) << bit)
    order = order ^ me
    rows = hid // count
    if rows % BLOCK:
        w_in, w_out, b_in = [
            jnp.take(v.reshape((count, rows) + v.shape[1:]), order, axis=0).reshape(v.shape) for v in (w_in, w_out, b_in)
        ]
        order = jnp.arange(hid // BLOCK, dtype=jnp.int32)
    else:
        order = (order[:, None] * (rows // BLOCK) + jnp.arange(rows // BLOCK, dtype=jnp.int32)).reshape(-1)

    across = (((1,), (1,)), ((), ()))
    preact = lax.dot_general(w_in, feats, across, preferred_element_type=F32) + b_in[:, None]
    gelu_value, gelu_slope = gelu_parts(preact)
    hidden_act, gelu_slope = lax.optimization_barrier((gelu_value.astype(BF16), gelu_slope))

    bases = jnp.where(even, jnp.array([3, 1]), jnp.array([1, 3])).astype(jnp.int32) * tiles
    mid_places = (places - tiles)[tiles : 6 * tiles].reshape(-1)
    logit = propagate(mid_places, bases, block, low, high, mate, far, pats, tiles, slots)

    width = cot_img.shape[1]
    nodes = 2 * local_rows
    half = order.shape[0] // 2
    blocked = (2,) * (m - 1) + (rows,)

    def out_half(order, logit):
        return over_hidden(
            out_kernel, "part_out", order, grouped(nodes) + [whole(logit.shape)], rows_of(width),
            jax.ShapeDtypeStruct((hid // 2, width), BF16), [], [hidden_act] * GROUP + [logit],
        ).reshape(blocked + (width,))

    def in_half(order, logit):
        part, grad = over_hidden(
            in_kernel, "part_in", order,
            grouped(nodes) + grouped(width) + [whole(logit.shape), whole(feats.shape)],
            (rows_of(f_in + TILE), rows_of(nodes)),
            (jax.ShapeDtypeStruct((hid // 2, f_in + TILE), BF16), jax.ShapeDtypeStruct((hid // 2, nodes), BF16)),
            [], [gelu_slope] * GROUP + [w_out] * GROUP + [logit, feats],
        )
        return part.reshape(blocked + (f_in + TILE,)), grad

    core = 1 << a
    rest = bits[1:]
    orders = (cap_bits + img_bits, img_bits + cap_bits)
    near, last = m - 2, m - 1
    in_sent, grad_sent = in_half(order[half:], logit)
    in_came = flipped(in_sent, count, core)
    in_kept, grad_kept = in_half(order[:half], after(logit, grad_sent))
    r_in = Reduction(added(in_kept, in_came), count, rest, (), orders, (near, last))
    r_in.start()
    out_sent = out_half(order[half:], after(logit, *r_in.sent))
    out_came = flipped(out_sent, count, core)
    out_kept = out_half(order[:half], after(logit, out_sent))
    r_out = Reduction(added(out_kept, out_came), count, rest, (near,), orders, (last,))
    r_out.start()
    grad_img, grad_cap = over_hidden(
        feat_kernel, "feat_grad", order, grouped(f_in) + [rows_of_half(nodes, half, 0), rows_of_half(nodes, half, 1)],
        (whole((local_rows, f_in)),) * 2, (jax.ShapeDtypeStruct((local_rows, f_in), BF16),) * 2,
        [pltpu.VMEM((nodes, f_in), F32)], [w_in] * GROUP + [after(grad_kept, *r_out.sent), grad_sent],
    )
    done = (grad_img,)
    for _ in range(m - 2):
        r_in.finish(*done)
        r_in.start()
        r_out.finish(*r_in.sent)
        r_out.start()
        done = r_out.sent
    grad_scale = 1.0 / math.sqrt(nodes * count)
    g_out = r_out.result(slice(None)) * grad_scale
    g_in = r_in.result(slice(0, f_in)) * grad_scale
    g_bias = r_in.result(f_in) * grad_scale
    return (grad_img, grad_cap, g_in, g_out, g_bias)


def solution(mesh):
    rows = P(("img", "cap"), None)
    in_specs = (rows, rows, rows, rows, P(), P(), P(), rows, rows, P(("img", "cap")))
    out_specs = (rows, rows, rows, rows, P(("img", "cap")))
    return jax.shard_map(
        per_device, mesh=mesh, in_specs=in_specs, out_specs=out_specs, check_vma=False
    )
```

```python
import math

import jax
import jax.numpy as jnp
from jax import lax
from jax.experimental import pallas as pl
from jax.experimental.pallas import tpu as pltpu
from jax.sharding import PartitionSpec as P

TILE = 128
ALPHA = 0.1
SHORT = pl.CostEstimate(flops=1, transcendentals=0, bytes_accessed=1)
AXES = ("img", "cap")
F32 = jnp.float32
BF16 = jnp.bfloat16


def gelu_parts(preact):
    normal_cdf = 0.5 * (1.0 + jax.scipy.special.erf(preact * 0.7071067811865476))
    normal_pdf = jnp.exp(-0.5 * preact * preact) * 0.3989422804014327
    return (preact * normal_cdf, normal_cdf + preact * normal_pdf)


def tiles_kernel(seed_ref, place_ref, count_ref, *refs, tiles, slots):
    outs, (pat_ref, pat_t_ref, nimg_ref, ncap_ref, deg_ref, sems) = refs[:4], refs[4:]
    all_tiles, mid = 7 * tiles, 5 * tiles
    deg_ref[...] = jnp.zeros_like(deg_ref)
    row = lax.broadcasted_iota(jnp.int32, (TILE, TILE), 0)
    col = lax.broadcasted_iota(jnp.int32, (TILE, TILE), 1)
    first, second = jnp.int32(668265261), jnp.int32(374761393)
    base = (row * 40503 + col * 9973) * first
    base_t = (col * 40503 + row * 9973) * first
    off_diag = row - col

    def pattern(start, seed, live, s):
        mixed = start + seed * first
        mixed = jnp.bitwise_xor(mixed, jnp.right_shift(mixed, 15))
        mixed = mixed * second
        mixed = jnp.bitwise_xor(mixed, jnp.right_shift(mixed, 13))
        edge = jnp.bitwise_and(mixed, 15) == jnp.where(live, 0, 16)
        if s == 0:
            edge = edge | (off_diag == jnp.where(live, 0, TILE))
        return jnp.where(edge, 1.0, 0.0)

    def one(q, full):
        total = None
        for s in range(slots):
            live = s < count_ref[q]
            seed = seed_ref[q * slots + s]
            e = pattern(base, seed, live, s)
            c = place_ref[q * slots + s]
            deg_ref[c] += jnp.sum(e, axis=0, keepdims=True)
            if full:
                m = q - tiles
                pat_ref[m, :, pl.ds(s * TILE, TILE)] = e.astype(BF16)
                pat_t_ref[m, pl.ds(s * TILE, TILE), :] = pattern(base_t, seed, live, s).astype(BF16)
                total = e if total is None else total + e
        if full:
            d = jnp.sum(total, axis=1, keepdims=True)
            n = jnp.where(d > 0.0, lax.rsqrt(d), 0.0)
            nimg_ref[q - tiles] = jnp.broadcast_to(n, (TILE, TILE))
            for k, (src, dst) in enumerate(zip((pat_ref, pat_t_ref, nimg_ref), outs)):
                pltpu.make_async_copy(src.at[q - tiles], dst.at[q - tiles], sems.at[k]).start()

    def edge_body(q, c):
        one(q, False)
        return c

    def mid_body(q, c):
        one(q, True)
        return c

    lax.fori_loop(0, tiles, edge_body, 0)
    lax.fori_loop(tiles, tiles + mid, mid_body, 0)
    copies = [
        pltpu.make_async_copy(src, dst, sems.at[k])
        for k, (src, dst) in enumerate(zip((pat_ref, pat_t_ref, nimg_ref, ncap_ref), outs))
    ]
    lax.fori_loop(tiles + mid, all_tiles, edge_body, 0)
    for m in range(mid):
        d = deg_ref[m + 2 * tiles]
        n = jnp.where(d > 0.0, lax.rsqrt(d), 0.0)
        ncap_ref[m] = jnp.broadcast_to(n, (TILE, TILE)).T
    copies[3].start()
    for copy in copies:
        copy.wait()


def table_shapes(tiles, slots):
    mid = 5 * tiles
    return (
        ((mid, TILE, slots * TILE), BF16),
        ((mid, slots * TILE, TILE), BF16),
        ((mid, TILE, TILE), F32),
        ((mid, TILE, TILE), F32),
    )


def make_tiles(seeds, places, counts, tiles, slots):
    smem = pl.BlockSpec(memory_space=pltpu.SMEM)
    hbm = pl.BlockSpec(memory_space=pltpu.HBM)
    tables = table_shapes(tiles, slots)
    return pl.pallas_call(
        lambda *r: tiles_kernel(*r, tiles=tiles, slots=slots),
        out_shape=tuple(pltpu.HBM(*t) for t in tables),
        in_specs=[smem] * 3,
        out_specs=(hbm,) * 4,
        scratch_shapes=[pltpu.VMEM(*t) for t in tables]
        + [pltpu.VMEM((9 * tiles, 1, TILE), F32), pltpu.SemaphoreType.DMA((4,))],
        compiler_params=pltpu.CompilerParams(vmem_limit_bytes=16 << 20),
        cost_estimate=SHORT,
        name="tiles",
    )(seeds, places, counts)


def hops_kernel(
    place_ref, base_ref, own_hbm, low_hbm, high_hbm, mate_hbm, far_hbm, pat_hbm, pat_t_hbm, nimg_hbm, ncap_hbm,
    out_ref, bands, pat_ref, pat_t_ref, nimg_ref, ncap_ref, img0, cap0, img1, cap1, acc, acc2, keep_img, keep_cap,
    sems, *, tiles, slots, width,
):
    mid = 5 * tiles
    near = 3 * tiles
    keep = 1.0 - ALPHA
    sources = (own_hbm, nimg_hbm, ncap_hbm, pat_t_hbm, low_hbm, high_hbm, mate_hbm, far_hbm, pat_hbm)
    targets = (bands.at[0], nimg_ref, ncap_ref, pat_t_ref) + tuple(bands.at[k] for k in range(1, 5)) + (pat_ref,)
    copies = [pltpu.make_async_copy(s, t, sems.at[k]) for k, (s, t) in enumerate(zip(sources, targets))]
    for copy in copies:
        copy.start()

    def wide(n_ref, m):
        n = n_ref[m]
        return jnp.concatenate([n] * (width // TILE), axis=1)

    def scale(k, base):
        for t in range(tiles):
            m = base + t
            img0[m] = (bands[k, pl.ds(t * TILE, TILE), :].astype(F32) * wide(nimg_ref, m)).astype(BF16)
            cap0[m] = (bands[k, pl.ds((tiles + t) * TILE, TILE), :].astype(F32) * wide(ncap_ref, m)).astype(BF16)

    acc[...] = jnp.zeros_like(acc)
    acc2[...] = jnp.zeros_like(acc2)

    def push(q, state, target, lo, count):
        r = jnp.dot(pat_t_ref[q], state, preferred_element_type=F32)
        for s in range(slots):
            c = place_ref[q * slots + s] - lo
            c = jnp.where((c >= 0) & (c < count), c, count)
            target[c] += r[s * TILE : (s + 1) * TILE]

    def pull(q, source, lo):
        total = None
        for s in range(slots):
            c = place_ref[q * slots + s] - lo
            r = jnp.dot(pat_ref[q, :, pl.ds(s * TILE, TILE)], source[c], preferred_element_type=F32)
            total = r if total is None else total + r
        return total

    for copy in copies[:4]:
        copy.wait()
    for k, base in enumerate((2 * tiles, 0, 4 * tiles, base_ref[0], base_ref[1])):
        if k:
            copies[3 + k].wait()
        scale(k, base)
        for t in range(tiles):
            push(base + t, img0[base + t], acc, tiles, near)
    copies[8].wait()

    def pull1(q, c):
        n = wide(nimg_ref, q)
        flow = keep * n * pull(q, cap0, 0)
        img1[q - tiles] = (flow * n).astype(BF16)
        keep_img[q - tiles] = flow
        return c

    lax.fori_loop(tiles, tiles + near, pull1, 0, unroll=9)

    def finish1(m, c):
        n = wide(ncap_ref, m + tiles)
        flow = keep * n * acc[m]
        cap1[m] = (flow * n).astype(BF16)
        keep_cap[m] = flow
        return c

    lax.fori_loop(0, near, finish1, 0, unroll=3)

    def push2(q, c):
        push(q, img1[q - tiles], acc2, 2 * tiles, tiles)
        return c

    lax.fori_loop(tiles, tiles + near, push2, 0, unroll=3)
    for t in range(tiles):
        q = 2 * tiles + t
        rows = pl.ds(t * TILE, TILE)
        flow = keep * wide(nimg_ref, q) * pull(q, cap1, tiles)
        out_ref[rows, :] = (ALPHA * (bands[0, rows, :].astype(F32) + keep_img[tiles + t]) + flow).astype(BF16)
        flow = keep * wide(ncap_ref, q) * acc2[t]
        rows = pl.ds((tiles + t) * TILE, TILE)
        out_ref[rows, :] = (ALPHA * (bands[0, rows, :].astype(F32) + keep_cap[tiles + t]) + flow).astype(BF16)


def propagate(places, bases, own, low, high, mate, far, tables, tiles, slots):
    width = own.shape[1]
    smem = pl.BlockSpec(memory_space=pltpu.SMEM)
    vmem = pl.BlockSpec(memory_space=pltpu.VMEM)
    hbm = pl.BlockSpec(memory_space=pltpu.HBM)
    mid, near = 5 * tiles, 3 * tiles
    return pl.pallas_call(
        lambda *r: hops_kernel(*r, tiles=tiles, slots=slots, width=width),
        out_shape=jax.ShapeDtypeStruct(own.shape, BF16),
        in_specs=[smem] * 2 + [hbm] * 9,
        out_specs=vmem,
        scratch_shapes=[
            pltpu.VMEM((5,) + own.shape, BF16),
            *[pltpu.VMEM(*t) for t in table_shapes(tiles, slots)],
            pltpu.VMEM((mid, TILE, width), BF16),
            pltpu.VMEM((mid, TILE, width), BF16),
            pltpu.VMEM((near, TILE, width), BF16),
            pltpu.VMEM((near, TILE, width), BF16),
            pltpu.VMEM((near + 1, TILE, width), F32),
            pltpu.VMEM((tiles + 1, TILE, width), F32),
            pltpu.VMEM((near, TILE, width), F32),
            pltpu.VMEM((near, TILE, width), F32),
            pltpu.SemaphoreType.DMA((9,)),
        ],
        compiler_params=pltpu.CompilerParams(vmem_limit_bytes=34 << 20),
        cost_estimate=SHORT,
        name="hops",
    )(places, bases, *[pltpu.with_memory_space_constraint(v, pltpu.HBM) for v in (own, low, high, mate, far, *tables)])


BLOCK = 64
GROUP = 4


def grouped(width):
    return [
        pl.BlockSpec((BLOCK, width), lambda i, order, k=k: (order[i * GROUP + k], 0)) for k in range(GROUP)
    ]


def stacked(refs):
    return jnp.concatenate([r[...] for r in refs], axis=0)


def whole(shape):
    return pl.BlockSpec(shape, lambda i, order: (0,) * len(shape))


def out_kernel(order_ref, *refs):
    act, (logit_ref, part_ref) = refs[:GROUP], refs[GROUP:]
    part_ref[...] = jnp.dot(stacked(act), logit_ref[...], preferred_element_type=F32).astype(BF16)


def in_kernel(order_ref, *refs):
    slope, w_out = refs[:GROUP], refs[GROUP : 2 * GROUP]
    logit_ref, feats_ref, part_ref, grad_ref = refs[2 * GROUP :]
    hidden = lax.dot_general(
        stacked(w_out), logit_ref[...], (((1,), (1,)), ((), ())), preferred_element_type=F32
    )
    grad = (hidden * stacked(slope)).astype(BF16)
    grad_ref[...] = grad
    f_in = feats_ref.shape[1]
    part_ref[:, :f_in] = jnp.dot(grad, feats_ref[...], preferred_element_type=F32).astype(BF16)
    bias = jnp.sum(grad.astype(F32), axis=1, keepdims=True)
    part_ref[:, f_in:] = jnp.broadcast_to(bias, (bias.shape[0], TILE)).astype(BF16)


def feat_kernel(order_ref, *refs):
    w_in = refs[:GROUP]
    kept_ref, sent_ref, img_ref, cap_ref, acc_ref = refs[GROUP:]
    i = pl.program_id(0)
    steps = pl.num_programs(0)

    @pl.when(i == 0)
    def _():
        acc_ref[...] = jnp.zeros_like(acc_ref)

    grad = jnp.where(i < steps // 2, kept_ref[...], sent_ref[...])
    acc_ref[...] += lax.dot_general(
        grad, stacked(w_in), (((0,), (0,)), ((), ())), preferred_element_type=F32
    )

    @pl.when(i == steps - 1)
    def _():
        half = img_ref.shape[0]
        img_ref[...] = acc_ref[:half].astype(BF16)
        cap_ref[...] = acc_ref[half:].astype(BF16)


def over_hidden(kernel, name, order, in_specs, out_specs, out_shape, scratch, args):
    return pl.pallas_call(
        kernel,
        out_shape=out_shape,
        grid_spec=pltpu.PrefetchScalarGridSpec(
            num_scalar_prefetch=1,
            grid=(order.shape[0] // GROUP,),
            in_specs=in_specs,
            out_specs=out_specs,
            scratch_shapes=scratch,
        ),
        compiler_params=pltpu.CompilerParams(
            dimension_semantics=("arbitrary",), vmem_limit_bytes=28 << 20
        ),
        cost_estimate=SHORT,
        name=name,
    )(order, *args)


def rows_of_half(width, half, side):
    steps = half // GROUP
    if side:
        return pl.BlockSpec((GROUP * BLOCK, width), lambda i, order: (jnp.maximum(i - steps, 0), 0))
    return pl.BlockSpec((GROUP * BLOCK, width), lambda i, order: (jnp.minimum(i, steps - 1), 0))


def rows_of(width):
    return pl.BlockSpec((GROUP * BLOCK, width), lambda i, order: (i, 0))


def stack_kernel(count_ref, top_ref, bottom_ref, seed_ref, cols_ref, out_ref, meta_ref):
    half = top_ref.shape[0]
    out_ref[:half] = top_ref[...]
    out_ref[half:] = bottom_ref[...]
    tiles, slots = seed_ref.shape
    meta_ref[:, :slots] = seed_ref[...]
    meta_ref[:, slots : 2 * slots] = cols_ref[...]
    row = lax.broadcasted_iota(jnp.int32, (tiles, slots), 0)
    live = jnp.zeros((tiles, slots), jnp.int32)
    for t in range(tiles):
        live = jnp.where(row == t, count_ref[t], live)
    meta_ref[:, 2 * slots :] = live


def stack(top, bottom, seed, cols, counts):
    vmem = pl.BlockSpec(memory_space=pltpu.VMEM)
    shape = (2 * top.shape[0], top.shape[1])
    codes = (seed.shape[0], 3 * seed.shape[1])
    return pl.pallas_call(
        stack_kernel,
        out_shape=(pltpu.HBM(shape, top.dtype), jax.ShapeDtypeStruct(codes, jnp.int32)),
        in_specs=[pl.BlockSpec(memory_space=pltpu.SMEM)] + [vmem] * 4,
        out_specs=(pl.BlockSpec(shape, lambda: (0, 0)), pl.BlockSpec(codes, lambda: (0, 0))),
        cost_estimate=SHORT,
        name="stack",
    )(counts, top, bottom, seed, cols)


def after(value, *done):
    return lax.optimization_barrier((value,) + done)[0]


def moved(array, count, by):
    return lax.ppermute(array, AXES, [(i, i + by) for i in range(count) if 0 <= i + by < count])


def flipped(array, count, mask):
    return lax.ppermute(array, AXES, [(i, i ^ mask) for i in range(count)])


def added(kept, came):
    return (kept.astype(F32) + came.astype(F32)).astype(BF16)


def parts(array, axis):
    return lax.index_in_dim(array, 0, axis, keepdims=False), lax.index_in_dim(array, 1, axis, keepdims=False)


def nearest_pair(count, by):
    return [(i, i + by) for i in range(0, count - by, 2)] + [(i, i - by) for i in range(by + 1, count, 2)]


class Reduction:

    def __init__(self, part, count, bits, first, orders, ends):
        self.count, self.parts, self.left = count, [part], [list(bits)]
        self.steps = [(bit,) for bit in first] + list(zip(*orders)) + [(bit,) for bit in ends]

    def start(self):
        step = self.steps.pop(0)
        if len(step) > len(self.parts):
            part = self.parts[0]
            cut = part.shape[-2] // 2
            self.parts = [part[..., :cut, :], part[..., cut:, :]]
            self.left = [list(self.left[0]), list(self.left[0])]
        elif len(step) < len(self.parts):
            self.parts = [jnp.concatenate(self.parts, axis=-2)]
        self.kept, self.sent, self.came = [], [], []
        for part, left, bit in zip(self.parts, self.left, step):
            kept, sent = parts(part, left.index(bit))
            left.remove(bit)
            self.kept.append(kept)
            self.sent.append(sent)
            self.came.append(flipped(sent, self.count, 1 << bit))

    def finish(self, *done):
        self.parts = [added(after(k, *done), c) for k, c in zip(self.kept, self.came)]

    def result(self, lanes):
        return self.kept[0][:, lanes].astype(F32) + self.came[0][:, lanes].astype(F32)


def per_device(
    feats_img, feats_cap, cot_img, cot_cap, w_in, b_in, w_out, tile_seed, tile_cols, tile_count
):
    local_rows = feats_img.shape[0]
    tiles = local_rows // TILE
    slots = tile_seed.shape[1]
    hid, f_in = w_in.shape
    n_img, n_cap = lax.axis_size("img"), lax.axis_size("cap")
    count = n_img * n_cap
    me = lax.axis_index(AXES)

    even = (me & 1) == 0
    block, meta = stack(cot_img, cot_cap, tile_seed, tile_cols, tile_count)
    other = flipped(meta, count, 1)
    third = lax.ppermute(
        meta, AXES, [(i, i + 3) for i in range(1, count - 3, 2)] + [(i, i - 3) for i in range(4, count, 2)]
    )
    behind = after(block, other)
    mate = flipped(behind, count, 1)
    low = moved(block, count, 2)
    high = moved(block, count, -2)
    far = lax.ppermute(mate, AXES, nearest_pair(count, 2))
    pair = jnp.where(even, jnp.concatenate([meta, other]), jnp.concatenate([other, meta]))
    feats = jnp.concatenate([after(feats_img, behind), feats_cap], axis=0)
    pair, feats, third = lax.optimization_barrier((pair, feats, third))
    pair_low = moved(pair, count, 2)
    pair_high = moved(pair, count, -2)
    wide = jnp.where(
        even,
        jnp.concatenate([third, pair_low, pair, pair_high]),
        jnp.concatenate([pair_low, pair, pair_high, third]),
    )
    frame = jnp.arange(7 * tiles, dtype=jnp.int32)[:, None]
    counts = wide[:, 2 * slots]
    seeds = wide[:, :slots].reshape(-1)
    places = jnp.where(counts[:, None] > 0, wide[:, slots : 2 * slots] - (me - 3) * tiles, frame)
    pats = make_tiles(seeds, (places + tiles).reshape(-1), counts, tiles, slots)

    m = count.bit_length() - 1
    a = n_cap.bit_length() - 1
    cap_bits = list(range(a))
    img_bits = list(range(a + 1, m - 2))
    bits = [a] + cap_bits + img_bits + [m - 2, m - 1]
    pos = jnp.arange(count, dtype=jnp.int32)
    order = jnp.zeros_like(pos)
    for k, bit in enumerate(bits):
        order = order | (((pos >> (m - 1 - k)) & 1) << bit)
    order = order ^ me
    rows = hid // count
    if rows % BLOCK:
        w_in, w_out, b_in = [
            jnp.take(v.reshape((count, rows) + v.shape[1:]), order, axis=0).reshape(v.shape) for v in (w_in, w_out, b_in)
        ]
        order = jnp.arange(hid // BLOCK, dtype=jnp.int32)
    else:
        order = (order[:, None] * (rows // BLOCK) + jnp.arange(rows // BLOCK, dtype=jnp.int32)).reshape(-1)

    across = (((1,), (1,)), ((), ()))
    preact = lax.dot_general(w_in, feats, across, preferred_element_type=F32) + b_in[:, None]
    gelu_value, gelu_slope = gelu_parts(preact)
    hidden_act, gelu_slope = lax.optimization_barrier((gelu_value.astype(BF16), gelu_slope))

    bases = jnp.where(even, jnp.array([3, 1]), jnp.array([1, 3])).astype(jnp.int32) * tiles
    mid_places = (places - tiles)[tiles : 6 * tiles].reshape(-1)
    logit = propagate(mid_places, bases, block, low, high, mate, far, pats, tiles, slots)

    width = cot_img.shape[1]
    nodes = 2 * local_rows
    half = order.shape[0] // 2
    blocked = (2,) * (m - 1) + (rows,)

    def out_half(order, logit):
        return over_hidden(
            out_kernel, "part_out", order, grouped(nodes) + [whole(logit.shape)], rows_of(width),
            jax.ShapeDtypeStruct((hid // 2, width), BF16), [], [hidden_act] * GROUP + [logit],
        ).reshape(blocked + (width,))

    def in_half(order, logit):
        part, grad = over_hidden(
            in_kernel, "part_in", order,
            grouped(nodes) + grouped(width) + [whole(logit.shape), whole(feats.shape)],
            (rows_of(f_in + TILE), rows_of(nodes)),
            (jax.ShapeDtypeStruct((hid // 2, f_in + TILE), BF16), jax.ShapeDtypeStruct((hid // 2, nodes), BF16)),
            [], [gelu_slope] * GROUP + [w_out] * GROUP + [logit, feats],
        )
        return part.reshape(blocked + (f_in + TILE,)), grad

    core = 1 << a
    rest = bits[1:]
    orders = (cap_bits + img_bits, img_bits + cap_bits)
    near, last = m - 2, m - 1
    in_sent, grad_sent = in_half(order[half:], logit)
    in_came = flipped(in_sent, count, core)
    in_kept, grad_kept = in_half(order[:half], after(logit, grad_sent))
    r_in = Reduction(added(in_kept, in_came), count, rest, (), orders, (near, last))
    r_in.start()
    out_sent = out_half(order[half:], after(logit, *r_in.sent))
    out_came = flipped(out_sent, count, core)
    out_kept = out_half(order[:half], after(logit, out_sent))
    r_out = Reduction(added(out_kept, out_came), count, rest, (near,), orders, (last,))
    r_out.start()
    grad_img, grad_cap = over_hidden(
        feat_kernel, "feat_grad", order, grouped(f_in) + [rows_of_half(nodes, half, 0), rows_of_half(nodes, half, 1)],
        (whole((local_rows, f_in)),) * 2, (jax.ShapeDtypeStruct((local_rows, f_in), BF16),) * 2,
        [pltpu.VMEM((nodes, f_in), F32)], [w_in] * GROUP + [after(grad_kept, *r_out.sent), grad_sent],
    )
    done = (grad_img,)
    for _ in range(m - 2):
        r_in.finish(*done)
        r_in.start()
        r_out.finish(*r_in.sent)
        r_out.start()
        done = r_out.sent
    grad_scale = 1.0 / math.sqrt(nodes * count)
    g_out = r_out.result(slice(None)) * grad_scale
    g_in = r_in.result(slice(0, f_in)) * grad_scale
    g_bias = r_in.result(f_in) * grad_scale
    return (grad_img, grad_cap, g_in, g_out, g_bias)


def solution(mesh):
    rows = P(("img", "cap"), None)
    in_specs = (rows, rows, rows, rows, P(), P(), P(), rows, rows, P(("img", "cap")))
    out_specs = (rows, rows, rows, rows, P(("img", "cap")))
    return jax.shard_map(
        per_device, mesh=mesh, in_specs=in_specs, out_specs=out_specs, check_vma=False
    )
```

```python
import math

import jax
import jax.numpy as jnp
from jax import lax
from jax.experimental import pallas as pl
from jax.experimental.pallas import tpu as pltpu
from jax.sharding import PartitionSpec as P

TILE = 128
ALPHA = 0.1
SHORT = pl.CostEstimate(flops=1, transcendentals=0, bytes_accessed=1)
AXES = ("img", "cap")
F32 = jnp.float32
BF16 = jnp.bfloat16


def gelu_parts(preact):
    normal_cdf = 0.5 * (1.0 + jax.scipy.special.erf(preact * 0.7071067811865476))
    normal_pdf = jnp.exp(-0.5 * preact * preact) * 0.3989422804014327
    return (preact * normal_cdf, normal_cdf + preact * normal_pdf)


def tiles_kernel(seed_ref, place_ref, count_ref, *refs, tiles, slots):
    outs, (pat_ref, pat_t_ref, nimg_ref, ncap_ref, deg_ref, sems) = refs[:4], refs[4:]
    all_tiles, mid = 7 * tiles, 5 * tiles
    deg_ref[...] = jnp.zeros_like(deg_ref)
    row = lax.broadcasted_iota(jnp.int32, (TILE, TILE), 0)
    col = lax.broadcasted_iota(jnp.int32, (TILE, TILE), 1)
    first, second = jnp.int32(668265261), jnp.int32(374761393)
    base = (row * 40503 + col * 9973) * first
    base_t = (col * 40503 + row * 9973) * first
    off_diag = row - col

    def pattern(start, seed, live, s):
        mixed = start + seed * first
        mixed = jnp.bitwise_xor(mixed, jnp.right_shift(mixed, 15))
        mixed = mixed * second
        mixed = jnp.bitwise_xor(mixed, jnp.right_shift(mixed, 13))
        edge = jnp.bitwise_and(mixed, 15) == jnp.where(live, 0, 16)
        if s == 0:
            edge = edge | (off_diag == jnp.where(live, 0, TILE))
        return jnp.where(edge, 1.0, 0.0)

    def one(q, full):
        total = None
        for s in range(slots):
            live = s < count_ref[q]
            seed = seed_ref[q * slots + s]
            e = pattern(base, seed, live, s)
            c = place_ref[q * slots + s]
            deg_ref[c] += jnp.sum(e, axis=0, keepdims=True)
            if full:
                m = q - tiles
                pat_ref[m, :, pl.ds(s * TILE, TILE)] = e.astype(BF16)
                pat_t_ref[m, pl.ds(s * TILE, TILE), :] = pattern(base_t, seed, live, s).astype(BF16)
                total = e if total is None else total + e
        if full:
            d = jnp.sum(total, axis=1, keepdims=True)
            n = jnp.where(d > 0.0, lax.rsqrt(d), 0.0)
            nimg_ref[q - tiles] = jnp.broadcast_to(n, (TILE, TILE))
            for k, (src, dst) in enumerate(zip((pat_ref, pat_t_ref, nimg_ref), outs)):
                pltpu.make_async_copy(src.at[q - tiles], dst.at[q - tiles], sems.at[k]).start()

    def edge_body(q, c):
        one(q, False)
        return c

    def mid_body(q, c):
        one(q, True)
        return c

    lax.fori_loop(0, tiles, edge_body, 0)
    lax.fori_loop(tiles, tiles + mid, mid_body, 0)
    copies = [
        pltpu.make_async_copy(src, dst, sems.at[k])
        for k, (src, dst) in enumerate(zip((pat_ref, pat_t_ref, nimg_ref, ncap_ref), outs))
    ]
    lax.fori_loop(tiles + mid, all_tiles, edge_body, 0)
    for m in range(mid):
        d = deg_ref[m + 2 * tiles]
        n = jnp.where(d > 0.0, lax.rsqrt(d), 0.0)
        ncap_ref[m] = jnp.broadcast_to(n, (TILE, TILE)).T
    copies[3].start()
    for copy in copies:
        copy.wait()


def table_shapes(tiles, slots):
    mid = 5 * tiles
    return (
        ((mid, TILE, slots * TILE), BF16),
        ((mid, slots * TILE, TILE), BF16),
        ((mid, TILE, TILE), F32),
        ((mid, TILE, TILE), F32),
    )


def make_tiles(seeds, places, counts, tiles, slots):
    smem = pl.BlockSpec(memory_space=pltpu.SMEM)
    hbm = pl.BlockSpec(memory_space=pltpu.HBM)
    tables = table_shapes(tiles, slots)
    return pl.pallas_call(
        lambda *r: tiles_kernel(*r, tiles=tiles, slots=slots),
        out_shape=tuple(pltpu.HBM(*t) for t in tables),
        in_specs=[smem] * 3,
        out_specs=(hbm,) * 4,
        scratch_shapes=[pltpu.VMEM(*t) for t in tables]
        + [pltpu.VMEM((9 * tiles, 1, TILE), F32), pltpu.SemaphoreType.DMA((4,))],
        compiler_params=pltpu.CompilerParams(vmem_limit_bytes=16 << 20),
        cost_estimate=SHORT,
        name="tiles",
    )(seeds, places, counts)


def hops_kernel(
    place_ref, base_ref, own_hbm, low_hbm, high_hbm, mate_hbm, far_hbm, pat_hbm, pat_t_hbm, nimg_hbm, ncap_hbm,
    out_ref, bands, pat_ref, pat_t_ref, nimg_ref, ncap_ref, img0, cap0, img1, cap1, acc, acc2, keep_img, keep_cap,
    sems, *, tiles, slots, width,
):
    mid = 5 * tiles
    near = 3 * tiles
    keep = 1.0 - ALPHA
    sources = (own_hbm, nimg_hbm, ncap_hbm, pat_t_hbm, low_hbm, high_hbm, mate_hbm, far_hbm, pat_hbm)
    targets = (bands.at[0], nimg_ref, ncap_ref, pat_t_ref) + tuple(bands.at[k] for k in range(1, 5)) + (pat_ref,)
    copies = [pltpu.make_async_copy(s, t, sems.at[k]) for k, (s, t) in enumerate(zip(sources, targets))]
    for copy in copies:
        copy.start()

    def wide(n_ref, m):
        n = n_ref[m]
        return jnp.concatenate([n] * (width // TILE), axis=1)

    def scale(k, base):
        for t in range(tiles):
            m = base + t
            img0[m] = (bands[k, pl.ds(t * TILE, TILE), :].astype(F32) * wide(nimg_ref, m)).astype(BF16)
            cap0[m] = (bands[k, pl.ds((tiles + t) * TILE, TILE), :].astype(F32) * wide(ncap_ref, m)).astype(BF16)

    acc[...] = jnp.zeros_like(acc)
    acc2[...] = jnp.zeros_like(acc2)

    def push(q, state, target, lo, count):
        r = jnp.dot(pat_t_ref[q], state, preferred_element_type=F32)
        for s in range(slots):
            c = place_ref[q * slots + s] - lo
            c = jnp.where((c >= 0) & (c < count), c, count)
            target[c] += r[s * TILE : (s + 1) * TILE]

    def pull(q, source, lo):
        total = None
        for s in range(slots):
            c = place_ref[q * slots + s] - lo
            r = jnp.dot(pat_ref[q, :, pl.ds(s * TILE, TILE)], source[c], preferred_element_type=F32)
            total = r if total is None else total + r
        return total

    for copy in copies[:4]:
        copy.wait()
    for k, base in enumerate((2 * tiles, 0, 4 * tiles, base_ref[0], base_ref[1])):
        if k:
            copies[3 + k].wait()
        scale(k, base)
        for t in range(tiles):
            push(base + t, img0[base + t], acc, tiles, near)
    copies[8].wait()

    def pull1(q, c):
        n = wide(nimg_ref, q)
        flow = keep * n * pull(q, cap0, 0)
        img1[q - tiles] = (flow * n).astype(BF16)
        keep_img[q - tiles] = flow
        return c

    lax.fori_loop(tiles, tiles + near, pull1, 0, unroll=9)

    def finish1(m, c):
        n = wide(ncap_ref, m + tiles)
        flow = keep * n * acc[m]
        cap1[m] = (flow * n).astype(BF16)
        keep_cap[m] = flow
        return c

    lax.fori_loop(0, near, finish1, 0, unroll=3)

    def push2(q, c):
        push(q, img1[q - tiles], acc2, 2 * tiles, tiles)
        return c

    lax.fori_loop(tiles, tiles + near, push2, 0, unroll=3)
    for t in range(tiles):
        q = 2 * tiles + t
        rows = pl.ds(t * TILE, TILE)
        flow = keep * wide(nimg_ref, q) * pull(q, cap1, tiles)
        out_ref[rows, :] = (ALPHA * (bands[0, rows, :].astype(F32) + keep_img[tiles + t]) + flow).astype(BF16)
        flow = keep * wide(ncap_ref, q) * acc2[t]
        rows = pl.ds((tiles + t) * TILE, TILE)
        out_ref[rows, :] = (ALPHA * (bands[0, rows, :].astype(F32) + keep_cap[tiles + t]) + flow).astype(BF16)


def propagate(places, bases, own, low, high, mate, far, tables, tiles, slots):
    width = own.shape[1]
    smem = pl.BlockSpec(memory_space=pltpu.SMEM)
    vmem = pl.BlockSpec(memory_space=pltpu.VMEM)
    hbm = pl.BlockSpec(memory_space=pltpu.HBM)
    mid, near = 5 * tiles, 3 * tiles
    return pl.pallas_call(
        lambda *r: hops_kernel(*r, tiles=tiles, slots=slots, width=width),
        out_shape=jax.ShapeDtypeStruct(own.shape, BF16),
        in_specs=[smem] * 2 + [hbm] * 9,
        out_specs=vmem,
        scratch_shapes=[
            pltpu.VMEM((5,) + own.shape, BF16),
            *[pltpu.VMEM(*t) for t in table_shapes(tiles, slots)],
            pltpu.VMEM((mid, TILE, width), BF16),
            pltpu.VMEM((mid, TILE, width), BF16),
            pltpu.VMEM((near, TILE, width), BF16),
            pltpu.VMEM((near, TILE, width), BF16),
            pltpu.VMEM((near + 1, TILE, width), F32),
            pltpu.VMEM((tiles + 1, TILE, width), F32),
            pltpu.VMEM((near, TILE, width), F32),
            pltpu.VMEM((near, TILE, width), F32),
            pltpu.SemaphoreType.DMA((9,)),
        ],
        compiler_params=pltpu.CompilerParams(vmem_limit_bytes=34 << 20),
        cost_estimate=SHORT,
        name="hops",
    )(places, bases, *[pltpu.with_memory_space_constraint(v, pltpu.HBM) for v in (own, low, high, mate, far, *tables)])


BLOCK = 64
GROUP = 4


def grouped(width):
    return [
        pl.BlockSpec((BLOCK, width), lambda i, order, k=k: (order[i * GROUP + k], 0)) for k in range(GROUP)
    ]


def stacked(refs):
    return jnp.concatenate([r[...] for r in refs], axis=0)


def whole(shape):
    return pl.BlockSpec(shape, lambda i, order: (0,) * len(shape))


def out_kernel(order_ref, *refs):
    act, (logit_ref, part_ref) = refs[:GROUP], refs[GROUP:]
    part_ref[...] = jnp.dot(stacked(act), logit_ref[...], preferred_element_type=F32).astype(BF16)


def in_kernel(order_ref, *refs):
    slope, w_out = refs[:GROUP], refs[GROUP : 2 * GROUP]
    logit_ref, feats_ref, part_ref, grad_ref = refs[2 * GROUP :]
    hidden = lax.dot_general(
        stacked(w_out), logit_ref[...], (((1,), (1,)), ((), ())), preferred_element_type=F32
    )
    grad = (hidden * stacked(slope)).astype(BF16)
    grad_ref[...] = grad
    f_in = feats_ref.shape[1]
    part_ref[:, :f_in] = jnp.dot(grad, feats_ref[...], preferred_element_type=F32).astype(BF16)
    bias = jnp.sum(grad.astype(F32), axis=1, keepdims=True)
    part_ref[:, f_in:] = jnp.broadcast_to(bias, (bias.shape[0], TILE)).astype(BF16)


def feat_kernel(order_ref, *refs):
    w_in = refs[:GROUP]
    kept_ref, sent_ref, img_ref, cap_ref, acc_ref = refs[GROUP:]
    i = pl.program_id(0)
    steps = pl.num_programs(0)

    @pl.when(i == 0)
    def _():
        acc_ref[...] = jnp.zeros_like(acc_ref)

    grad = jnp.where(i < steps // 2, kept_ref[...], sent_ref[...])
    acc_ref[...] += lax.dot_general(
        grad, stacked(w_in), (((0,), (0,)), ((), ())), preferred_element_type=F32
    )

    @pl.when(i == steps - 1)
    def _():
        half = img_ref.shape[0]
        img_ref[...] = acc_ref[:half].astype(BF16)
        cap_ref[...] = acc_ref[half:].astype(BF16)


def over_hidden(kernel, name, order, in_specs, out_specs, out_shape, scratch, args):
    return pl.pallas_call(
        kernel,
        out_shape=out_shape,
        grid_spec=pltpu.PrefetchScalarGridSpec(
            num_scalar_prefetch=1,
            grid=(order.shape[0] // GROUP,),
            in_specs=in_specs,
            out_specs=out_specs,
            scratch_shapes=scratch,
        ),
        compiler_params=pltpu.CompilerParams(
            dimension_semantics=("arbitrary",), vmem_limit_bytes=28 << 20
        ),
        cost_estimate=SHORT,
        name=name,
    )(order, *args)


def rows_of_half(width, half, side):
    steps = half // GROUP
    if side:
        return pl.BlockSpec((GROUP * BLOCK, width), lambda i, order: (jnp.maximum(i - steps, 0), 0))
    return pl.BlockSpec((GROUP * BLOCK, width), lambda i, order: (jnp.minimum(i, steps - 1), 0))


def rows_of(width):
    return pl.BlockSpec((GROUP * BLOCK, width), lambda i, order: (i, 0))


def stack_kernel(count_ref, top_ref, bottom_ref, seed_ref, cols_ref, out_ref, meta_ref):
    half = top_ref.shape[0]
    out_ref[:half] = top_ref[...]
    out_ref[half:] = bottom_ref[...]
    tiles, slots = seed_ref.shape
    meta_ref[:, :slots] = seed_ref[...]
    meta_ref[:, slots : 2 * slots] = cols_ref[...]
    row = lax.broadcasted_iota(jnp.int32, (tiles, slots), 0)
    live = jnp.zeros((tiles, slots), jnp.int32)
    for t in range(tiles):
        live = jnp.where(row == t, count_ref[t], live)
    meta_ref[:, 2 * slots :] = live


def stack(top, bottom, seed, cols, counts):
    vmem = pl.BlockSpec(memory_space=pltpu.VMEM)
    shape = (2 * top.shape[0], top.shape[1])
    codes = (seed.shape[0], 3 * seed.shape[1])
    return pl.pallas_call(
        stack_kernel,
        out_shape=(pltpu.HBM(shape, top.dtype), jax.ShapeDtypeStruct(codes, jnp.int32)),
        in_specs=[pl.BlockSpec(memory_space=pltpu.SMEM)] + [vmem] * 4,
        out_specs=(pl.BlockSpec(shape, lambda: (0, 0)), pl.BlockSpec(codes, lambda: (0, 0))),
        cost_estimate=SHORT,
        name="stack",
    )(counts, top, bottom, seed, cols)


def after(value, *done):
    return lax.optimization_barrier((value,) + done)[0]


def moved(array, count, by):
    return lax.ppermute(array, AXES, [(i, i + by) for i in range(count) if 0 <= i + by < count])


def flipped(array, count, mask):
    return lax.ppermute(array, AXES, [(i, i ^ mask) for i in range(count)])


def added(kept, came):
    return (kept.astype(F32) + came.astype(F32)).astype(BF16)


def parts(array, axis):
    return lax.index_in_dim(array, 0, axis, keepdims=False), lax.index_in_dim(array, 1, axis, keepdims=False)


def nearest_pair(count, by):
    return [(i, i + by) for i in range(0, count - by, 2)] + [(i, i - by) for i in range(by + 1, count, 2)]


class Reduction:

    def __init__(self, part, count, bits, first, orders, ends):
        self.count, self.parts, self.left = count, [part], [list(bits)]
        self.steps = [(bit,) for bit in first] + list(zip(*orders)) + [(bit,) for bit in ends]

    def start(self):
        step = self.steps.pop(0)
        if len(step) > len(self.parts):
            part = self.parts[0]
            cut = part.shape[-2] // 2
            self.parts = [part[..., :cut, :], part[..., cut:, :]]
            self.left = [list(self.left[0]), list(self.left[0])]
        elif len(step) < len(self.parts):
            self.parts = [jnp.concatenate(self.parts, axis=-2)]
        self.kept, self.sent, self.came = [], [], []
        for part, left, bit in zip(self.parts, self.left, step):
            kept, sent = parts(part, left.index(bit))
            left.remove(bit)
            self.kept.append(kept)
            self.sent.append(sent)
            self.came.append(flipped(sent, self.count, 1 << bit))

    def finish(self, *done):
        self.parts = [added(after(k, *done), c) for k, c in zip(self.kept, self.came)]

    def result(self, lanes):
        return self.kept[0][:, lanes].astype(F32) + self.came[0][:, lanes].astype(F32)


def per_device(
    feats_img, feats_cap, cot_img, cot_cap, w_in, b_in, w_out, tile_seed, tile_cols, tile_count
):
    local_rows = feats_img.shape[0]
    tiles = local_rows // TILE
    slots = tile_seed.shape[1]
    hid, f_in = w_in.shape
    n_img, n_cap = lax.axis_size("img"), lax.axis_size("cap")
    count = n_img * n_cap
    me = lax.axis_index(AXES)

    even = (me & 1) == 0
    block, meta = stack(cot_img, cot_cap, tile_seed, tile_cols, tile_count)
    other = flipped(meta, count, 1)
    third = lax.ppermute(
        meta, AXES, [(i, i + 3) for i in range(1, count - 3, 2)] + [(i, i - 3) for i in range(4, count, 2)]
    )
    block = after(block, other)
    mate = flipped(block, count, 1)
    low = moved(block, count, 2)
    high = moved(block, count, -2)
    far = lax.ppermute(mate, AXES, nearest_pair(count, 2))
    pair = jnp.where(even, jnp.concatenate([meta, other]), jnp.concatenate([other, meta]))
    feats = jnp.concatenate([after(feats_img, block), feats_cap], axis=0)
    pair, feats, third = lax.optimization_barrier((pair, feats, third))
    pair_low = moved(pair, count, 2)
    pair_high = moved(pair, count, -2)
    wide = jnp.where(
        even,
        jnp.concatenate([third, pair_low, pair, pair_high]),
        jnp.concatenate([pair_low, pair, pair_high, third]),
    )
    frame = jnp.arange(7 * tiles, dtype=jnp.int32)[:, None]
    counts = wide[:, 2 * slots]
    seeds = wide[:, :slots].reshape(-1)
    places = jnp.where(counts[:, None] > 0, wide[:, slots : 2 * slots] - (me - 3) * tiles, frame)
    pats = make_tiles(seeds, (places + tiles).reshape(-1), counts, tiles, slots)

    m = count.bit_length() - 1
    a = n_cap.bit_length() - 1
    cap_bits = list(range(a))
    img_bits = list(range(a + 1, m - 2))
    bits = [a] + cap_bits + img_bits + [m - 2, m - 1]
    pos = jnp.arange(count, dtype=jnp.int32)
    order = jnp.zeros_like(pos)
    for k, bit in enumerate(bits):
        order = order | (((pos >> (m - 1 - k)) & 1) << bit)
    order = order ^ me
    rows = hid // count
    if rows % BLOCK:
        w_in, w_out, b_in = [
            jnp.take(v.reshape((count, rows) + v.shape[1:]), order, axis=0).reshape(v.shape) for v in (w_in, w_out, b_in)
        ]
        order = jnp.arange(hid // BLOCK, dtype=jnp.int32)
    else:
        order = (order[:, None] * (rows // BLOCK) + jnp.arange(rows // BLOCK, dtype=jnp.int32)).reshape(-1)

    across = (((1,), (1,)), ((), ()))
    preact = lax.dot_general(w_in, feats, across, preferred_element_type=F32) + b_in[:, None]
    gelu_value, gelu_slope = gelu_parts(preact)
    hidden_act, gelu_slope = lax.optimization_barrier((gelu_value.astype(BF16), gelu_slope))

    bases = jnp.where(even, jnp.array([3, 1]), jnp.array([1, 3])).astype(jnp.int32) * tiles
    mid_places = (places - tiles)[tiles : 6 * tiles].reshape(-1)
    logit = propagate(mid_places, bases, block, low, high, mate, far, pats, tiles, slots)

    width = cot_img.shape[1]
    nodes = 2 * local_rows
    half = order.shape[0] // 2
    blocked = (2,) * (m - 1) + (rows,)

    def out_half(order, logit):
        return over_hidden(
            out_kernel, "part_out", order, grouped(nodes) + [whole(logit.shape)], rows_of(width),
            jax.ShapeDtypeStruct((hid // 2, width), BF16), [], [hidden_act] * GROUP + [logit],
        ).reshape(blocked + (width,))

    def in_half(order, logit):
        part, grad = over_hidden(
            in_kernel, "part_in", order,
            grouped(nodes) + grouped(width) + [whole(logit.shape), whole(feats.shape)],
            (rows_of(f_in + TILE), rows_of(nodes)),
            (jax.ShapeDtypeStruct((hid // 2, f_in + TILE), BF16), jax.ShapeDtypeStruct((hid // 2, nodes), BF16)),
            [], [gelu_slope] * GROUP + [w_out] * GROUP + [logit, feats],
        )
        return part.reshape(blocked + (f_in + TILE,)), grad

    core = 1 << a
    rest = bits[1:]
    orders = (cap_bits + img_bits, img_bits + cap_bits)
    near, last = m - 2, m - 1
    in_sent, grad_sent = in_half(order[half:], logit)
    in_came = flipped(in_sent, count, core)
    in_kept, grad_kept = in_half(order[:half], after(logit, grad_sent))
    r_in = Reduction(added(in_kept, in_came), count, rest, (), orders, (near, last))
    r_in.start()
    out_sent = out_half(order[half:], after(logit, *r_in.sent))
    out_came = flipped(out_sent, count, core)
    out_kept = out_half(order[:half], after(logit, out_sent))
    r_out = Reduction(added(out_kept, out_came), count, rest, (near,), orders, (last,))
    r_out.start()
    grad_img, grad_cap = over_hidden(
        feat_kernel, "feat_grad", order, grouped(f_in) + [rows_of_half(nodes, half, 0), rows_of_half(nodes, half, 1)],
        (whole((local_rows, f_in)),) * 2, (jax.ShapeDtypeStruct((local_rows, f_in), BF16),) * 2,
        [pltpu.VMEM((nodes, f_in), F32)], [w_in] * GROUP + [after(grad_kept, *r_out.sent), grad_sent],
    )
    done = (grad_img,)
    for _ in range(m - 2):
        r_in.finish(*done)
        r_in.start()
        r_out.finish(*r_in.sent)
        r_out.start()
        done = r_out.sent
    grad_scale = 1.0 / math.sqrt(nodes * count)
    g_in = r_in.result(slice(0, f_in)) * grad_scale
    g_bias = r_in.result(f_in) * grad_scale
    r_out.kept = [after(r_out.kept[0], g_in, g_bias)]
    g_out = r_out.result(slice(None)) * grad_scale
    return (grad_img, grad_cap, g_in, g_out, g_bias)


def solution(mesh):
    rows = P(("img", "cap"), None)
    in_specs = (rows, rows, rows, rows, P(), P(), P(), rows, rows, P(("img", "cap")))
    out_specs = (rows, rows, rows, rows, P(("img", "cap")))
    return jax.shard_map(
        per_device, mesh=mesh, in_specs=in_specs, out_specs=out_specs, check_vma=False
    )
```
